32 devices in a mesh: scene: 4 (over z), tile: 8 (over y, x, core).
Axes of the slice: x: 2, y: 2, z: 4, core: 2. Of those that a mesh axis runs over, the one named last changes fastest.
Arguments:
- tokens: bfloat16 [32, 16, 128, 1024], P(('scene', 'tile')), may hold values from -40 to 40
- gain: bfloat16 [1024], replicated, may hold values from 0.5 to 1.5
- w_qkv: bfloat16 [1024, 3072], replicated, may hold values from -4 to 4
- w_proj: bfloat16 [1024, 1024], replicated, may hold values from -1 to 1
- scene_first: int32 [32], replicated, may hold values 0 or 1
- window_valid: int32 [32, 16], P(('scene', 'tile')), may hold values 0 or 1
- partner_tile: int32 [4, 8, 16, 1], P('scene'), may hold values from 0 to 7; in each aligned block of 16 rows (0 to 15, 16 to 31, ..., all dimensions but the last counted through in order) at most 4 rows name the same one
- partner_panel: int32 [4, 8, 16], P('scene'), may hold values from 0 to 15
Outputs:
- update: bfloat16 [32, 16, 128, 1024], P(('scene', 'tile'))
The draws below stay inside these ranges and needn't reach their ends.
Inputs may be any that keep to these rules, and one draw needn't show every extreme that they name: `partner_tile`: among the 16 panels of one slab at most 4 name the same tile, and in every draw some slab names some tile exactly 4 times. `scene_first`: slab 0 opens a scene group whatever its entry.
All inputs are finite; a program needn't handle non-finite values. No bound on the sum of `window_valid` on one device may be relied on, other than what follows from the above.
Results may differ from the reference program's by a relative error of at most 0.009.
Values may be sent and summed in bfloat16 or wider, within the bound.
No kernel may reach another device: no remote copies, remote signals or barrier semaphores. Data moves between devices by JAX's collectives and lax.ppermute only.
A program may use at most 256 MiB of HBM per device.

```python
import math
import jax
import jax.numpy as jnp
import numpy as np
from jax import lax

D = 1024
HEADS = 16
CW = 128
TILES = 8
SCENE_ROWS = 4
SLABS = 32
PANELS = 16
CAP = 4


def draw_tokens(key, part):
    base = jax.random.normal(jax.random.fold_in(key, 11), (SLABS, 16, CW, D), jnp.float32)
    values = jnp.clip(base, -6.0, 6.0)
    return values.astype(jnp.bfloat16)


def draw_w_qkv(key, part):
    base = jax.random.normal(jax.random.fold_in(key, 21), (D, 3 * D), jnp.float32) * D ** (-0.5)
    values = base
    return jnp.clip(values, -4.0, 4.0).astype(jnp.bfloat16)


def plant(drawn, rng, smallest, high):
    place = [jax.random.randint(jax.random.fold_in(rng, axis), (), 0, length) for axis, length in enumerate(drawn.shape)]
    longest = drawn.shape.index(max(drawn.shape))
    next_to = place[:longest] + [(place[longest] + 1) % drawn.shape[longest]] + place[longest + 1:]
    return drawn.at[tuple(place)].set(smallest).at[tuple(next_to)].set(high)


def assign_block(rng, own, number, rows, number_of, top, limit, slope):
    order = jax.random.permutation(rng, number_of)
    crowded, usual = portions_of(number_of, rows * top, limit, slope, True), portions_of(number_of, rows * top, limit, slope, False)
    places = jnp.arange(number_of)

    def named(lengths, offset_by):
        used = int((lengths > 0).sum())
        fixed = max(1, used // 4)
        shifted = fixed + (places - fixed + offset_by * (used - fixed)) % max(1, number_of - fixed)
        return jnp.zeros((number_of,), jnp.int32).at[order[jnp.where(places < fixed, places, shifted)]].set(jnp.asarray(lengths, jnp.int32))

    lengths = jnp.where(number % 4 == 0, named(crowded, number // 4), named(usual, number - number // 4 - 1))
    mixed = jax.random.permutation(jax.random.fold_in(own, 3), number_of)
    giver, receiver = mixed[0:number_of // 2 * 2:2], mixed[1:number_of // 2 * 2:2]
    slack = jnp.minimum(lengths[giver] - 1, limit - lengths[receiver]) // 2
    slack = jnp.where((giver == order[0]) | (receiver == order[0]) | (lengths[receiver] == 0), 0, jnp.maximum(slack, 0))
    shifted = jax.random.randint(jax.random.fold_in(own, 4), (number_of // 2,), 0, 1 << 20) % (slack + 1)
    lengths = lengths.at[giver].add(-shifted).at[receiver].add(shifted)
    members = jnp.searchsorted(jnp.cumsum(lengths), jnp.arange(rows * top), side="right").astype(jnp.int32)
    grid = members.reshape(top, rows).T
    grid = grid[jax.random.permutation(jax.random.fold_in(own, 1), rows)]
    offset_by = jax.random.randint(jax.random.fold_in(own, 2), (rows, 1), 0, top)
    return jnp.take_along_axis(grid, (jnp.arange(top)[None, :] + offset_by) % top, axis=1)


def portions_of(number_of, total, bound, slope, full):
    loads = [(1 << 20) // math.isqrt(rank ** slope) + 1 for rank in range(1, number_of + 1)]
    largest = bound if full else min(bound, max(-(-total // number_of), total * loads[0] // sum(loads)))
    least = 1 if total - largest >= number_of - 1 else 0
    counts, spare = [largest] + [least] * (number_of - 1), total - largest - least * (number_of - 1)
    while spare > 0:
        movable = [i for i in range(1, number_of) if counts[i] < largest] or [i for i in range(1, number_of) if counts[i] < bound]
        pool, budget = sum([loads[i] for i in movable]), spare
        for i in movable:
            extra = min(bound - counts[i], max(1, budget * loads[i] // pool), spare)
            counts[i] = counts[i] + extra
            spare = spare - extra
    return np.array(counts)


def bell_draw(key, dims, deviation, bound, kind=jnp.bfloat16):
    return jnp.clip(deviation * jax.random.normal(key, dims, jnp.float32), -bound, bound).astype(kind)


def setup_inputs(seed: int = 0) -> dict:
    keys = jax.random.split(jax.random.key(seed), 9)
    tokens = draw_tokens(jax.random.fold_in(keys[8], 71), 0)
    gain = jnp.clip(1.0 + 0.1 * jax.random.normal(keys[1], (D,), jnp.float32), 0.5, 1.5).astype(jnp.bfloat16)
    w_qkv = draw_w_qkv(jax.random.fold_in(keys[8], 71), 0)
    w_proj = bell_draw(keys[3], (D, D), (D / 25) ** -0.5, 1.0)
    scene_first = plant((jax.random.randint(keys[4], (SLABS,), 0, 4) < 1).astype(jnp.int32), jax.random.fold_in(keys[4], 1), 0, 1)
    window_valid = plant((jax.random.randint(keys[5], (SLABS, PANELS), 0, 4) < 3).astype(jnp.int32), jax.random.fold_in(keys[5], 1), 0, 1)
    partner_tile_keys = jax.random.split(jax.random.fold_in(keys[6], 1), SCENE_ROWS * TILES * PANELS // PANELS)
    partner_tile_turns = jax.random.permutation(jax.random.fold_in(keys[6], 3), SCENE_ROWS * TILES * PANELS // PANELS)
    partner_tile = jax.vmap(lambda own, number: assign_block(jax.random.fold_in(keys[6], 2), own, number, PANELS, TILES, 1, CAP, 2))(partner_tile_keys, partner_tile_turns).reshape((SCENE_ROWS, TILES, PANELS, 1))
    partner_panel = plant(jax.random.randint(keys[7], (SCENE_ROWS, TILES, PANELS), 0, PANELS), jax.random.fold_in(keys[7], 1), 0, PANELS - 1).astype(jnp.int32)
    return {"tokens": tokens, "gain": gain, "w_qkv": w_qkv, "w_proj": w_proj, "scene_first": scene_first, "window_valid": window_valid, "partner_tile": partner_tile, "partner_panel": partner_panel}


NORM_EPS = 1e-05

def to_panels(grid_in):
    feat_dim = grid_in.shape[2]
    blocks = grid_in.shape[1] // 16
    return grid_in.reshape(2, 8, blocks, 16, feat_dim).transpose(0, 2, 1, 3, 4).reshape(2 * blocks, 128, feat_dim)

def from_panels(panel_in):
    feat_dim = panel_in.shape[2]
    blocks = panel_in.shape[0] // 2
    return panel_in.reshape(2, blocks, 8, 16, feat_dim).transpose(0, 2, 1, 3, 4).reshape(16, blocks * 16, feat_dim)

def normalize(flat_in, gain):
    values = flat_in.astype(jnp.float32)
    centred = values - lax.optimization_barrier(jnp.mean(values, axis=-1, keepdims=True))
    spread = lax.optimization_barrier(jnp.mean(centred * centred, axis=-1, keepdims=True))
    return (centred * lax.rsqrt(spread + NORM_EPS) * gain.astype(jnp.float32)).astype(jnp.bfloat16)

def attend(queries, key_rows, value_rows, key_keep, head_count):
    panel_count, query_rows, feat_dim = queries.shape
    key_length = key_rows.shape[1]
    head_width = feat_dim // head_count
    query_heads = queries.astype(jnp.float32).reshape(panel_count, query_rows, head_count, head_width)
    key_heads = key_rows.astype(jnp.float32).reshape(panel_count, key_length, head_count, head_width)
    value_heads = value_rows.astype(jnp.float32).reshape(panel_count, key_length, head_count, head_width)
    scores = jnp.einsum('pqhd,pkhd->phqk', query_heads, key_heads) * head_width ** (-0.5)
    scores = jnp.where(key_keep[:, None, None, :], scores, -jnp.inf)
    row_max = lax.optimization_barrier(jnp.max(scores, axis=-1, keepdims=True))
    exponent = jnp.exp(scores - row_max)
    weights = (exponent / lax.optimization_barrier(jnp.sum(exponent, axis=-1, keepdims=True))).astype(jnp.bfloat16)
    mixed_out = jnp.einsum('phqk,pkhd->pqhd', weights.astype(jnp.float32), value_heads)
    return mixed_out.reshape(panel_count, query_rows, feat_dim)

def reference(tokens, gain, w_qkv, w_proj, scene_first, window_valid, partner_tile, partner_panel):
    slab_count = tokens.shape[0]
    feat_dim = tokens.shape[3]

    def project_slab(grid_in):
        normed = normalize(grid_in.reshape(-1, feat_dim), gain)
        packed = jnp.dot(normed, w_qkv, preferred_element_type=jnp.float32).astype(jnp.bfloat16)
        return to_panels(packed.reshape(grid_in.shape[0], grid_in.shape[1], 3 * feat_dim))
    panels = lax.map(project_slab, tokens)
    panel_count = panels.shape[1]
    halfway = panel_count // 2

    def one_slab(slab_index):
        own_panels = panels[slab_index]
        before = panels[jnp.maximum(slab_index - 1, 0)]
        after_index = jnp.minimum(slab_index + 1, slab_count - 1)
        after = panels[after_index]
        own_first = jnp.logical_or(scene_first[slab_index] == 1, slab_index == 0)
        next_first = jnp.logical_or(scene_first[after_index] == 1, slab_index + 1 >= slab_count)
        upper = jnp.concatenate([before[halfway:], own_panels[:halfway]], axis=1)
        lower = jnp.concatenate([own_panels[halfway:], after[:halfway]], axis=1)
        window_keys = jnp.concatenate([upper, lower], axis=0)
        always = jnp.ones((128,), dtype=bool)
        keep_upper = jnp.concatenate([jnp.broadcast_to(jnp.logical_not(own_first), (128,)), always])
        keep_lower = jnp.concatenate([always, jnp.broadcast_to(jnp.logical_not(next_first), (128,))])
        key_keep = jnp.concatenate([jnp.broadcast_to(keep_upper, (halfway, 256)), jnp.broadcast_to(keep_lower, (halfway, 256))], axis=0)
        queries = own_panels[:, :, :feat_dim]
        own_mix = attend(queries, window_keys[:, :, feat_dim:2 * feat_dim], window_keys[:, :, 2 * feat_dim:], key_keep, HEADS)
        scene_index = slab_index // TILES
        tile_index = slab_index % TILES
        partner_slabs = scene_index * TILES + partner_tile[scene_index, tile_index, :, 0]
        matched = panels[partner_slabs, partner_panel[scene_index, tile_index]]
        cross_mix = attend(queries, matched[:, :, feat_dim:2 * feat_dim], matched[:, :, 2 * feat_dim:], jnp.ones((panel_count, 128), dtype=bool), HEADS).astype(jnp.bfloat16)
        window_gate = window_valid[slab_index].astype(jnp.float32)[:, None, None]
        blended = (window_gate * own_mix + cross_mix.astype(jnp.float32)).astype(jnp.bfloat16)
        grid_out = from_panels(blended)
        result = jnp.dot(grid_out.reshape(-1, feat_dim), w_proj, preferred_element_type=jnp.float32).astype(jnp.bfloat16)
        return result.reshape(grid_out.shape)
    return lax.map(one_slab, jnp.arange(slab_count, dtype=jnp.int32))
```

```python
import functools

import jax
import jax.numpy as jnp
from jax import lax
from jax.experimental import pallas as pl
from jax.experimental.pallas import tpu as pltpu
from jax.sharding import PartitionSpec as P

HEADS = 16
NORM_EPS = 1e-05
LOG2E = 1.4426950408889634
VMEM_LIMIT = 56 * 1024 * 1024
GROUP = 4


def layer_norm(rows, gain_row):
    values = rows.astype(jnp.float32)
    centred = values - jnp.mean(values, axis=-1, keepdims=True)
    spread = jnp.mean(centred * centred, axis=-1, keepdims=True)
    return (centred * lax.rsqrt(spread + NORM_EPS) * gain_row.astype(jnp.float32)).astype(jnp.bfloat16)


def dot_f32(left, right):
    return jnp.dot(left, right, preferred_element_type=jnp.float32)


def dot_t(left, right):
    return lax.dot_general(left, right, (((1,), (1,)), ((), ())), preferred_element_type=jnp.float32)


def low_lanes(rows, width, head_width):
    return lax.broadcasted_iota(jnp.int32, (rows, width), 1) < head_width


def pack_kernel(tiles, panels, cap, me_ref, tile_ref, panel_ref, tok_ref, *rest):
    outs, sems = rest[: tiles - 1], rest[tiles - 1]
    me = me_ref[0]
    counts = []
    for r in range(1, tiles):
        asker = me ^ r
        out = outs[r - 1]

        def body(p, count, asker=asker, out=out, r=r):
            hit = jnp.logical_and(tile_ref[asker * panels + p] == me, count < cap)

            @pl.when(hit)
            def _():
                j = panel_ref[asker * panels + p]
                pltpu.make_async_copy(
                    tok_ref.at[j // (panels // 2), :, j % (panels // 2)], out.at[count], sems.at[r, count]
                ).start()

            return count + hit.astype(jnp.int32)

        counts.append(lax.fori_loop(0, panels, body, jnp.int32(0)))
    for r in range(1, tiles):
        for c in range(cap):

            @pl.when(c < counts[r - 1])
            def _(r=r, c=c):
                pltpu.make_async_copy(tok_ref.at[0, :, 0], outs[r - 1].at[c], sems.at[r, c]).wait()


def pack(me, tile_table, panel_table, tok, tiles, cap):
    panels = 2 * tok.shape[2]
    block = (cap, tok.shape[1], tok.shape[3], tok.shape[4])
    smem = pl.BlockSpec(memory_space=pltpu.SMEM)
    anym = pl.BlockSpec(memory_space=pl.ANY)
    return pl.pallas_call(
        functools.partial(pack_kernel, tiles, panels, cap),
        out_shape=[jax.ShapeDtypeStruct(block, tok.dtype)] * (tiles - 1),
        in_specs=[smem, smem, smem, anym],
        out_specs=[anym] * (tiles - 1),
        scratch_shapes=[pltpu.SemaphoreType.DMA((tiles, cap))],
        cost_estimate=pl.CostEstimate(flops=0, bytes_accessed=16 << 20, transcendentals=0),
    )(me, tile_table, panel_table, tok)


def qkv_kernel(tok_ref, gain_ref, w_ref, q_ref, kv_ref):
    dims = tok_ref.shape
    feat = dims[-1]
    rows = dims[1] * dims[2] * dims[3]
    normed = layer_norm(tok_ref[...].reshape(rows, feat), gain_ref[...])
    q_ref[...] = dot_f32(normed, w_ref[:, :feat]).astype(jnp.bfloat16).reshape(q_ref.shape)
    kv_ref[...] = dot_f32(normed, w_ref[:, feat:]).astype(jnp.bfloat16).reshape(kv_ref.shape)


def project_own(tok, gain_row, w_qkv):
    halves, deep, wide, run, feat = tok.shape
    step = deep // 2
    spec = lambda width: pl.BlockSpec((1, step, wide, run, width), lambda i: (i // 2, i % 2, 0, 0, 0))
    tokens = halves * deep * wide * run
    return pl.pallas_call(
        qkv_kernel,
        grid=(halves * 2,),
        out_shape=[
            jax.ShapeDtypeStruct((halves, deep, wide, run, feat), jnp.bfloat16),
            jax.ShapeDtypeStruct((halves, deep, wide, run, 2 * feat), jnp.bfloat16),
        ],
        in_specs=[
            spec(feat),
            pl.BlockSpec((1, feat), lambda i: (0, 0)),
            pl.BlockSpec((feat, 3 * feat), lambda i: (0, 0), pipeline_mode=pl.Buffered(1)),
        ],
        out_specs=[spec(feat), spec(2 * feat)],
        compiler_params=pltpu.CompilerParams(vmem_limit_bytes=VMEM_LIMIT),
        cost_estimate=pl.CostEstimate(
            flops=2 * tokens * feat * 3 * feat, bytes_accessed=tokens * feat * 8 + feat * feat * 6, transcendentals=0
        ),
    )(tok, gain_row, w_qkv)


def window_kernel(head_width, keep_ref, edge_ref, q_ref, kvo_ref, gain_ref, w_ref, mix_ref, kv_s):
    deep, group, run, feat = edge_ref.shape
    length = deep * run
    rows = edge_ref[...].reshape(deep * group * run, feat)
    normed = layer_norm(rows, gain_ref[...])
    kv_s[...] = dot_f32(normed, w_ref[:, feat:]).astype(jnp.bfloat16).reshape(kv_s.shape)
    pair = 2 * head_width
    scale = LOG2E * head_width ** (-0.5)
    bias = jnp.where(
        jnp.logical_and(keep_ref[0] == 0, lax.broadcasted_iota(jnp.int32, (1, 2 * length), 1) < length), -jnp.inf, 0.0
    )
    low = low_lanes(length, pair, head_width)
    ones = jnp.ones((2 * length, pair), jnp.bfloat16)
    zero = jnp.zeros((length, pair), jnp.bfloat16)
    for i in range(group):

        def body(g, carry, i=i):
            at = pl.ds(pl.multiple_of(g * pair, pair), pair)
            at_v = pl.ds(pl.multiple_of(feat + g * pair, pair), pair)
            q = q_ref[0, :, i, :, at].reshape(length, pair)
            qs = jnp.concatenate([jnp.where(low, q, zero), jnp.where(low, zero, q)], axis=0)
            keys = jnp.concatenate(
                [kv_s[:, i, :, at].reshape(length, pair), kvo_ref[0, :, i, :, at].reshape(length, pair)], axis=0
            )
            vals = jnp.concatenate(
                [kv_s[:, i, :, at_v].reshape(length, pair), kvo_ref[0, :, i, :, at_v].reshape(length, pair)], axis=0
            )
            scores = dot_t(qs, keys) + bias
            peak = jnp.max(scores, axis=1, keepdims=True)
            weights = jnp.exp2((scores - peak) * scale).astype(jnp.bfloat16)
            both = dot_f32(weights, jnp.concatenate([vals, ones], axis=1))
            mixed = both[:, :pair] / both[:, pair:]
            out = jnp.where(low, mixed[:length], mixed[length:])
            mix_ref[:, i, :, at] = out.astype(jnp.bfloat16).reshape(deep, run, pair)
            return carry

        lax.fori_loop(0, feat // pair, body, 0, unroll=2)


def window_mix(half, keep, edge, q, kv_own, gain_row, w_qkv):
    deep, wide, run, feat = edge.shape
    group = min(GROUP, wide)
    head_width = feat // HEADS
    own = lambda width: pl.BlockSpec((1, deep, group, run, width), lambda i: (half, 0, i, 0, 0))
    flat = pl.BlockSpec((deep, group, run, feat), lambda i: (0, i, 0, 0))
    tokens = deep * wide * run
    return pl.pallas_call(
        functools.partial(window_kernel, head_width),
        grid=(wide // group,),
        out_shape=jax.ShapeDtypeStruct(edge.shape, jnp.bfloat16),
        in_specs=[
            pl.BlockSpec(memory_space=pltpu.SMEM),
            flat,
            own(feat),
            own(2 * feat),
            pl.BlockSpec((1, feat), lambda i: (0, 0)),
            pl.BlockSpec((feat, 3 * feat), lambda i: (0, 0), pipeline_mode=pl.Buffered(1)),
        ],
        out_specs=flat,
        scratch_shapes=[pltpu.VMEM((deep, group, run, 2 * feat), jnp.bfloat16)],
        compiler_params=pltpu.CompilerParams(vmem_limit_bytes=VMEM_LIMIT),
        cost_estimate=pl.CostEstimate(
            flops=2 * tokens * feat * 2 * feat + 8 * tokens * 256 * feat,
            bytes_accessed=tokens * feat * 10 + feat * feat * 6,
            transcendentals=tokens * 256 * HEADS,
        ),
    )(keep, edge, q, kv_own, gain_row, w_qkv)


def cross_kernel(tiles, head_width, group, me_ref, tile_ref, panel_ref, valid_ref, tok_ref, *rest):
    recv = rest[: tiles - 1]
    q_ref, up_ref, down_ref, gain_ref, w_ref, wp_ref, out_ref, got, kv_s, mixed_s, seen, sems = rest[tiles - 1 :]
    panels, deep, run, feat = got.shape
    half = panels // 2
    length = deep * run
    step = pl.program_id(0)
    me = me_ref[0]

    @pl.when(step == 0)
    def _():
        for t in range(tiles):
            seen[t] = 0

        def body(p, carry):
            source = tile_ref[me * panels + p]
            slot = seen[source]
            seen[source] = slot + 1
            j = panel_ref[me * panels + p]
            r = source ^ me

            @pl.when(r == 0)
            def _():
                pltpu.make_async_copy(tok_ref.at[j // half, :, j % half], got.at[p], sems.at[p]).start()

            for k in range(1, tiles):

                @pl.when(r == k)
                def _(k=k):
                    pltpu.make_async_copy(recv[k - 1].at[slot], got.at[p], sems.at[p]).start()

            return carry

        lax.fori_loop(0, panels, body, 0)

    for i in range(group):
        pltpu.make_async_copy(tok_ref.at[0, :, 0], got.at[step * group + i], sems.at[step * group + i]).wait()
    rows = got[pl.ds(step * group, group)].reshape(group * length, feat)
    normed = layer_norm(rows, gain_ref[...])
    kv_s[...] = dot_f32(normed, w_ref[:, feat:]).astype(jnp.bfloat16)
    pair = 2 * head_width
    scale = LOG2E * head_width ** (-0.5)
    low = low_lanes(length, pair, head_width)
    zero = jnp.zeros((length, pair), jnp.bfloat16)
    one = jnp.ones((length, pair), jnp.bfloat16)
    marks = jnp.concatenate([jnp.where(low, one, zero), jnp.where(low, zero, one)], axis=0)
    upper = step < half // group
    for i in range(group):
        gate = valid_ref[step * group + i].astype(jnp.float32)

        def body(g, carry, i=i, gate=gate):
            at = pl.ds(pl.multiple_of(g * pair, pair), pair)
            at_v = pl.ds(pl.multiple_of(feat + g * pair, pair), pair)
            q = q_ref[0, :, i, :, at].reshape(length, pair)
            key = kv_s[i * length : (i + 1) * length, at]
            val = kv_s[i * length : (i + 1) * length, at_v]
            keys = jnp.concatenate([jnp.where(low, key, zero), jnp.where(low, zero, key)], axis=0)
            vals = jnp.concatenate([jnp.where(low, val, zero), jnp.where(low, zero, val)], axis=0)
            scores = dot_t(q, keys)
            parts = []
            for h in range(2):
                part = scores[:, h * length : (h + 1) * length]
                peak = jnp.max(part, axis=1, keepdims=True)
                parts.append(jnp.exp2((part - peak) * scale).astype(jnp.bfloat16))
            both = dot_f32(jnp.concatenate(parts, axis=1), jnp.concatenate([vals, marks], axis=1))
            cross = (both[:, :pair] / both[:, pair:]).astype(jnp.bfloat16)
            own = jnp.where(
                upper, up_ref[:, i, :, at].reshape(length, pair), down_ref[:, i, :, at].reshape(length, pair)
            )
            blended = gate * own.astype(jnp.float32) + cross.astype(jnp.float32)
            mixed_s[i * length : (i + 1) * length, at] = blended.astype(jnp.bfloat16)
            return carry

        lax.fori_loop(0, feat // pair, body, 0, unroll=2)
    result = dot_f32(mixed_s[...], wp_ref[...]).astype(jnp.bfloat16)
    for i in range(group):
        out_ref[0, :, i] = result[i * length : (i + 1) * length].reshape(deep, run, feat)


def cross_and_project(me, tile_table, panel_table, valid, tok, recv, q, mix_up, mix_down, gain_row, w_qkv, w_proj):
    halves, deep, wide, run, feat = tok.shape
    panels = halves * wide
    tiles = len(recv) + 1
    group = min(GROUP, wide)
    per_half = wide // group
    head_width = feat // HEADS
    length = deep * run
    smem = pl.BlockSpec(memory_space=pltpu.SMEM)
    anym = pl.BlockSpec(memory_space=pl.ANY)
    whole = pl.BlockSpec((1, deep, group, run, feat), lambda i: (i // per_half, 0, i % per_half, 0, 0))
    up = pl.BlockSpec((deep, group, run, feat), lambda i: (0, jnp.minimum(i, per_half - 1), 0, 0))
    down = pl.BlockSpec((deep, group, run, feat), lambda i: (0, jnp.maximum(i - per_half, 0), 0, 0))
    tokens = panels * length
    return pl.pallas_call(
        functools.partial(cross_kernel, tiles, head_width, group),
        grid=(panels // group,),
        out_shape=jax.ShapeDtypeStruct(tok.shape, jnp.bfloat16),
        in_specs=[smem, smem, smem, smem, anym]
        + [anym] * (tiles - 1)
        + [
            whole,
            up,
            down,
            pl.BlockSpec((1, feat), lambda i: (0, 0)),
            pl.BlockSpec((feat, 3 * feat), lambda i: (0, 0), pipeline_mode=pl.Buffered(1)),
            pl.BlockSpec((feat, feat), lambda i: (0, 0), pipeline_mode=pl.Buffered(1)),
        ],
        out_specs=whole,
        scratch_shapes=[
            pltpu.VMEM((panels, deep, run, feat), jnp.bfloat16),
            pltpu.VMEM((group * length, 2 * feat), jnp.bfloat16),
            pltpu.VMEM((group * length, feat), jnp.bfloat16),
            pltpu.SMEM((tiles,), jnp.int32),
            pltpu.SemaphoreType.DMA((panels,)),
        ],
        compiler_params=pltpu.CompilerParams(vmem_limit_bytes=VMEM_LIMIT),
        cost_estimate=pl.CostEstimate(
            flops=2 * tokens * feat * 3 * feat + 8 * tokens * 128 * feat,
            bytes_accessed=tokens * feat * 8 + feat * feat * 8,
            transcendentals=tokens * 128 * HEADS,
        ),
    )(me, tile_table, panel_table, valid, tok, *recv, q, mix_up, mix_down, gain_row, w_qkv, w_proj)


def per_device(tokens, gain, w_qkv, w_proj, scene_first, window_valid, partner_tile, partner_panel):
    _, tok_rows, tok_cols, feat = tokens.shape
    run = 16
    wide = tok_cols // run
    tok = tokens.reshape(2, tok_rows // 2, wide, run, feat)
    gain_row = gain.reshape(1, feat)
    tiles = partner_tile.shape[1]
    panels = partner_tile.shape[2]
    cap = 2 * max(1, panels // tiles)
    slab_count = scene_first.shape[0]
    forward = [(i, i + 1) for i in range(slab_count - 1)]
    backward = [(i + 1, i) for i in range(slab_count - 1)]
    before = lax.ppermute(tok[1], ("scene", "tile"), forward)
    after = lax.ppermute(tok[0], ("scene", "tile"), backward)

    me = lax.axis_index("tile").reshape(1).astype(jnp.int32)
    tile_table = partner_tile.reshape(tiles * panels)
    panel_table = partner_panel.reshape(tiles * panels)
    outgoing = pack(me, tile_table, panel_table, tok, tiles, cap)
    recv = [
        lax.ppermute(outgoing[r - 1], "tile", [(i, i ^ r) for i in range(tiles)]) for r in range(1, tiles)
    ]

    slab_index = lax.axis_index(("scene", "tile"))
    after_index = jnp.minimum(slab_index + 1, slab_count - 1)
    own_first = jnp.logical_or(scene_first[slab_index] == 1, slab_index == 0)
    next_first = jnp.logical_or(scene_first[after_index] == 1, slab_index + 1 >= slab_count)
    keep_before = jnp.logical_not(own_first).astype(jnp.int32).reshape(1)
    keep_after = jnp.logical_not(next_first).astype(jnp.int32).reshape(1)

    q, kv = project_own(tok, gain_row, w_qkv)
    mix_up = window_mix(0, keep_before, before, q, kv, gain_row, w_qkv)
    mix_down = window_mix(1, keep_after, after, q, kv, gain_row, w_qkv)
    valid = window_valid.reshape(panels)
    out = cross_and_project(
        me, tile_table, panel_table, valid, tok, recv, q, mix_up, mix_down, gain_row, w_qkv, w_proj
    )
    return out.reshape(tokens.shape)


def solution(mesh):
    in_specs = (
        P(("scene", "tile"), None, None, None),
        P(),
        P(),
        P(),
        P(),
        P(("scene", "tile"), None),
        P("scene", None, None, None),
        P("scene", None, None),
    )
    out_specs = P(("scene", "tile"), None, None, None)
    return jax.shard_map(per_device, mesh=mesh, in_specs=in_specs, out_specs=out_specs, check_vma=False)
```

```python
import functools

import jax
import jax.numpy as jnp
from jax import lax
from jax.experimental import pallas as pl
from jax.experimental.pallas import tpu as pltpu
from jax.sharding import PartitionSpec as P

HEADS = 16
NORM_EPS = 1e-05
LOG2E = 1.4426950408889634
VMEM_LIMIT = 56 * 1024 * 1024
GROUP = 4


def layer_norm(rows, gain_row):
    values = rows.astype(jnp.float32)
    centred = values - jnp.mean(values, axis=-1, keepdims=True)
    spread = jnp.mean(centred * centred, axis=-1, keepdims=True)
    return (centred * lax.rsqrt(spread + NORM_EPS) * gain_row.astype(jnp.float32)).astype(jnp.bfloat16)


def dot_f32(left, right):
    return jnp.dot(left, right, preferred_element_type=jnp.float32)


def dot_t(left, right):
    return lax.dot_general(left, right, (((1,), (1,)), ((), ())), preferred_element_type=jnp.float32)


def staged(count, first, second):
    held = first(0)
    for g in range(count):
        coming = first(g + 1) if g + 1 < count else None
        second(g, held)
        held = coming


def low_lanes(rows, width, head_width):
    return lax.broadcasted_iota(jnp.int32, (rows, width), 1) < head_width


def pack_kernel(tiles, panels, cap, me_ref, tile_ref, panel_ref, tok_ref, *rest):
    outs, slab, sem, sems = rest[: tiles - 1], rest[tiles - 1], rest[tiles], rest[tiles + 1]
    me = me_ref[0]
    load = pltpu.make_async_copy(tok_ref, slab, sem)
    load.start()
    load.wait()
    counts = []
    for r in range(1, tiles):
        asker = me ^ r
        out = outs[r - 1]

        def body(p, count, asker=asker, out=out, r=r):
            hit = jnp.logical_and(tile_ref[asker * panels + p] == me, count < cap)

            @pl.when(hit)
            def _():
                j = panel_ref[asker * panels + p]
                pltpu.make_async_copy(
                    slab.at[j // (panels // 2), :, j % (panels // 2)], out.at[count], sems.at[r, count]
                ).start()

            return count + hit.astype(jnp.int32)

        counts.append(lax.fori_loop(0, panels, body, jnp.int32(0)))
    for r in range(1, tiles):
        for c in range(cap):

            @pl.when(c < counts[r - 1])
            def _(r=r, c=c):
                pltpu.make_async_copy(slab.at[0, :, 0], outs[r - 1].at[c], sems.at[r, c]).wait()


def pack(me, tile_table, panel_table, tok, tiles, cap):
    panels = 2 * tok.shape[2]
    block = (cap, tok.shape[1], tok.shape[3], tok.shape[4])
    smem = pl.BlockSpec(memory_space=pltpu.SMEM)
    anym = pl.BlockSpec(memory_space=pl.ANY)
    return pl.pallas_call(
        functools.partial(pack_kernel, tiles, panels, cap),
        out_shape=[jax.ShapeDtypeStruct(block, tok.dtype)] * (tiles - 1),
        in_specs=[smem, smem, smem, anym],
        out_specs=[anym] * (tiles - 1),
        scratch_shapes=[
            pltpu.VMEM(tok.shape, tok.dtype),
            pltpu.SemaphoreType.DMA,
            pltpu.SemaphoreType.DMA((tiles, cap)),
        ],
        cost_estimate=pl.CostEstimate(flops=0, bytes_accessed=16 << 20, transcendentals=0),
    )(me, tile_table, panel_table, tok)


def qkv_kernel(tok_ref, gain_ref, w_ref, q_ref, kv_ref):
    dims = tok_ref.shape
    feat = dims[-1]
    rows = dims[1] * dims[2] * dims[3]
    normed = layer_norm(tok_ref[...].reshape(rows, feat), gain_ref[...])
    q_ref[...] = dot_f32(normed, w_ref[:, :feat]).astype(jnp.bfloat16).reshape(q_ref.shape)
    kv_ref[...] = dot_f32(normed, w_ref[:, feat:]).astype(jnp.bfloat16).reshape(kv_ref.shape)


def project_own(tok, gain_row, w_qkv):
    halves, deep, wide, run, feat = tok.shape
    step = deep // 2
    spec = lambda width: pl.BlockSpec((1, step, wide, run, width), lambda i: (i // 2, i % 2, 0, 0, 0))
    tokens = halves * deep * wide * run
    return pl.pallas_call(
        qkv_kernel,
        grid=(halves * 2,),
        out_shape=[
            jax.ShapeDtypeStruct((halves, deep, wide, run, feat), jnp.bfloat16),
            jax.ShapeDtypeStruct((halves, deep, wide, run, 2 * feat), jnp.bfloat16),
        ],
        in_specs=[
            spec(feat),
            pl.BlockSpec((1, feat), lambda i: (0, 0)),
            pl.BlockSpec((feat, 3 * feat), lambda i: (0, 0), pipeline_mode=pl.Buffered(1)),
        ],
        out_specs=[spec(feat), spec(2 * feat)],
        compiler_params=pltpu.CompilerParams(vmem_limit_bytes=VMEM_LIMIT),
        cost_estimate=pl.CostEstimate(
            flops=2 * tokens * feat * 3 * feat, bytes_accessed=tokens * feat * 8 + feat * feat * 6, transcendentals=0
        ),
    )(tok, gain_row, w_qkv)


def window_kernel(head_width, keep_ref, edge_ref, q_ref, kvo_ref, gain_ref, w_ref, mix_ref, kv_s):
    deep, group, run, feat = edge_ref.shape
    length = deep * run
    rows = edge_ref[...].reshape(deep * group * run, feat)
    normed = layer_norm(rows, gain_ref[...])
    kv_s[...] = dot_f32(normed, w_ref[:, feat:]).astype(jnp.bfloat16).reshape(kv_s.shape)
    pair = 2 * head_width
    scale = LOG2E * head_width ** (-0.5)
    bias = jnp.where(
        jnp.logical_and(keep_ref[0] == 0, lax.broadcasted_iota(jnp.int32, (1, 2 * length), 1) < length), -jnp.inf, 0.0
    )
    low = low_lanes(length, pair, head_width)
    ones = jnp.ones((2 * length, pair), jnp.bfloat16)
    zero = jnp.zeros((length, pair), jnp.bfloat16)
    def panel(i, carry):
        def score(g):
            at = slice(g * pair, (g + 1) * pair)
            q = q_ref[0, :, i, :, at].reshape(length, pair)
            qs = jnp.concatenate([jnp.where(low, q, zero), jnp.where(low, zero, q)], axis=0)
            keys = jnp.concatenate(
                [kv_s[:, i, :, at].reshape(length, pair), kvo_ref[0, :, i, :, at].reshape(length, pair)], axis=0
            )
            return dot_t(qs, keys) + bias

        def mix(g, scores):
            at_v = slice(feat + g * pair, feat + (g + 1) * pair)
            vals = jnp.concatenate(
                [kv_s[:, i, :, at_v].reshape(length, pair), kvo_ref[0, :, i, :, at_v].reshape(length, pair)], axis=0
            )
            peak = jnp.max(scores, axis=1, keepdims=True)
            weights = jnp.exp2((scores - peak) * scale).astype(jnp.bfloat16)
            both = dot_f32(weights, jnp.concatenate([vals, ones], axis=1))
            mixed = both[:, :pair] / both[:, pair:]
            out = jnp.where(low, mixed[:length], mixed[length:])
            mix_ref[:, i, :, g * pair : (g + 1) * pair] = out.astype(jnp.bfloat16).reshape(deep, run, pair)

        staged(feat // pair, score, mix)
        return carry

    lax.fori_loop(0, group, panel, 0)


def window_mix(half, keep, edge, q, kv_own, gain_row, w_qkv):
    deep, wide, run, feat = edge.shape
    group = min(GROUP, wide)
    head_width = feat // HEADS
    own = lambda width: pl.BlockSpec((1, deep, group, run, width), lambda i: (half, 0, i, 0, 0))
    flat = pl.BlockSpec((deep, group, run, feat), lambda i: (0, i, 0, 0))
    tokens = deep * wide * run
    return pl.pallas_call(
        functools.partial(window_kernel, head_width),
        grid=(wide // group,),
        out_shape=jax.ShapeDtypeStruct(edge.shape, jnp.bfloat16),
        in_specs=[
            pl.BlockSpec(memory_space=pltpu.SMEM),
            flat,
            own(feat),
            own(2 * feat),
            pl.BlockSpec((1, feat), lambda i: (0, 0)),
            pl.BlockSpec((feat, 3 * feat), lambda i: (0, 0), pipeline_mode=pl.Buffered(1)),
        ],
        out_specs=flat,
        scratch_shapes=[pltpu.VMEM((deep, group, run, 2 * feat), jnp.bfloat16)],
        compiler_params=pltpu.CompilerParams(vmem_limit_bytes=VMEM_LIMIT),
        cost_estimate=pl.CostEstimate(
            flops=2 * tokens * feat * 2 * feat + 8 * tokens * 256 * feat,
            bytes_accessed=tokens * feat * 10 + feat * feat * 6,
            transcendentals=tokens * 256 * HEADS,
        ),
    )(keep, edge, q, kv_own, gain_row, w_qkv)


def cross_kernel(tiles, head_width, group, me_ref, tile_ref, panel_ref, valid_ref, tok_ref, *rest):
    recv = rest[: tiles - 1]
    q_ref, up_ref, down_ref, gain_ref, w_ref, wp_ref, out_ref, got, kv_s, mixed_s, seen, sems = rest[tiles - 1 :]
    panels, deep, run, feat = got.shape
    half = panels // 2
    length = deep * run
    step = pl.program_id(0)
    me = me_ref[0]

    @pl.when(step == 0)
    def _():
        for t in range(tiles):
            seen[t] = 0

        def body(p, carry):
            source = tile_ref[me * panels + p]
            slot = seen[source]
            seen[source] = slot + 1
            j = panel_ref[me * panels + p]
            r = source ^ me

            @pl.when(r == 0)
            def _():
                pltpu.make_async_copy(tok_ref.at[j // half, :, j % half], got.at[p], sems.at[p]).start()

            for k in range(1, tiles):

                @pl.when(r == k)
                def _(k=k):
                    pltpu.make_async_copy(recv[k - 1].at[slot], got.at[p], sems.at[p]).start()

            return carry

        lax.fori_loop(0, panels, body, 0)

    for i in range(group):
        pltpu.make_async_copy(tok_ref.at[0, :, 0], got.at[step * group + i], sems.at[step * group + i]).wait()
    rows = got[pl.ds(step * group, group)].reshape(group * length, feat)
    normed = layer_norm(rows, gain_ref[...])
    kv_s[...] = dot_f32(normed, w_ref[:, feat:]).astype(jnp.bfloat16)
    pair = 2 * head_width
    scale = LOG2E * head_width ** (-0.5)
    low = low_lanes(length, pair, head_width)
    zero = jnp.zeros((length, pair), jnp.bfloat16)
    one = jnp.ones((length, pair), jnp.bfloat16)
    marks = jnp.concatenate([jnp.where(low, one, zero), jnp.where(low, zero, one)], axis=0)
    upper = step < half // group
    def panel(i, carry):
        gate = valid_ref[step * group + i].astype(jnp.float32)
        rows_i = pl.ds(pl.multiple_of(i * length, length), length)

        def score(g):
            at = slice(g * pair, (g + 1) * pair)
            q = q_ref[0, :, i, :, at].reshape(length, pair)
            key = kv_s[rows_i, at]
            keys = jnp.concatenate([jnp.where(low, key, zero), jnp.where(low, zero, key)], axis=0)
            return dot_t(q, keys)

        def mix(g, scores):
            at = slice(g * pair, (g + 1) * pair)
            val = kv_s[rows_i, feat + g * pair : feat + (g + 1) * pair]
            vals = jnp.concatenate([jnp.where(low, val, zero), jnp.where(low, zero, val)], axis=0)
            parts = []
            for h in range(2):
                part = scores[:, h * length : (h + 1) * length]
                peak = jnp.max(part, axis=1, keepdims=True)
                parts.append(jnp.exp2((part - peak) * scale).astype(jnp.bfloat16))
            both = dot_f32(jnp.concatenate(parts, axis=1), jnp.concatenate([vals, marks], axis=1))
            cross = (both[:, :pair] / both[:, pair:]).astype(jnp.bfloat16)
            own = jnp.where(
                upper, up_ref[:, i, :, at].reshape(length, pair), down_ref[:, i, :, at].reshape(length, pair)
            )
            blended = gate * own.astype(jnp.float32) + cross.astype(jnp.float32)
            mixed_s[rows_i, at] = blended.astype(jnp.bfloat16)

        staged(feat // pair, score, mix)
        return carry

    lax.fori_loop(0, group, panel, 0)
    result = dot_f32(mixed_s[...], wp_ref[...]).astype(jnp.bfloat16)
    for i in range(group):
        out_ref[0, :, i] = result[i * length : (i + 1) * length].reshape(deep, run, feat)


def cross_and_project(me, tile_table, panel_table, valid, tok, recv, q, mix_up, mix_down, gain_row, w_qkv, w_proj):
    halves, deep, wide, run, feat = tok.shape
    panels = halves * wide
    tiles = len(recv) + 1
    group = min(GROUP, wide)
    per_half = wide // group
    head_width = feat // HEADS
    length = deep * run
    smem = pl.BlockSpec(memory_space=pltpu.SMEM)
    anym = pl.BlockSpec(memory_space=pl.ANY)
    whole = pl.BlockSpec((1, deep, group, run, feat), lambda i: (i // per_half, 0, i % per_half, 0, 0))
    up = pl.BlockSpec((deep, group, run, feat), lambda i: (0, jnp.minimum(i, per_half - 1), 0, 0))
    down = pl.BlockSpec((deep, group, run, feat), lambda i: (0, jnp.maximum(i - per_half, 0), 0, 0))
    tokens = panels * length
    return pl.pallas_call(
        functools.partial(cross_kernel, tiles, head_width, group),
        grid=(panels // group,),
        out_shape=jax.ShapeDtypeStruct(tok.shape, jnp.bfloat16),
        in_specs=[smem, smem, smem, smem, anym]
        + [anym] * (tiles - 1)
        + [
            whole,
            up,
            down,
            pl.BlockSpec((1, feat), lambda i: (0, 0)),
            pl.BlockSpec((feat, 3 * feat), lambda i: (0, 0), pipeline_mode=pl.Buffered(1)),
            pl.BlockSpec((feat, feat), lambda i: (0, 0), pipeline_mode=pl.Buffered(1)),
        ],
        out_specs=whole,
        scratch_shapes=[
            pltpu.VMEM((panels, deep, run, feat), jnp.bfloat16),
            pltpu.VMEM((group * length, 2 * feat), jnp.bfloat16),
            pltpu.VMEM((group * length, feat), jnp.bfloat16),
            pltpu.SMEM((tiles,), jnp.int32),
            pltpu.SemaphoreType.DMA((panels,)),
        ],
        compiler_params=pltpu.CompilerParams(vmem_limit_bytes=VMEM_LIMIT),
        cost_estimate=pl.CostEstimate(
            flops=2 * tokens * feat * 3 * feat + 8 * tokens * 128 * feat,
            bytes_accessed=tokens * feat * 8 + feat * feat * 8,
            transcendentals=tokens * 128 * HEADS,
        ),
    )(me, tile_table, panel_table, valid, tok, *recv, q, mix_up, mix_down, gain_row, w_qkv, w_proj)


def per_device(tokens, gain, w_qkv, w_proj, scene_first, window_valid, partner_tile, partner_panel):
    _, tok_rows, tok_cols, feat = tokens.shape
    run = 16
    wide = tok_cols // run
    tok = tokens.reshape(2, tok_rows // 2, wide, run, feat)
    gain_row = gain.reshape(1, feat)
    tiles = partner_tile.shape[1]
    panels = partner_tile.shape[2]
    cap = 2 * max(1, panels // tiles)
    slab_count = scene_first.shape[0]
    forward = [(i, i + 1) for i in range(slab_count - 1)]
    backward = [(i + 1, i) for i in range(slab_count - 1)]
    before = lax.ppermute(tok[1], ("scene", "tile"), forward)
    after = lax.ppermute(tok[0], ("scene", "tile"), backward)

    me = lax.axis_index("tile").reshape(1).astype(jnp.int32)
    tile_table = partner_tile.reshape(tiles * panels)
    panel_table = partner_panel.reshape(tiles * panels)
    outgoing = pack(me, tile_table, panel_table, tok, tiles, cap)
    recv = [
        lax.ppermute(outgoing[r - 1], "tile", [(i, i ^ r) for i in range(tiles)]) for r in range(1, tiles)
    ]

    slab_index = lax.axis_index(("scene", "tile"))
    after_index = jnp.minimum(slab_index + 1, slab_count - 1)
    own_first = jnp.logical_or(scene_first[slab_index] == 1, slab_index == 0)
    next_first = jnp.logical_or(scene_first[after_index] == 1, slab_index + 1 >= slab_count)
    keep_before = jnp.logical_not(own_first).astype(jnp.int32).reshape(1)
    keep_after = jnp.logical_not(next_first).astype(jnp.int32).reshape(1)

    q, kv = project_own(tok, gain_row, w_qkv)
    mix_up = window_mix(0, keep_before, before, q, kv, gain_row, w_qkv)
    mix_down = window_mix(1, keep_after, after, q, kv, gain_row, w_qkv)
    valid = window_valid.reshape(panels)
    out = cross_and_project(
        me, tile_table, panel_table, valid, tok, recv, q, mix_up, mix_down, gain_row, w_qkv, w_proj
    )
    return out.reshape(tokens.shape)


def solution(mesh):
    in_specs = (
        P(("scene", "tile"), None, None, None),
        P(),
        P(),
        P(),
        P(),
        P(("scene", "tile"), None),
        P("scene", None, None, None),
        P("scene", None, None),
    )
    out_specs = P(("scene", "tile"), None, None, None)
    return jax.shard_map(per_device, mesh=mesh, in_specs=in_specs, out_specs=out_specs, check_vma=False)
```

```python
import functools

import jax
import jax.numpy as jnp
from jax import lax
from jax.experimental import pallas as pl
from jax.experimental.pallas import tpu as pltpu
from jax.sharding import PartitionSpec as P

HEADS = 16
NORM_EPS = 1e-05
LOG2E = 1.4426950408889634
VMEM_LIMIT = 56 * 1024 * 1024
GROUP = 4


def layer_norm(rows, gain_row):
    values = rows.astype(jnp.float32)
    centred = values - jnp.mean(values, axis=-1, keepdims=True)
    spread = jnp.mean(centred * centred, axis=-1, keepdims=True)
    return (centred * lax.rsqrt(spread + NORM_EPS) * gain_row.astype(jnp.float32)).astype(jnp.bfloat16)


def dot_f32(left, right):
    return jnp.dot(left, right, preferred_element_type=jnp.float32)


def dot_t(left, right):
    return lax.dot_general(left, right, (((1,), (1,)), ((), ())), preferred_element_type=jnp.float32)


def staged(count, first, second):
    held = first(0)
    for g in range(count):
        coming = first(g + 1) if g + 1 < count else None
        second(g, held)
        held = coming


def low_lanes(rows, width, head_width):
    return lax.broadcasted_iota(jnp.int32, (rows, width), 1) < head_width


def pack_kernel(tiles, panels, cap, me_ref, tile_ref, panel_ref, tok_ref, *rest):
    outs, slab, sem, sems = rest[: tiles - 1], rest[tiles - 1], rest[tiles], rest[tiles + 1]
    me = me_ref[0]
    load = pltpu.make_async_copy(tok_ref, slab, sem)
    load.start()
    load.wait()
    counts = []
    for r in range(1, tiles):
        asker = me ^ r
        out = outs[r - 1]

        def body(p, count, asker=asker, out=out, r=r):
            hit = jnp.logical_and(tile_ref[asker * panels + p] == me, count < cap)

            @pl.when(hit)
            def _():
                j = panel_ref[asker * panels + p]
                pltpu.make_async_copy(
                    slab.at[j // (panels // 2), :, j % (panels // 2)], out.at[count], sems.at[r, count]
                ).start()

            return count + hit.astype(jnp.int32)

        counts.append(lax.fori_loop(0, panels, body, jnp.int32(0)))
    for r in range(1, tiles):
        for c in range(cap):

            @pl.when(c < counts[r - 1])
            def _(r=r, c=c):
                pltpu.make_async_copy(slab.at[0, :, 0], outs[r - 1].at[c], sems.at[r, c]).wait()


def pack(me, tile_table, panel_table, tok, tiles, cap):
    panels = 2 * tok.shape[2]
    block = (cap, tok.shape[1], tok.shape[3], tok.shape[4])
    smem = pl.BlockSpec(memory_space=pltpu.SMEM)
    anym = pl.BlockSpec(memory_space=pl.ANY)
    return pl.pallas_call(
        functools.partial(pack_kernel, tiles, panels, cap),
        out_shape=[jax.ShapeDtypeStruct(block, tok.dtype)] * (tiles - 1),
        in_specs=[smem, smem, smem, anym],
        out_specs=[anym] * (tiles - 1),
        scratch_shapes=[
            pltpu.VMEM(tok.shape, tok.dtype),
            pltpu.SemaphoreType.DMA,
            pltpu.SemaphoreType.DMA((tiles, cap)),
        ],
        cost_estimate=pl.CostEstimate(flops=0, bytes_accessed=16 << 20, transcendentals=0),
    )(me, tile_table, panel_table, tok)


def qkv_kernel(tok_ref, gain_ref, w_ref, q_ref, kv_ref):
    dims = tok_ref.shape
    feat = dims[-1]
    rows = dims[1] * dims[2] * dims[3]
    normed = layer_norm(tok_ref[...].reshape(rows, feat), gain_ref[...])
    q_ref[...] = dot_f32(normed, w_ref[:, :feat]).astype(jnp.bfloat16).reshape(q_ref.shape)
    kv_ref[...] = dot_f32(normed, w_ref[:, feat:]).astype(jnp.bfloat16).reshape(kv_ref.shape)


def project_own(tok, gain_row, w_qkv):
    halves, deep, wide, run, feat = tok.shape
    step = deep // 2
    spec = lambda width: pl.BlockSpec((1, step, wide, run, width), lambda i: (i // 2, i % 2, 0, 0, 0))
    tokens = halves * deep * wide * run
    return pl.pallas_call(
        qkv_kernel,
        grid=(halves * 2,),
        out_shape=[
            jax.ShapeDtypeStruct((halves, deep, wide, run, feat), jnp.bfloat16),
            jax.ShapeDtypeStruct((halves, deep, wide, run, 2 * feat), jnp.bfloat16),
        ],
        in_specs=[
            spec(feat),
            pl.BlockSpec((1, feat), lambda i: (0, 0)),
            pl.BlockSpec((feat, 3 * feat), lambda i: (0, 0), pipeline_mode=pl.Buffered(1)),
        ],
        out_specs=[spec(feat), spec(2 * feat)],
        compiler_params=pltpu.CompilerParams(vmem_limit_bytes=VMEM_LIMIT),
        cost_estimate=pl.CostEstimate(
            flops=2 * tokens * feat * 3 * feat, bytes_accessed=tokens * feat * 8 + feat * feat * 6, transcendentals=0
        ),
    )(tok, gain_row, w_qkv)


def window_kernel(head_width, keep_ref, edge_ref, q_ref, kvo_ref, gain_ref, w_ref, mix_ref, kv_s):
    deep, group, run, feat = edge_ref.shape
    length = deep * run
    rows = edge_ref[...].reshape(deep * group * run, feat)
    normed = layer_norm(rows, gain_ref[...])
    kv_s[...] = dot_f32(normed, w_ref[:, feat:]).astype(jnp.bfloat16).reshape(kv_s.shape)
    pair = 2 * head_width
    scale = LOG2E * head_width ** (-0.5)
    bias = jnp.where(
        jnp.logical_and(keep_ref[0] == 0, lax.broadcasted_iota(jnp.int32, (1, 2 * length), 1) < length), -jnp.inf, 0.0
    )
    low = low_lanes(length, pair, head_width)
    ones = jnp.ones((2 * length, pair), jnp.bfloat16)
    zero = jnp.zeros((length, pair), jnp.bfloat16)
    def panel(i, carry):
        def score(g):
            at = slice(g * pair, (g + 1) * pair)
            q = q_ref[0, :, i, :, at].reshape(length, pair)
            qs = jnp.concatenate([jnp.where(low, q, zero), jnp.where(low, zero, q)], axis=0)
            keys = jnp.concatenate(
                [kv_s[:, i, :, at].reshape(length, pair), kvo_ref[0, :, i, :, at].reshape(length, pair)], axis=0
            )
            return dot_t(qs, keys) + bias

        def mix(g, scores):
            at_v = slice(feat + g * pair, feat + (g + 1) * pair)
            vals = jnp.concatenate(
                [kv_s[:, i, :, at_v].reshape(length, pair), kvo_ref[0, :, i, :, at_v].reshape(length, pair)], axis=0
            )
            peak = jnp.max(scores, axis=1, keepdims=True)
            weights = jnp.exp2((scores - peak) * scale).astype(jnp.bfloat16)
            both = dot_f32(weights, jnp.concatenate([vals, ones], axis=1))
            mixed = both[:, :pair] / both[:, pair:]
            out = jnp.where(low, mixed[:length], mixed[length:])
            mix_ref[:, i, :, g * pair : (g + 1) * pair] = out.astype(jnp.bfloat16).reshape(deep, run, pair)

        staged(feat // pair, score, mix)
        return carry

    lax.fori_loop(0, group, panel, 0)


def window_mix(half, keep, edge, q, kv_own, gain_row, w_qkv):
    deep, wide, run, feat = edge.shape
    group = min(GROUP, wide)
    head_width = feat // HEADS
    own = lambda width: pl.BlockSpec((1, deep, group, run, width), lambda i: (half, 0, i, 0, 0))
    flat = pl.BlockSpec((deep, group, run, feat), lambda i: (0, i, 0, 0))
    tokens = deep * wide * run
    return pl.pallas_call(
        functools.partial(window_kernel, head_width),
        grid=(wide // group,),
        out_shape=jax.ShapeDtypeStruct(edge.shape, jnp.bfloat16),
        in_specs=[
            pl.BlockSpec(memory_space=pltpu.SMEM),
            flat,
            own(feat),
            own(2 * feat),
            pl.BlockSpec((1, feat), lambda i: (0, 0)),
            pl.BlockSpec((feat, 3 * feat), lambda i: (0, 0), pipeline_mode=pl.Buffered(1)),
        ],
        out_specs=flat,
        scratch_shapes=[pltpu.VMEM((deep, group, run, 2 * feat), jnp.bfloat16)],
        compiler_params=pltpu.CompilerParams(vmem_limit_bytes=VMEM_LIMIT),
        cost_estimate=pl.CostEstimate(
            flops=2 * tokens * feat * 2 * feat + 8 * tokens * 256 * feat,
            bytes_accessed=tokens * feat * 10 + feat * feat * 6,
            transcendentals=tokens * 256 * HEADS,
        ),
    )(keep, edge, q, kv_own, gain_row, w_qkv)


def cross_kernel(tiles, head_width, wanted, own_halves, refs):
    me_ref, tile_ref, panel_ref, valid_ref, tok_ref = refs[:5]
    recv = refs[5 : 4 + tiles]
    q_ref, mix_a, mix_b, gain_ref, wqkv_ref, wproj_ref = refs[4 + tiles : 10 + tiles]
    out_ref, got, q_s, own_s, res_s, wkv_s, wp_s, kv_s, mixed_s, seen, ids, w_sem, sems = refs[-13:]
    panels, deep, run, feat = got.shape
    half = panels // 2
    length = deep * run
    me = me_ref[0]
    for t in range(tiles):
        seen[t] = 0

    def fetch(p, count):
        source = tile_ref[me * panels + p]
        slot = seen[source]
        seen[source] = slot + 1
        r = source ^ me
        hit = ((wanted >> r) & 1) == 1

        @pl.when(hit)
        def _():
            ids[count] = p
            j = panel_ref[me * panels + p]

            @pl.when(r == 0)
            def _():
                pltpu.make_async_copy(tok_ref.at[j // half, :, j % half], got.at[count], sems.at[0, count]).start()

            for k in range(1, tiles):
                if (wanted >> k) & 1:

                    @pl.when(r == k)
                    def _(k=k):
                        pltpu.make_async_copy(recv[k - 1].at[slot], got.at[count], sems.at[0, count]).start()

            u = p // half
            w = p % half
            pltpu.make_async_copy(q_ref.at[u, :, w], q_s.at[count], sems.at[1, count]).start()

            @pl.when(u == own_halves[0])
            def _():
                pltpu.make_async_copy(mix_a.at[:, w], own_s.at[count], sems.at[2, count]).start()

            @pl.when(u == own_halves[1])
            def _():
                pltpu.make_async_copy(mix_b.at[:, w], own_s.at[count], sems.at[2, count]).start()

        return count + hit.astype(jnp.int32)

    load_wkv = pltpu.make_async_copy(wqkv_ref.at[:, feat:], wkv_s, w_sem.at[0])
    load_wp = pltpu.make_async_copy(wproj_ref, wp_s, w_sem.at[1])
    load_wkv.start()
    total = lax.fori_loop(0, panels, fetch, jnp.int32(0))
    load_wp.start()
    load_wkv.wait()
    load_wp.wait()

    pair = 2 * head_width
    scale = LOG2E * head_width ** (-0.5)
    low = low_lanes(length, pair, head_width)
    zero = jnp.zeros((length, pair), jnp.bfloat16)
    one = jnp.ones((length, pair), jnp.bfloat16)
    marks = jnp.concatenate([jnp.where(low, one, zero), jnp.where(low, zero, one)], axis=0)
    pairs = feat // pair

    def unit(n, carry):
        first = 2 * n
        for i in range(2):

            @pl.when(first + i < total)
            def _(i=i):
                for k, place in enumerate((got, q_s, own_s)):
                    pltpu.make_async_copy(tok_ref.at[0, :, 0], place.at[first + i], sems.at[k, first + i]).wait()

        rows = got[pl.ds(first, 2)].reshape(2 * length, feat)
        normed = layer_norm(rows, gain_ref[...])
        kv_s[...] = dot_f32(normed, wkv_s[...]).astype(jnp.bfloat16)
        gates = [valid_ref[ids[jnp.minimum(first + i, total - 1)]].astype(jnp.float32) for i in range(2)]

        def score(t):
            i, g = t // pairs, t % pairs
            at = slice(g * pair, (g + 1) * pair)
            q = q_s[first + i, :, :, at].reshape(length, pair)
            key = kv_s[i * length : (i + 1) * length, at]
            keys = jnp.concatenate([jnp.where(low, key, zero), jnp.where(low, zero, key)], axis=0)
            return dot_t(q, keys)

        def mix(t, scores):
            i, g = t // pairs, t % pairs
            at = slice(g * pair, (g + 1) * pair)
            val = kv_s[i * length : (i + 1) * length, feat + g * pair : feat + (g + 1) * pair]
            vals = jnp.concatenate([jnp.where(low, val, zero), jnp.where(low, zero, val)], axis=0)
            parts = []
            for h in range(2):
                part = scores[:, h * length : (h + 1) * length]
                peak = jnp.max(part, axis=1, keepdims=True)
                parts.append(jnp.exp2((part - peak) * scale).astype(jnp.bfloat16))
            both = dot_f32(jnp.concatenate(parts, axis=1), jnp.concatenate([vals, marks], axis=1))
            cross = (both[:, :pair] / both[:, pair:]).astype(jnp.bfloat16)
            own = own_s[first + i, :, :, at].reshape(length, pair)
            blended = gates[i] * own.astype(jnp.float32) + cross.astype(jnp.float32)
            mixed_s[i * length : (i + 1) * length, at] = blended.astype(jnp.bfloat16)

        staged(2 * pairs, score, mix)
        res_s[pl.ds(first, 2)] = dot_f32(mixed_s[...], wp_s[...]).astype(jnp.bfloat16).reshape(2, deep, run, feat)
        for i in range(2):

            @pl.when(first + i < total)
            def _(i=i):
                p = ids[first + i]
                pltpu.make_async_copy(
                    res_s.at[first + i], out_ref.at[p // half, :, p % half], sems.at[3, first + i]
                ).start()

        return carry

    lax.fori_loop(0, (total + 1) // 2, unit, 0)

    def finish(n, carry):
        pltpu.make_async_copy(res_s.at[n], out_ref.at[0, :, 0], sems.at[3, n]).wait()
        return carry

    lax.fori_loop(0, total, finish, 0)


def cross_and_project(wanted, me, tile_table, panel_table, valid, tok, recv, q, mixes, gain_row, w_qkv, w_proj, earlier):
    halves, deep, wide, run, feat = tok.shape
    panels = halves * wide
    tiles = len(recv) + 1
    head_width = feat // HEADS
    length = deep * run
    smem = pl.BlockSpec(memory_space=pltpu.SMEM)
    anym = pl.BlockSpec(memory_space=pl.ANY)
    share = bin(wanted).count("1") / tiles
    tokens = int(panels * length * share)
    many = pltpu.VMEM((panels, deep, run, feat), jnp.bfloat16)
    operands = [me, tile_table, panel_table, valid, tok, *recv, q, *mixes, gain_row, w_qkv, w_proj]
    specs = [smem] * 4 + [anym] * (tiles + 3) + [pl.BlockSpec((1, feat), lambda: (0, 0))] + [anym] * 2
    aliases = {}
    if earlier is not None:
        aliases = {len(operands): 0}
        operands.append(earlier)
        specs.append(anym)

    def kernel(*refs):
        cross_kernel(tiles, head_width, wanted, (0, 1), refs)

    return pl.pallas_call(
        kernel,
        out_shape=jax.ShapeDtypeStruct(tok.shape, jnp.bfloat16),
        in_specs=specs,
        out_specs=anym,
        scratch_shapes=[
            many,
            many,
            many,
            many,
            pltpu.VMEM((feat, 2 * feat), jnp.bfloat16),
            pltpu.VMEM((feat, feat), jnp.bfloat16),
            pltpu.VMEM((2 * length, 2 * feat), jnp.bfloat16),
            pltpu.VMEM((2 * length, feat), jnp.bfloat16),
            pltpu.SMEM((tiles,), jnp.int32),
            pltpu.SMEM((panels,), jnp.int32),
            pltpu.SemaphoreType.DMA((2,)),
            pltpu.SemaphoreType.DMA((4, panels)),
        ],
        input_output_aliases=aliases,
        compiler_params=pltpu.CompilerParams(vmem_limit_bytes=VMEM_LIMIT),
        cost_estimate=pl.CostEstimate(
            flops=2 * tokens * feat * 3 * feat + 8 * tokens * 128 * feat,
            bytes_accessed=tokens * feat * 8 + feat * feat * 6,
            transcendentals=tokens * 128 * HEADS,
        ),
    )(*operands)


def per_device(tokens, gain, w_qkv, w_proj, scene_first, window_valid, partner_tile, partner_panel):
    _, tok_rows, tok_cols, feat = tokens.shape
    run = 16
    wide = tok_cols // run
    tok = tokens.reshape(2, tok_rows // 2, wide, run, feat)
    gain_row = gain.reshape(1, feat)
    tiles = partner_tile.shape[1]
    panels = partner_tile.shape[2]
    cap = 2 * max(1, panels // tiles)
    slab_count = scene_first.shape[0]
    forward = [(i, i + 1) for i in range(slab_count - 1)]
    backward = [(i + 1, i) for i in range(slab_count - 1)]
    before = lax.ppermute(tok[1], ("scene", "tile"), forward)
    after = lax.ppermute(tok[0], ("scene", "tile"), backward)

    me = lax.axis_index("tile").reshape(1).astype(jnp.int32)
    tile_table = partner_tile.reshape(tiles * panels)
    panel_table = partner_panel.reshape(tiles * panels)
    outgoing = pack(me, tile_table, panel_table, tok, tiles, cap)
    recv = [
        lax.ppermute(outgoing[r - 1], "tile", [(i, i ^ r) for i in range(tiles)]) for r in range(1, tiles)
    ]

    slab_index = lax.axis_index(("scene", "tile"))
    after_index = jnp.minimum(slab_index + 1, slab_count - 1)
    own_first = jnp.logical_or(scene_first[slab_index] == 1, slab_index == 0)
    next_first = jnp.logical_or(scene_first[after_index] == 1, slab_index + 1 >= slab_count)
    keep_before = jnp.logical_not(own_first).astype(jnp.int32).reshape(1)
    keep_after = jnp.logical_not(next_first).astype(jnp.int32).reshape(1)

    q, kv = project_own(tok, gain_row, w_qkv)
    mix_up = window_mix(0, keep_before, before, q, kv, gain_row, w_qkv)
    mix_down = window_mix(1, keep_after, after, q, kv, gain_row, w_qkv)
    valid = window_valid.reshape(panels)
    out = None
    late = (1 << tiles) - (1 << (tiles - tiles // 4))
    for wanted in ((1 << tiles) - 1 - late, late):
        parts = [block if (wanted >> r) & 1 else tok for r, block in enumerate(recv, 1)]
        out = cross_and_project(
            wanted, me, tile_table, panel_table, valid, tok, parts, q, (mix_up, mix_down), gain_row, w_qkv, w_proj, out
        )
    return out.reshape(tokens.shape)


def solution(mesh):
    in_specs = (
        P(("scene", "tile"), None, None, None),
        P(),
        P(),
        P(),
        P(),
        P(("scene", "tile"), None),
        P("scene", None, None, None),
        P("scene", None, None),
    )
    out_specs = P(("scene", "tile"), None, None, None)
    return jax.shard_map(per_device, mesh=mesh, in_specs=in_specs, out_specs=out_specs, check_vma=False)
```

```python
import functools

import jax
import jax.numpy as jnp
from jax import lax
from jax.experimental import pallas as pl
from jax.experimental.pallas import tpu as pltpu
from jax.sharding import PartitionSpec as P

HEADS = 16
NORM_EPS = 1e-05
LOG2E = 1.4426950408889634
VMEM_LIMIT = 56 * 1024 * 1024
GROUP = 4


def layer_norm(rows, gain_row):
    values = rows.astype(jnp.float32)
    centred = values - jnp.mean(values, axis=-1, keepdims=True)
    spread = jnp.mean(centred * centred, axis=-1, keepdims=True)
    return (centred * lax.rsqrt(spread + NORM_EPS) * gain_row.astype(jnp.float32)).astype(jnp.bfloat16)


def dot_f32(left, right):
    return jnp.dot(left, right, preferred_element_type=jnp.float32)


def dot_t(left, right):
    return lax.dot_general(left, right, (((1,), (1,)), ((), ())), preferred_element_type=jnp.float32)


def staged(count, first, second):
    held = first(0)
    for g in range(count):
        coming = first(g + 1) if g + 1 < count else None
        second(g, held)
        held = coming


def low_lanes(rows, width, head_width):
    return lax.broadcasted_iota(jnp.int32, (rows, width), 1) < head_width


def pack_kernel(tiles, panels, cap, me_ref, tile_ref, panel_ref, tok_ref, *rest):
    outs, slab, sem, sems = rest[: tiles - 1], rest[tiles - 1], rest[tiles], rest[tiles + 1]
    me = me_ref[0]
    load = pltpu.make_async_copy(tok_ref, slab, sem)
    load.start()
    load.wait()
    counts = []
    for r in range(1, tiles):
        asker = me ^ r
        out = outs[r - 1]

        def body(p, count, asker=asker, out=out, r=r):
            hit = jnp.logical_and(tile_ref[asker * panels + p] == me, count < cap)

            @pl.when(hit)
            def _():
                j = panel_ref[asker * panels + p]
                pltpu.make_async_copy(
                    slab.at[j // (panels // 2), :, j % (panels // 2)], out.at[count], sems.at[r, count]
                ).start()

            return count + hit.astype(jnp.int32)

        counts.append(lax.fori_loop(0, panels, body, jnp.int32(0)))
    for r in range(1, tiles):
        for c in range(cap):

            @pl.when(c < counts[r - 1])
            def _(r=r, c=c):
                pltpu.make_async_copy(slab.at[0, :, 0], outs[r - 1].at[c], sems.at[r, c]).wait()


def pack(me, tile_table, panel_table, tok, tiles, cap):
    panels = 2 * tok.shape[2]
    block = (cap, tok.shape[1], tok.shape[3], tok.shape[4])
    smem = pl.BlockSpec(memory_space=pltpu.SMEM)
    anym = pl.BlockSpec(memory_space=pl.ANY)
    return pl.pallas_call(
        functools.partial(pack_kernel, tiles, panels, cap),
        out_shape=[jax.ShapeDtypeStruct(block, tok.dtype)] * (tiles - 1),
        in_specs=[smem, smem, smem, anym],
        out_specs=[anym] * (tiles - 1),
        scratch_shapes=[
            pltpu.VMEM(tok.shape, tok.dtype),
            pltpu.SemaphoreType.DMA,
            pltpu.SemaphoreType.DMA((tiles, cap)),
        ],
        cost_estimate=pl.CostEstimate(flops=0, bytes_accessed=16 << 20, transcendentals=0),
    )(me, tile_table, panel_table, tok)


def copy_through(pairs, bounce, sems):
    loads = [pltpu.make_async_copy(src, bounce.at[k], sems.at[0, k]) for k, (src, _) in enumerate(pairs)]
    for load in loads:
        load.start()
    stores = []
    for k, (_, dst) in enumerate(pairs):
        loads[k].wait()
        store = pltpu.make_async_copy(bounce.at[k], dst, sems.at[1, k])
        store.start()
        stores.append(store)
    for store in stores:
        store.wait()


def halves_kernel(tok_ref, first_ref, second_ref, bounce, sems):
    deep = first_ref.shape[1]
    pairs = []
    for u in range(2):
        pairs.append((tok_ref.at[u, :deep], first_ref.at[u]))
        pairs.append((tok_ref.at[u, deep:], second_ref.at[u]))
    copy_through(pairs, bounce, sems)


def split_halves(tok):
    halves, deep, wide, run, feat = tok.shape
    part = (halves, deep // 2, wide, run, feat)
    anym = pl.BlockSpec(memory_space=pl.ANY)
    return pl.pallas_call(
        halves_kernel,
        out_shape=[jax.ShapeDtypeStruct(part, tok.dtype)] * 2,
        in_specs=[anym],
        out_specs=[anym] * 2,
        scratch_shapes=[pltpu.VMEM((4,) + part[1:], tok.dtype), pltpu.SemaphoreType.DMA((2, 4))],
        cost_estimate=pl.CostEstimate(flops=0, bytes_accessed=16 << 20, transcendentals=0),
    )(tok)


def near_kernel(cap, me_ref, tile_ref, panel_ref, tok_ref, out_ref, bounce, sems, slots, slot_sems):
    halves, deep, wide, run, feat = tok_ref.shape
    panels = halves * wide
    me = me_ref[0]
    asker = me ^ 1
    part = 1 - (me & 1)

    def body(p, count):
        hit = jnp.logical_and(tile_ref[asker * panels + p] == me, count < cap)

        @pl.when(hit)
        def _():
            j = panel_ref[asker * panels + p]
            pltpu.make_async_copy(tok_ref.at[j // wide, :, j % wide], slots.at[count], slot_sems.at[0, count]).start()

        return count + hit.astype(jnp.int32)

    total = lax.fori_loop(0, panels, body, jnp.int32(0))
    copy_through([(tok_ref.at[part, 2 * k : 2 * k + 2], out_ref.at[2 * k : 2 * k + 2]) for k in range(deep // 2)], bounce, sems)
    for c in range(cap):

        @pl.when(c < total)
        def _(c=c):
            pltpu.make_async_copy(tok_ref.at[0, :, 0], slots.at[c], slot_sems.at[0, c]).wait()
            pltpu.make_async_copy(slots.at[c], out_ref.at[deep + c], slot_sems.at[1, c]).start()

    for c in range(cap):

        @pl.when(c < total)
        def _(c=c):
            pltpu.make_async_copy(slots.at[c], out_ref.at[deep + c], slot_sems.at[1, c]).wait()


def pack_near(me, tile_table, panel_table, tok, cap):
    halves, deep, wide, run, feat = tok.shape
    smem = pl.BlockSpec(memory_space=pltpu.SMEM)
    anym = pl.BlockSpec(memory_space=pl.ANY)
    return pl.pallas_call(
        functools.partial(near_kernel, cap),
        out_shape=jax.ShapeDtypeStruct((deep + cap, wide, run, feat), tok.dtype),
        in_specs=[smem, smem, smem, anym],
        out_specs=anym,
        scratch_shapes=[
            pltpu.VMEM((deep // 2, 2, wide, run, feat), tok.dtype),
            pltpu.SemaphoreType.DMA((2, deep // 2)),
            pltpu.VMEM((cap, deep, run, feat), tok.dtype),
            pltpu.SemaphoreType.DMA((2, cap)),
        ],
        cost_estimate=pl.CostEstimate(flops=0, bytes_accessed=6 << 20, transcendentals=0),
    )(me, tile_table, panel_table, tok)


def rim_kernel(me_ref, tok_ref, first_ref, second_ref, out_a, out_b, bounce, sems):
    deep = out_a.shape[0]
    me = me_ref[0]
    part = me & 1
    held = jnp.logical_or(me % 4 == 1, me % 4 == 2)
    bite = deep // 2
    spots = [pl.ds(k * bite, bite) for k in range(2)]
    for k in range(2):
        pltpu.make_async_copy(first_ref.at[part, spots[k]], bounce.at[k], sems.at[0, k]).start()

        @pl.when(held)
        def _(k=k):
            pltpu.make_async_copy(
                tok_ref.at[part, pl.ds(deep + k * bite, bite)], bounce.at[2 + k], sems.at[0, 2 + k]
            ).start()

        @pl.when(jnp.logical_not(held))
        def _(k=k):
            pltpu.make_async_copy(second_ref.at[part, spots[k]], bounce.at[2 + k], sems.at[0, 2 + k]).start()

    stores = []
    for k in range(4):
        pltpu.make_async_copy(first_ref.at[0, spots[0]], bounce.at[k], sems.at[0, k]).wait()
        store = pltpu.make_async_copy(bounce.at[k], (out_a if k < 2 else out_b).at[spots[k % 2]], sems.at[1, k])
        store.start()
        stores.append(store)
    for store in stores:
        store.wait()


def pack_rim(me, tok, first, second):
    halves, deep, wide, run, feat = first.shape
    anym = pl.BlockSpec(memory_space=pl.ANY)
    return pl.pallas_call(
        rim_kernel,
        out_shape=[jax.ShapeDtypeStruct(first.shape[1:], tok.dtype)] * 2,
        in_specs=[pl.BlockSpec(memory_space=pltpu.SMEM), anym, anym, anym],
        out_specs=[anym] * 2,
        scratch_shapes=[pltpu.VMEM((4, deep // 2, wide, run, feat), tok.dtype), pltpu.SemaphoreType.DMA((2, 4))],
        cost_estimate=pl.CostEstimate(flops=0, bytes_accessed=4 << 20, transcendentals=0),
    )(me, tok, first, second)


def far_kernel(cap, me_ref, tile_ref, panel_ref, tok_ref, first_ref, second_ref, *rest):
    outs, slab, got_a, got_b, sem, sems = rest[:5], *rest[5:]
    halves, deep, wide, run, feat = tok_ref.shape
    panels = halves * wide
    cut = deep // 2
    me = me_ref[0]
    loads = [
        pltpu.make_async_copy(src, dst, sem.at[k])
        for k, (src, dst) in enumerate(((tok_ref, slab), (first_ref, got_a), (second_ref, got_b)))
    ]
    for load in loads:
        load.start()
    for load in loads:
        load.wait()
    totals = []
    for k, (bits, relay) in enumerate(((2, 4), (3, 4), (4, 2), (5, 2))):
        asker = me ^ bits
        buffer, rows = (got_b, slice(cut, deep)) if relay == 4 else (got_a, slice(0, cut))

        def body(p, count, k=k, asker=asker, relay=relay, buffer=buffer, rows=rows):
            named = tile_ref[asker * panels + p]
            own = named == me
            hit = jnp.logical_and(jnp.logical_or(own, named == me ^ relay), count < 2 * cap)
            j = panel_ref[asker * panels + p]

            @pl.when(jnp.logical_and(hit, own))
            def _():
                pltpu.make_async_copy(slab.at[j // wide, rows, j % wide], outs[k].at[count], sems.at[k, count]).start()

            @pl.when(jnp.logical_and(hit, jnp.logical_not(own)))
            def _():
                pltpu.make_async_copy(buffer.at[j // wide, :, j % wide], outs[k].at[count], sems.at[k, count]).start()

            return count + hit.astype(jnp.int32)

        totals.append(lax.fori_loop(0, panels, body, jnp.int32(0)))

    asker = me ^ 1

    def near(p, counts):
        named = tile_ref[asker * panels + p]
        j = panel_ref[asker * panels + p]
        fresh = []
        for k, (relay, buffer) in enumerate(((2, got_a), (4, got_b))):
            hit = jnp.logical_and(named == me ^ relay, counts[k] < cap)

            @pl.when(hit)
            def _(k=k, buffer=buffer):
                spot = k * cap + counts[k]
                pltpu.make_async_copy(buffer.at[j // wide, :, j % wide], outs[4].at[spot], sems.at[4, spot]).start()

            fresh.append(counts[k] + hit.astype(jnp.int32))
        return tuple(fresh)

    near_totals = lax.fori_loop(0, panels, near, (jnp.int32(0), jnp.int32(0)))
    for k in range(5):
        for c in range(2 * cap):
            used = c < totals[k] if k < 4 else c % cap < near_totals[c // cap]

            @pl.when(used)
            def _(k=k, c=c):
                pltpu.make_async_copy(got_a.at[0, :, 0], outs[k].at[c], sems.at[k, c]).wait()


def pack_far(me, tile_table, panel_table, tok, first, second, cap):
    halves, deep, wide, run, feat = tok.shape
    smem = pl.BlockSpec(memory_space=pltpu.SMEM)
    anym = pl.BlockSpec(memory_space=pl.ANY)
    block = (2 * cap, deep // 2, run, feat)
    return pl.pallas_call(
        functools.partial(far_kernel, cap),
        out_shape=[jax.ShapeDtypeStruct(block, tok.dtype)] * 5,
        in_specs=[smem, smem, smem, anym, anym, anym],
        out_specs=[anym] * 5,
        scratch_shapes=[
            pltpu.VMEM(tok.shape, tok.dtype),
            pltpu.VMEM(first.shape, tok.dtype),
            pltpu.VMEM(second.shape, tok.dtype),
            pltpu.SemaphoreType.DMA((3,)),
            pltpu.SemaphoreType.DMA((5, 2 * cap)),
        ],
        compiler_params=pltpu.CompilerParams(vmem_limit_bytes=VMEM_LIMIT),
        cost_estimate=pl.CostEstimate(flops=0, bytes_accessed=14 << 20, transcendentals=0),
    )(me, tile_table, panel_table, tok, first, second)


def qkv_kernel(tok_ref, gain_ref, w_ref, q_ref, kv_ref):
    dims = tok_ref.shape
    feat = dims[-1]
    rows = dims[1] * dims[2] * dims[3]
    normed = layer_norm(tok_ref[...].reshape(rows, feat), gain_ref[...])
    q_ref[...] = dot_f32(normed, w_ref[:, :feat]).astype(jnp.bfloat16).reshape(q_ref.shape)
    kv_ref[...] = dot_f32(normed, w_ref[:, feat:]).astype(jnp.bfloat16).reshape(kv_ref.shape)


def project_own(tok, gain_row, w_qkv):
    halves, deep, wide, run, feat = tok.shape
    step = deep // 2
    spec = lambda width: pl.BlockSpec((1, step, wide, run, width), lambda i: (i // 2, i % 2, 0, 0, 0))
    tokens = halves * deep * wide * run
    return pl.pallas_call(
        qkv_kernel,
        grid=(halves * 2,),
        out_shape=[
            jax.ShapeDtypeStruct((halves, deep, wide, run, feat), jnp.bfloat16),
            jax.ShapeDtypeStruct((halves, deep, wide, run, 2 * feat), jnp.bfloat16),
        ],
        in_specs=[
            spec(feat),
            pl.BlockSpec((1, feat), lambda i: (0, 0)),
            pl.BlockSpec((feat, 3 * feat), lambda i: (0, 0), pipeline_mode=pl.Buffered(1)),
        ],
        out_specs=[spec(feat), spec(2 * feat)],
        compiler_params=pltpu.CompilerParams(vmem_limit_bytes=VMEM_LIMIT),
        cost_estimate=pl.CostEstimate(
            flops=2 * tokens * feat * 3 * feat, bytes_accessed=tokens * feat * 8 + feat * feat * 6, transcendentals=0
        ),
    )(tok, gain_row, w_qkv)


def window_kernel(head_width, half_ref, top_ref, low_ref, q_ref, kvo_ref, gain_ref, w_ref, mix_ref, kv_s):
    deep, group, run, feat = mix_ref.shape
    length = deep * run
    rows = jnp.concatenate([top_ref[...], low_ref[...]], axis=0).reshape(deep * group * run, feat)
    normed = layer_norm(rows, gain_ref[...])
    kv_s[...] = dot_f32(normed, w_ref[:, feat:]).astype(jnp.bfloat16).reshape(kv_s.shape)
    pair = 2 * head_width
    scale = LOG2E * head_width ** (-0.5)
    bias = jnp.where(
        jnp.logical_and(half_ref[1] == 0, lax.broadcasted_iota(jnp.int32, (1, 2 * length), 1) < length), -jnp.inf, 0.0
    )
    low = low_lanes(length, pair, head_width)
    ones = jnp.ones((2 * length, pair), jnp.bfloat16)
    zero = jnp.zeros((length, pair), jnp.bfloat16)
    def panel(i, carry):
        def score(g):
            at = slice(g * pair, (g + 1) * pair)
            q = q_ref[0, :, i, :, at].reshape(length, pair)
            qs = jnp.concatenate([jnp.where(low, q, zero), jnp.where(low, zero, q)], axis=0)
            keys = jnp.concatenate(
                [kv_s[:, i, :, at].reshape(length, pair), kvo_ref[0, :, i, :, at].reshape(length, pair)], axis=0
            )
            return dot_t(qs, keys) + bias

        def mix(g, scores):
            at_v = slice(feat + g * pair, feat + (g + 1) * pair)
            vals = jnp.concatenate(
                [kv_s[:, i, :, at_v].reshape(length, pair), kvo_ref[0, :, i, :, at_v].reshape(length, pair)], axis=0
            )
            peak = jnp.max(scores, axis=1, keepdims=True)
            weights = jnp.exp2((scores - peak) * scale).astype(jnp.bfloat16)
            both = dot_f32(weights, jnp.concatenate([vals, ones], axis=1))
            mixed = both[:, :pair] / both[:, pair:]
            out = jnp.where(low, mixed[:length], mixed[length:])
            mix_ref[:, i, :, g * pair : (g + 1) * pair] = out.astype(jnp.bfloat16).reshape(deep, run, pair)

        staged(feat // pair, score, mix)
        return carry

    lax.fori_loop(0, group, panel, 0)


def window_mix(half_keep, edges, spots, q, kv_own, gain_row, w_qkv):
    _, deep, wide, run, feat = q.shape
    group = min(GROUP, wide)
    head_width = feat // HEADS
    own = lambda width: pl.BlockSpec((1, deep, group, run, width), lambda i, hk: (hk[0], 0, i, 0, 0))
    side = lambda spot: pl.BlockSpec((deep // 2, group, run, feat), lambda i, hk: (spot, i, 0, 0))
    flat = pl.BlockSpec((deep, group, run, feat), lambda i, hk: (0, i, 0, 0))
    tokens = deep * wide * run
    return pl.pallas_call(
        functools.partial(window_kernel, head_width),
        out_shape=jax.ShapeDtypeStruct((deep, wide, run, feat), jnp.bfloat16),
        grid_spec=pltpu.PrefetchScalarGridSpec(
            num_scalar_prefetch=1,
            grid=(wide // group,),
            in_specs=[
                side(spots[0]),
                side(spots[1]),
                own(feat),
                own(2 * feat),
                pl.BlockSpec((1, feat), lambda i, hk: (0, 0)),
                pl.BlockSpec((feat, 3 * feat), lambda i, hk: (0, 0), pipeline_mode=pl.Buffered(1)),
            ],
            out_specs=flat,
            scratch_shapes=[pltpu.VMEM((deep, group, run, 2 * feat), jnp.bfloat16)],
        ),
        compiler_params=pltpu.CompilerParams(vmem_limit_bytes=VMEM_LIMIT),
        cost_estimate=pl.CostEstimate(
            flops=2 * tokens * feat * 2 * feat + 8 * tokens * 256 * feat,
            bytes_accessed=tokens * feat * 10 + feat * feat * 6,
            transcendentals=tokens * 256 * HEADS,
        ),
    )(half_keep, edges[0], edges[1], q, kv_own, gain_row, w_qkv)


def direct_parts(recv, tok_ref, tiles, wanted, cap):
    cut = tok_ref.shape[1] // 2
    wide = tok_ref.shape[2]

    def own(j, seen):
        return tok_ref.at[j // wide, :cut, j % wide], tok_ref.at[j // wide, cut:, j % wide]

    def other(r):
        return lambda j, seen: (recv[r - 1].at[seen[r], :cut], recv[r - 1].at[seen[r], cut:])

    return {r: own if r == 0 else other(r) for r in range(tiles) if (wanted >> r) & 1}


def relay_parts(recv, tok_ref, tiles, wanted, cap):
    near, first, second, x_same, x_cross, y_same, y_cross, rest = recv
    cut = tok_ref.shape[1] // 2
    wide = tok_ref.shape[2]
    deep = tok_ref.shape[1]
    at = lambda ref, j: ref.at[j // wide, :, j % wide]
    table = {
        0: lambda j, seen: (tok_ref.at[j // wide, :cut, j % wide], tok_ref.at[j // wide, cut:, j % wide]),
        1: lambda j, seen: (near.at[deep + seen[1], :cut], near.at[deep + seen[1], cut:]),
        2: lambda j, seen: (at(first, j), x_same.at[seen[2] + seen[6]]),
        3: lambda j, seen: (rest.at[seen[3]], x_cross.at[seen[3] + seen[7]]),
        4: lambda j, seen: (y_same.at[seen[4] + seen[6]], at(second, j)),
        5: lambda j, seen: (y_cross.at[seen[5] + seen[7]], rest.at[cap + seen[5]]),
        6: lambda j, seen: (y_same.at[seen[4] + seen[6]], x_same.at[seen[2] + seen[6]]),
        7: lambda j, seen: (y_cross.at[seen[5] + seen[7]], x_cross.at[seen[3] + seen[7]]),
    }
    return {r: table[r] for r in range(tiles) if (wanted >> r) & 1}


def cross_kernel(plan, tiles, head_width, wanted, recv_count, cap, refs):
    me_ref, tile_ref, panel_ref, valid_ref, half_ref, tok_ref = refs[:6]
    recv = refs[6 : 6 + recv_count]
    q_ref, mix_a, mix_b, gain_ref, wqkv_ref, wproj_ref = refs[6 + recv_count : 12 + recv_count]
    out_ref, got, q_s, own_s, res_s, wkv_s, wp_s, kv_s, mixed_s, seen, ids, w_sem, sems = refs[-13:]
    panels, deep, run, feat = got.shape
    half = panels // 2
    cut = deep // 2
    length = deep * run
    me = me_ref[0]
    parts = plan(recv, tok_ref, tiles, wanted, cap)
    for t in range(tiles):
        seen[t] = 0

    def fetch(p, count):
        r = tile_ref[me * panels + p] ^ me
        hit = ((wanted >> r) & 1) == 1

        @pl.when(hit)
        def _():
            ids[count] = p
            j = panel_ref[me * panels + p]
            for k, pick in parts.items():

                @pl.when(r == k)
                def _(pick=pick):
                    top, bottom = pick(j, seen)
                    pltpu.make_async_copy(top, got.at[count, :cut], sems.at[0, count]).start()
                    pltpu.make_async_copy(bottom, got.at[count, cut:], sems.at[4, count]).start()

            u = p // half
            w = p % half
            pltpu.make_async_copy(q_ref.at[u, :, w], q_s.at[count], sems.at[1, count]).start()

            @pl.when(u == half_ref[0])
            def _():
                pltpu.make_async_copy(mix_a.at[:, w], own_s.at[count], sems.at[2, count]).start()

            @pl.when(u != half_ref[0])
            def _():
                pltpu.make_async_copy(mix_b.at[:, w], own_s.at[count], sems.at[2, count]).start()

        seen[r] = seen[r] + 1
        return count + hit.astype(jnp.int32)

    load_wkv = pltpu.make_async_copy(wqkv_ref.at[:, feat:], wkv_s, w_sem.at[0])
    load_wp = pltpu.make_async_copy(wproj_ref, wp_s, w_sem.at[1])
    load_wkv.start()
    total = lax.fori_loop(0, panels, fetch, jnp.int32(0))
    load_wp.start()
    load_wkv.wait()
    load_wp.wait()

    pair = 2 * head_width
    scale = LOG2E * head_width ** (-0.5)
    low = low_lanes(length, pair, head_width)
    zero = jnp.zeros((length, pair), jnp.bfloat16)
    one = jnp.ones((length, pair), jnp.bfloat16)
    marks = jnp.concatenate([jnp.where(low, one, zero), jnp.where(low, zero, one)], axis=0)
    pairs = feat // pair

    def unit(n, carry):
        first = 2 * n
        for i in range(2):

            @pl.when(first + i < total)
            def _(i=i):
                n_i = first + i
                for k, place in ((0, got.at[n_i, :cut]), (4, got.at[n_i, cut:])):
                    pltpu.make_async_copy(tok_ref.at[0, :cut, 0], place, sems.at[k, n_i]).wait()
                for k, place in ((1, q_s.at[n_i]), (2, own_s.at[n_i])):
                    pltpu.make_async_copy(tok_ref.at[0, :, 0], place, sems.at[k, n_i]).wait()

        rows = got[pl.ds(first, 2)].reshape(2 * length, feat)
        normed = layer_norm(rows, gain_ref[...])
        kv_s[...] = dot_f32(normed, wkv_s[...]).astype(jnp.bfloat16)
        gates = [valid_ref[ids[jnp.minimum(first + i, total - 1)]].astype(jnp.float32) for i in range(2)]

        def score(t):
            i, g = t // pairs, t % pairs
            at = slice(g * pair, (g + 1) * pair)
            q = q_s[first + i, :, :, at].reshape(length, pair)
            key = kv_s[i * length : (i + 1) * length, at]
            keys = jnp.concatenate([jnp.where(low, key, zero), jnp.where(low, zero, key)], axis=0)
            return dot_t(q, keys)

        def mix(t, scores):
            i, g = t // pairs, t % pairs
            at = slice(g * pair, (g + 1) * pair)
            val = kv_s[i * length : (i + 1) * length, feat + g * pair : feat + (g + 1) * pair]
            vals = jnp.concatenate([jnp.where(low, val, zero), jnp.where(low, zero, val)], axis=0)
            parts = []
            for h in range(2):
                part = scores[:, h * length : (h + 1) * length]
                peak = jnp.max(part, axis=1, keepdims=True)
                parts.append(jnp.exp2((part - peak) * scale).astype(jnp.bfloat16))
            both = dot_f32(jnp.concatenate(parts, axis=1), jnp.concatenate([vals, marks], axis=1))
            cross = (both[:, :pair] / both[:, pair:]).astype(jnp.bfloat16)
            own = own_s[first + i, :, :, at].reshape(length, pair)
            blended = gates[i] * own.astype(jnp.float32) + cross.astype(jnp.float32)
            mixed_s[i * length : (i + 1) * length, at] = blended.astype(jnp.bfloat16)

        staged(2 * pairs, score, mix)
        res_s[pl.ds(first, 2)] = dot_f32(mixed_s[...], wp_s[...]).astype(jnp.bfloat16).reshape(2, deep, run, feat)
        for i in range(2):

            @pl.when(first + i < total)
            def _(i=i):
                p = ids[first + i]
                pltpu.make_async_copy(
                    res_s.at[first + i], out_ref.at[p // half, :, p % half], sems.at[3, first + i]
                ).start()

        return carry

    lax.fori_loop(0, (total + 1) // 2, unit, 0)

    def finish(n, carry):
        pltpu.make_async_copy(res_s.at[n], out_ref.at[0, :, 0], sems.at[3, n]).wait()
        return carry

    lax.fori_loop(0, total, finish, 0)


def cross_and_project(
    plan, wanted, tiles, cap, me, tile_table, panel_table, valid, half_keep, tok, recv, q, mixes, gain_row, w_qkv, w_proj, earlier
):
    halves, deep, wide, run, feat = tok.shape
    panels = halves * wide
    head_width = feat // HEADS
    length = deep * run
    smem = pl.BlockSpec(memory_space=pltpu.SMEM)
    anym = pl.BlockSpec(memory_space=pl.ANY)
    share = bin(wanted).count("1") / tiles
    tokens = int(panels * length * share)
    many = pltpu.VMEM((panels, deep, run, feat), jnp.bfloat16)
    operands = [me, tile_table, panel_table, valid, half_keep, tok, *recv, q, *mixes, gain_row, w_qkv, w_proj]
    specs = [smem] * 5 + [anym] * (len(recv) + 4) + [pl.BlockSpec((1, feat), lambda: (0, 0))] + [anym] * 2
    aliases = {}
    if earlier is not None:
        aliases = {len(operands): 0}
        operands.append(earlier)
        specs.append(anym)

    def kernel(*refs):
        cross_kernel(plan, tiles, head_width, wanted, len(recv), cap, refs)

    return pl.pallas_call(
        kernel,
        out_shape=jax.ShapeDtypeStruct(tok.shape, jnp.bfloat16),
        in_specs=specs,
        out_specs=anym,
        scratch_shapes=[
            many,
            many,
            many,
            many,
            pltpu.VMEM((feat, 2 * feat), jnp.bfloat16),
            pltpu.VMEM((feat, feat), jnp.bfloat16),
            pltpu.VMEM((2 * length, 2 * feat), jnp.bfloat16),
            pltpu.VMEM((2 * length, feat), jnp.bfloat16),
            pltpu.SMEM((tiles,), jnp.int32),
            pltpu.SMEM((panels,), jnp.int32),
            pltpu.SemaphoreType.DMA((2,)),
            pltpu.SemaphoreType.DMA((5, panels)),
        ],
        input_output_aliases=aliases,
        compiler_params=pltpu.CompilerParams(vmem_limit_bytes=VMEM_LIMIT),
        cost_estimate=pl.CostEstimate(
            flops=2 * tokens * feat * 3 * feat + 8 * tokens * 128 * feat,
            bytes_accessed=tokens * feat * 8 + feat * feat * 6,
            transcendentals=tokens * 128 * HEADS,
        ),
    )(*operands)


def per_device(tokens, gain, w_qkv, w_proj, scene_first, window_valid, partner_tile, partner_panel):
    _, tok_rows, tok_cols, feat = tokens.shape
    run = 16
    wide = tok_cols // run
    tok = tokens.reshape(2, tok_rows // 2, wide, run, feat)
    tiles = partner_tile.shape[1]
    panels = partner_tile.shape[2]
    cap = 2 * max(1, panels // tiles)
    slab_count = scene_first.shape[0]
    me = lax.axis_index("tile").reshape(1).astype(jnp.int32)
    tile_table = partner_tile.reshape(tiles * panels)
    panel_table = partner_panel.reshape(tiles * panels)
    valid = window_valid.reshape(panels)
    gain_row = gain.reshape(1, feat)
    slab_index = lax.axis_index(("scene", "tile"))
    after_index = jnp.minimum(slab_index + 1, slab_count - 1)
    own_first = jnp.logical_or(scene_first[slab_index] == 1, slab_index == 0)
    next_first = jnp.logical_or(scene_first[after_index] == 1, slab_index + 1 >= slab_count)
    keep_before = jnp.logical_not(own_first).astype(jnp.int32)
    keep_after = jnp.logical_not(next_first).astype(jnp.int32)

    def xor(block, bits):
        return lax.ppermute(block, "tile", [(i, i ^ bits) for i in range(tiles)])

    def cross(plan, wanted, recv, mixes, half_keep, earlier):
        return cross_and_project(
            plan,
            wanted,
            tiles,
            cap,
            me,
            tile_table,
            panel_table,
            valid,
            half_keep,
            tok,
            recv,
            q,
            mixes,
            gain_row,
            w_qkv,
            w_proj,
            earlier,
        )

    if tiles == 8:
        first, second = split_halves(tok)
        first = xor(first, 2)
        second = xor(second, 4)
        near = xor(pack_near(me, tile_table, panel_table, tok, cap), 1)
        q, kv = project_own(tok, gain_row, w_qkv)
        odd = slab_index % 2
        near_half = jnp.stack([1 - odd, jnp.where(odd == 1, keep_before, keep_after)]).astype(jnp.int32)
        far_half = jnp.stack([odd, jnp.where(odd == 1, keep_after, keep_before)]).astype(jnp.int32)
        mix_near = window_mix(near_half, (near, near), (0, 1), q, kv, gain_row, w_qkv)
        rim_a, rim_b = pack_rim(me, tok, first, second)
        links_a, links_b = [], []
        for low in range(1, slab_count - 1, 2):
            held = (low, low + 1) if low % 4 == 1 else (low ^ 4, (low + 1) ^ 4)
            links_a += [(low ^ 2, low + 1), ((low + 1) ^ 2, low)]
            links_b += [(held[0], low + 1), (held[1], low)]
        rim_a = lax.ppermute(rim_a, ("scene", "tile"), links_a)
        rim_b = lax.ppermute(rim_b, ("scene", "tile"), links_b)
        x_same, x_cross, y_same, y_cross, rest = pack_far(me, tile_table, panel_table, tok, first, second, cap)
        rim_a, rim_b, x_same, y_same, rest = lax.optimization_barrier((rim_a, rim_b, x_same, y_same, rest))
        x_same, y_same, rest = xor(x_same, 2), xor(y_same, 4), xor(rest, 1)
        mix_far = window_mix(far_half, (rim_a, rim_b), (0, 0), q, kv, gain_row, w_qkv)
        x_same, y_same, x_cross, y_cross = lax.optimization_barrier((x_same, y_same, x_cross, y_cross))
        x_cross, y_cross = xor(x_cross, 3), xor(y_cross, 5)
        mixes = (mix_near, mix_far)
        idle = rest
        early = (near, first, second, x_same, idle, y_same, idle, idle)
        late = (near, first, second, x_same, x_cross, y_same, y_cross, rest)
        out = cross(relay_parts, 0b01010111, early, mixes, near_half, None)
        out = cross(relay_parts, 0b10101000, late, mixes, near_half, out)
    else:
        forward = [(i, i + 1) for i in range(slab_count - 1)]
        backward = [(i + 1, i) for i in range(slab_count - 1)]
        before = lax.ppermute(tok[1], ("scene", "tile"), forward)
        after = lax.ppermute(tok[0], ("scene", "tile"), backward)
        outgoing = pack(me, tile_table, panel_table, tok, tiles, cap)
        recv = [xor(outgoing[r - 1], r) for r in range(1, tiles)]
        q, kv = project_own(tok, gain_row, w_qkv)
        zero = jnp.zeros((), jnp.int32)
        upper = jnp.stack([zero, keep_before])
        mix_up = window_mix(upper, (before, before), (0, 1), q, kv, gain_row, w_qkv)
        mix_down = window_mix(jnp.stack([zero + 1, keep_after]), (after, after), (0, 1), q, kv, gain_row, w_qkv)
        out = cross(direct_parts, (1 << tiles) - 1, recv, (mix_up, mix_down), upper, None)
    return out.reshape(tokens.shape)


def solution(mesh):
    in_specs = (
        P(("scene", "tile"), None, None, None),
        P(),
        P(),
        P(),
        P(),
        P(("scene", "tile"), None),
        P("scene", None, None, None),
        P("scene", None, None),
    )
    out_specs = P(("scene", "tile"), None, None, None)
    return jax.shard_map(per_device, mesh=mesh, in_specs=in_specs, out_specs=out_specs, check_vma=False)
```

```python
import functools

import jax
import jax.numpy as jnp
from jax import lax
from jax.experimental import pallas as pl
from jax.experimental.pallas import tpu as pltpu
from jax.sharding import PartitionSpec as P

HEADS = 16
NORM_EPS = 1e-05
LOG2E = 1.4426950408889634
VMEM_LIMIT = 56 * 1024 * 1024
GROUP = 4


def layer_norm(rows, gain_row):
    values = rows.astype(jnp.float32)
    centred = values - jnp.mean(values, axis=-1, keepdims=True)
    spread = jnp.mean(centred * centred, axis=-1, keepdims=True)
    return (centred * lax.rsqrt(spread + NORM_EPS) * gain_row.astype(jnp.float32)).astype(jnp.bfloat16)


def dot_f32(left, right):
    return jnp.dot(left, right, preferred_element_type=jnp.float32)


def dot_t(left, right):
    return lax.dot_general(left, right, (((1,), (1,)), ((), ())), preferred_element_type=jnp.float32)


def staged(count, first, second):
    held = first(0)
    for g in range(count):
        coming = first(g + 1) if g + 1 < count else None
        second(g, held)
        held = coming


def low_lanes(rows, width, head_width):
    return lax.broadcasted_iota(jnp.int32, (rows, width), 1) < head_width


def pack_kernel(tiles, panels, cap, me_ref, tile_ref, panel_ref, tok_ref, *rest):
    outs, slab, sem, sems = rest[: tiles - 1], rest[tiles - 1], rest[tiles], rest[tiles + 1]
    me = me_ref[0]
    load = pltpu.make_async_copy(tok_ref, slab, sem)
    load.start()
    load.wait()
    counts = []
    for r in range(1, tiles):
        asker = me ^ r
        out = outs[r - 1]

        def body(p, count, asker=asker, out=out, r=r):
            hit = jnp.logical_and(tile_ref[asker * panels + p] == me, count < cap)

            @pl.when(hit)
            def _():
                j = panel_ref[asker * panels + p]
                pltpu.make_async_copy(
                    slab.at[j // (panels // 2), :, j % (panels // 2)], out.at[count], sems.at[r, count]
                ).start()

            return count + hit.astype(jnp.int32)

        counts.append(lax.fori_loop(0, panels, body, jnp.int32(0)))
    for r in range(1, tiles):
        for c in range(cap):

            @pl.when(c < counts[r - 1])
            def _(r=r, c=c):
                pltpu.make_async_copy(slab.at[0, :, 0], outs[r - 1].at[c], sems.at[r, c]).wait()


def pack(me, tile_table, panel_table, tok, tiles, cap):
    panels = 2 * tok.shape[2]
    block = (cap, tok.shape[1], tok.shape[3], tok.shape[4])
    smem = pl.BlockSpec(memory_space=pltpu.SMEM)
    anym = pl.BlockSpec(memory_space=pl.ANY)
    return pl.pallas_call(
        functools.partial(pack_kernel, tiles, panels, cap),
        out_shape=[jax.ShapeDtypeStruct(block, tok.dtype)] * (tiles - 1),
        in_specs=[smem, smem, smem, anym],
        out_specs=[anym] * (tiles - 1),
        scratch_shapes=[
            pltpu.VMEM(tok.shape, tok.dtype),
            pltpu.SemaphoreType.DMA,
            pltpu.SemaphoreType.DMA((tiles, cap)),
        ],
        cost_estimate=pl.CostEstimate(flops=0, bytes_accessed=16 << 20, transcendentals=0),
    )(me, tile_table, panel_table, tok)


def copy_through(pairs, bounce, sems):
    loads = [pltpu.make_async_copy(src, bounce.at[k], sems.at[0, k]) for k, (src, _) in enumerate(pairs)]
    for load in loads:
        load.start()
    stores = []
    for k, (_, dst) in enumerate(pairs):
        loads[k].wait()
        store = pltpu.make_async_copy(bounce.at[k], dst, sems.at[1, k])
        store.start()
        stores.append(store)
    for store in stores:
        store.wait()


def halves_kernel(me_ref, tok_ref, *rest):
    outs, bounce, sems = rest[:4], rest[4], rest[5]
    deep = outs[0].shape[0]
    part = me_ref[0] & 1
    sources = [
        tok_ref.at[part, :deep],
        tok_ref.at[part, deep:],
        tok_ref.at[1 - part, :deep],
        tok_ref.at[1 - part, deep:],
    ]
    copy_through(list(zip(sources, outs)), bounce, sems)


def split_halves(me, tok):
    halves, deep, wide, run, feat = tok.shape
    part = (deep // 2, wide, run, feat)
    anym = pl.BlockSpec(memory_space=pl.ANY)
    return pl.pallas_call(
        halves_kernel,
        out_shape=[jax.ShapeDtypeStruct(part, tok.dtype)] * 4,
        in_specs=[pl.BlockSpec(memory_space=pltpu.SMEM), anym],
        out_specs=[anym] * 4,
        scratch_shapes=[pltpu.VMEM((4,) + part, tok.dtype), pltpu.SemaphoreType.DMA((2, 4))],
        cost_estimate=pl.CostEstimate(flops=0, bytes_accessed=8 << 20, transcendentals=0),
    )(me, tok)


def near_kernel(cap, me_ref, tile_ref, panel_ref, tok_ref, out_ref, bounce, sems, slots, slot_sems):
    halves, deep, wide, run, feat = tok_ref.shape
    panels = halves * wide
    me = me_ref[0]
    asker = me ^ 1
    part = 1 - (me & 1)

    def body(p, count):
        hit = jnp.logical_and(tile_ref[asker * panels + p] == me, count < cap)

        @pl.when(hit)
        def _():
            j = panel_ref[asker * panels + p]
            pltpu.make_async_copy(tok_ref.at[j // wide, :, j % wide], slots.at[count], slot_sems.at[0, count]).start()

        return count + hit.astype(jnp.int32)

    total = lax.fori_loop(0, panels, body, jnp.int32(0))
    copy_through([(tok_ref.at[part, 2 * k : 2 * k + 2], out_ref.at[2 * k : 2 * k + 2]) for k in range(deep // 2)], bounce, sems)
    for c in range(cap):

        @pl.when(c < total)
        def _(c=c):
            pltpu.make_async_copy(tok_ref.at[0, :, 0], slots.at[c], slot_sems.at[0, c]).wait()
            pltpu.make_async_copy(slots.at[c], out_ref.at[deep + c], slot_sems.at[1, c]).start()

    for c in range(cap):

        @pl.when(c < total)
        def _(c=c):
            pltpu.make_async_copy(slots.at[c], out_ref.at[deep + c], slot_sems.at[1, c]).wait()


def pack_near(me, tile_table, panel_table, tok, cap):
    halves, deep, wide, run, feat = tok.shape
    smem = pl.BlockSpec(memory_space=pltpu.SMEM)
    anym = pl.BlockSpec(memory_space=pl.ANY)
    return pl.pallas_call(
        functools.partial(near_kernel, cap),
        out_shape=jax.ShapeDtypeStruct((deep + cap, wide, run, feat), tok.dtype),
        in_specs=[smem, smem, smem, anym],
        out_specs=anym,
        scratch_shapes=[
            pltpu.VMEM((deep // 2, 2, wide, run, feat), tok.dtype),
            pltpu.SemaphoreType.DMA((2, deep // 2)),
            pltpu.VMEM((cap, deep, run, feat), tok.dtype),
            pltpu.SemaphoreType.DMA((2, cap)),
        ],
        cost_estimate=pl.CostEstimate(flops=0, bytes_accessed=6 << 20, transcendentals=0),
    )(me, tile_table, panel_table, tok)


def far_kernel(cap, me_ref, tile_ref, panel_ref, tok_ref, *rest):
    sides, outs, slab, got, sem, sems = rest[:4], rest[4:9], *rest[9:]
    halves, deep, wide, run, feat = tok_ref.shape
    panels = halves * wide
    cut = deep // 2
    me = me_ref[0]
    part = me & 1
    loads = [pltpu.make_async_copy(tok_ref, slab, sem.at[4])]
    for k in range(4):
        u = part if k < 2 else 1 - part
        loads.append(pltpu.make_async_copy(sides[k], got.at[k % 2, u], sem.at[k]))
    for load in loads:
        load.start()
    for load in loads:
        load.wait()
    totals = []
    for k, (bits, relay) in enumerate(((2, 4), (3, 4), (4, 2), (5, 2))):
        asker = me ^ bits
        buffer, rows = (1, slice(cut, deep)) if relay == 4 else (0, slice(0, cut))

        def body(p, count, k=k, asker=asker, relay=relay, buffer=buffer, rows=rows):
            named = tile_ref[asker * panels + p]
            own = named == me
            hit = jnp.logical_and(jnp.logical_or(own, named == me ^ relay), count < 2 * cap)
            j = panel_ref[asker * panels + p]

            @pl.when(jnp.logical_and(hit, own))
            def _():
                pltpu.make_async_copy(slab.at[j // wide, rows, j % wide], outs[k].at[count], sems.at[k, count]).start()

            @pl.when(jnp.logical_and(hit, jnp.logical_not(own)))
            def _():
                pltpu.make_async_copy(
                    got.at[buffer, j // wide, :, j % wide], outs[k].at[count], sems.at[k, count]
                ).start()

            return count + hit.astype(jnp.int32)

        totals.append(lax.fori_loop(0, panels, body, jnp.int32(0)))

    asker = me ^ 1

    def near(p, counts):
        named = tile_ref[asker * panels + p]
        j = panel_ref[asker * panels + p]
        fresh = []
        for k, relay in enumerate((2, 4)):
            hit = jnp.logical_and(named == me ^ relay, counts[k] < cap)

            @pl.when(hit)
            def _(k=k):
                spot = k * cap + counts[k]
                pltpu.make_async_copy(got.at[k, j // wide, :, j % wide], outs[4].at[spot], sems.at[4, spot]).start()

            fresh.append(counts[k] + hit.astype(jnp.int32))
        return tuple(fresh)

    near_totals = lax.fori_loop(0, panels, near, (jnp.int32(0), jnp.int32(0)))
    for k in range(5):
        for c in range(2 * cap):
            used = c < totals[k] if k < 4 else c % cap < near_totals[c // cap]

            @pl.when(used)
            def _(k=k, c=c):
                pltpu.make_async_copy(got.at[0, 0, :, 0], outs[k].at[c], sems.at[k, c]).wait()


def pack_far(me, tile_table, panel_table, tok, sides, cap):
    halves, deep, wide, run, feat = tok.shape
    smem = pl.BlockSpec(memory_space=pltpu.SMEM)
    anym = pl.BlockSpec(memory_space=pl.ANY)
    block = (2 * cap, deep // 2, run, feat)
    return pl.pallas_call(
        functools.partial(far_kernel, cap),
        out_shape=[jax.ShapeDtypeStruct(block, tok.dtype)] * 5,
        in_specs=[smem, smem, smem] + [anym] * 5,
        out_specs=[anym] * 5,
        scratch_shapes=[
            pltpu.VMEM(tok.shape, tok.dtype),
            pltpu.VMEM((2, halves, deep // 2, wide, run, feat), tok.dtype),
            pltpu.SemaphoreType.DMA((5,)),
            pltpu.SemaphoreType.DMA((5, 2 * cap)),
        ],
        compiler_params=pltpu.CompilerParams(vmem_limit_bytes=VMEM_LIMIT),
        cost_estimate=pl.CostEstimate(flops=0, bytes_accessed=14 << 20, transcendentals=0),
    )(me, tile_table, panel_table, tok, *sides)


def qkv_kernel(tok_ref, gain_ref, w_ref, q_ref, kv_ref):
    dims = tok_ref.shape
    feat = dims[-1]
    rows = dims[1] * dims[2] * dims[3]
    normed = layer_norm(tok_ref[...].reshape(rows, feat), gain_ref[...])
    q_ref[...] = dot_f32(normed, w_ref[:, :feat]).astype(jnp.bfloat16).reshape(q_ref.shape)
    kv_ref[...] = dot_f32(normed, w_ref[:, feat:]).astype(jnp.bfloat16).reshape(kv_ref.shape)


def project_own(tok, gain_row, w_qkv):
    halves, deep, wide, run, feat = tok.shape
    step = deep // 2
    spec = lambda width: pl.BlockSpec((1, step, wide, run, width), lambda i: (i // 2, i % 2, 0, 0, 0))
    tokens = halves * deep * wide * run
    return pl.pallas_call(
        qkv_kernel,
        grid=(halves * 2,),
        out_shape=[
            jax.ShapeDtypeStruct((halves, deep, wide, run, feat), jnp.bfloat16),
            jax.ShapeDtypeStruct((halves, deep, wide, run, 2 * feat), jnp.bfloat16),
        ],
        in_specs=[
            spec(feat),
            pl.BlockSpec((1, feat), lambda i: (0, 0)),
            pl.BlockSpec((feat, 3 * feat), lambda i: (0, 0), pipeline_mode=pl.Buffered(1)),
        ],
        out_specs=[spec(feat), spec(2 * feat)],
        compiler_params=pltpu.CompilerParams(vmem_limit_bytes=VMEM_LIMIT),
        cost_estimate=pl.CostEstimate(
            flops=2 * tokens * feat * 3 * feat, bytes_accessed=tokens * feat * 8 + feat * feat * 6, transcendentals=0
        ),
    )(tok, gain_row, w_qkv)


def window_kernel(head_width, half_ref, *refs):
    edges, (q_ref, kvo_ref, gain_ref, w_ref, mix_ref, kv_s) = refs[:-6], refs[-6:]
    deep, group, run, feat = mix_ref.shape
    length = deep * run
    bottom = edges[1][...]
    if len(edges) == 3:
        bottom = jnp.where(half_ref[2] == 1, bottom, edges[2][...])
    rows = jnp.concatenate([edges[0][...], bottom], axis=0).reshape(deep * group * run, feat)
    normed = layer_norm(rows, gain_ref[...])
    kv_s[...] = dot_f32(normed, w_ref[:, feat:]).astype(jnp.bfloat16).reshape(kv_s.shape)
    pair = 2 * head_width
    scale = LOG2E * head_width ** (-0.5)
    bias = jnp.where(
        jnp.logical_and(half_ref[1] == 0, lax.broadcasted_iota(jnp.int32, (1, 2 * length), 1) < length), -jnp.inf, 0.0
    )
    low = low_lanes(length, pair, head_width)
    ones = jnp.ones((2 * length, pair), jnp.bfloat16)
    zero = jnp.zeros((length, pair), jnp.bfloat16)
    def panel(i, carry):
        def score(g):
            at = slice(g * pair, (g + 1) * pair)
            q = q_ref[0, :, i, :, at].reshape(length, pair)
            qs = jnp.concatenate([jnp.where(low, q, zero), jnp.where(low, zero, q)], axis=0)
            keys = jnp.concatenate(
                [kv_s[:, i, :, at].reshape(length, pair), kvo_ref[0, :, i, :, at].reshape(length, pair)], axis=0
            )
            return dot_t(qs, keys) + bias

        def mix(g, scores):
            at_v = slice(feat + g * pair, feat + (g + 1) * pair)
            vals = jnp.concatenate(
                [kv_s[:, i, :, at_v].reshape(length, pair), kvo_ref[0, :, i, :, at_v].reshape(length, pair)], axis=0
            )
            peak = jnp.max(scores, axis=1, keepdims=True)
            weights = jnp.exp2((scores - peak) * scale).astype(jnp.bfloat16)
            both = dot_f32(weights, jnp.concatenate([vals, ones], axis=1))
            mixed = both[:, :pair] / both[:, pair:]
            out = jnp.where(low, mixed[:length], mixed[length:])
            mix_ref[:, i, :, g * pair : (g + 1) * pair] = out.astype(jnp.bfloat16).reshape(deep, run, pair)

        staged(feat // pair, score, mix)
        return carry

    lax.fori_loop(0, group, panel, 0)


def window_mix(half_keep, edges, spots, q, kv_own, gain_row, w_qkv):
    _, deep, wide, run, feat = q.shape
    group = min(GROUP, wide)
    head_width = feat // HEADS
    own = lambda width: pl.BlockSpec((1, deep, group, run, width), lambda i, hk: (hk[0], 0, i, 0, 0))
    side = lambda spot: pl.BlockSpec((deep // 2, group, run, feat), lambda i, hk: (spot, i, 0, 0))
    flat = pl.BlockSpec((deep, group, run, feat), lambda i, hk: (0, i, 0, 0))
    tokens = deep * wide * run
    return pl.pallas_call(
        functools.partial(window_kernel, head_width),
        out_shape=jax.ShapeDtypeStruct((deep, wide, run, feat), jnp.bfloat16),
        grid_spec=pltpu.PrefetchScalarGridSpec(
            num_scalar_prefetch=1,
            grid=(wide // group,),
            in_specs=[
                *[side(spot) for spot in spots],
                own(feat),
                own(2 * feat),
                pl.BlockSpec((1, feat), lambda i, hk: (0, 0)),
                pl.BlockSpec((feat, 3 * feat), lambda i, hk: (0, 0), pipeline_mode=pl.Buffered(1)),
            ],
            out_specs=flat,
            scratch_shapes=[pltpu.VMEM((deep, group, run, 2 * feat), jnp.bfloat16)],
        ),
        compiler_params=pltpu.CompilerParams(vmem_limit_bytes=VMEM_LIMIT),
        cost_estimate=pl.CostEstimate(
            flops=2 * tokens * feat * 2 * feat + 8 * tokens * 256 * feat,
            bytes_accessed=tokens * feat * 10 + feat * feat * 6,
            transcendentals=tokens * 256 * HEADS,
        ),
    )(half_keep, *edges, q, kv_own, gain_row, w_qkv)


def direct_parts(recv, tok_ref, tiles, wanted, cap):
    cut = tok_ref.shape[1] // 2
    wide = tok_ref.shape[2]

    def own(j, seen):
        return tok_ref.at[j // wide, :cut, j % wide], tok_ref.at[j // wide, cut:, j % wide]

    def other(r):
        return lambda j, seen: (recv[r - 1].at[seen[r], :cut], recv[r - 1].at[seen[r], cut:])

    return {r: own if r == 0 else other(r) for r in range(tiles) if (wanted >> r) & 1}


def relay_parts(recv, tok_ref, tiles, wanted, cap):
    near, whole, x_same, x_cross, y_same, y_cross, rest = recv[0], recv[1:5], *recv[5:]
    cut = tok_ref.shape[1] // 2
    wide = tok_ref.shape[2]
    deep = tok_ref.shape[1]
    same = lambda k, j: [(True, whole[k].at[:, j % wide]), (False, whole[k + 2].at[:, j % wide])]
    table = {
        0: lambda j, seen: (tok_ref.at[j // wide, :cut, j % wide], tok_ref.at[j // wide, cut:, j % wide]),
        1: lambda j, seen: (near.at[deep + seen[1], :cut], near.at[deep + seen[1], cut:]),
        2: lambda j, seen: (same(0, j), x_same.at[seen[2] + seen[6]]),
        3: lambda j, seen: (rest.at[seen[3]], x_cross.at[seen[3] + seen[7]]),
        4: lambda j, seen: (y_same.at[seen[4] + seen[6]], same(1, j)),
        5: lambda j, seen: (y_cross.at[seen[5] + seen[7]], rest.at[cap + seen[5]]),
        6: lambda j, seen: (y_same.at[seen[4] + seen[6]], x_same.at[seen[2] + seen[6]]),
        7: lambda j, seen: (y_cross.at[seen[5] + seen[7]], x_cross.at[seen[3] + seen[7]]),
    }
    return {r: table[r] for r in range(tiles) if (wanted >> r) & 1}


def cross_kernel(plan, tiles, head_width, wanted, recv_count, cap, refs):
    me_ref, tile_ref, panel_ref, valid_ref, half_ref, tok_ref = refs[:6]
    recv = refs[6 : 6 + recv_count]
    q_ref, mix_a, mix_b, gain_ref, wqkv_ref, wproj_ref = refs[6 + recv_count : 12 + recv_count]
    out_ref, got, q_s, own_s, res_s, wkv_s, wp_s, kv_s, mixed_s, seen, ids, w_sem, sems = refs[-13:]
    panels, deep, run, feat = got.shape
    half = panels // 2
    cut = deep // 2
    length = deep * run
    me = me_ref[0]
    parts = plan(recv, tok_ref, tiles, wanted, cap)
    for t in range(tiles):
        seen[t] = 0

    def fetch(p, count):
        r = tile_ref[me * panels + p] ^ me
        hit = ((wanted >> r) & 1) == 1

        @pl.when(hit)
        def _():
            ids[count] = p
            j = panel_ref[me * panels + p]
            for k, pick in parts.items():

                @pl.when(r == k)
                def _(pick=pick):
                    for ref, rows, k in zip(pick(j, seen), (slice(0, cut), slice(cut, deep)), (0, 4)):
                        if not isinstance(ref, list):
                            pltpu.make_async_copy(ref, got.at[count, rows], sems.at[k, count]).start()
                            continue
                        for mine, choice in ref:

                            @pl.when((j // half == (me & 1)) == mine)
                            def _(choice=choice, rows=rows, k=k):
                                pltpu.make_async_copy(choice, got.at[count, rows], sems.at[k, count]).start()

            u = p // half
            w = p % half
            pltpu.make_async_copy(q_ref.at[u, :, w], q_s.at[count], sems.at[1, count]).start()

            @pl.when(u == half_ref[0])
            def _():
                pltpu.make_async_copy(mix_a.at[:, w], own_s.at[count], sems.at[2, count]).start()

            @pl.when(u != half_ref[0])
            def _():
                pltpu.make_async_copy(mix_b.at[:, w], own_s.at[count], sems.at[2, count]).start()

        seen[r] = seen[r] + 1
        return count + hit.astype(jnp.int32)

    load_wkv = pltpu.make_async_copy(wqkv_ref.at[:, feat:], wkv_s, w_sem.at[0])
    load_wp = pltpu.make_async_copy(wproj_ref, wp_s, w_sem.at[1])
    load_wkv.start()
    total = lax.fori_loop(0, panels, fetch, jnp.int32(0))
    load_wp.start()
    load_wkv.wait()
    load_wp.wait()

    pair = 2 * head_width
    scale = LOG2E * head_width ** (-0.5)
    low = low_lanes(length, pair, head_width)
    zero = jnp.zeros((length, pair), jnp.bfloat16)
    one = jnp.ones((length, pair), jnp.bfloat16)
    marks = jnp.concatenate([jnp.where(low, one, zero), jnp.where(low, zero, one)], axis=0)
    pairs = feat // pair

    def unit(n, carry):
        first = 2 * n
        for i in range(2):

            @pl.when(first + i < total)
            def _(i=i):
                n_i = first + i
                for k, place in ((0, got.at[n_i, :cut]), (4, got.at[n_i, cut:])):
                    pltpu.make_async_copy(tok_ref.at[0, :cut, 0], place, sems.at[k, n_i]).wait()
                for k, place in ((1, q_s.at[n_i]), (2, own_s.at[n_i])):
                    pltpu.make_async_copy(tok_ref.at[0, :, 0], place, sems.at[k, n_i]).wait()

        rows = got[pl.ds(first, 2)].reshape(2 * length, feat)
        normed = layer_norm(rows, gain_ref[...])
        kv_s[...] = dot_f32(normed, wkv_s[...]).astype(jnp.bfloat16)
        gates = [valid_ref[ids[jnp.minimum(first + i, total - 1)]].astype(jnp.float32) for i in range(2)]

        def score(t):
            i, g = t // pairs, t % pairs
            at = slice(g * pair, (g + 1) * pair)
            q = q_s[first + i, :, :, at].reshape(length, pair)
            key = kv_s[i * length : (i + 1) * length, at]
            keys = jnp.concatenate([jnp.where(low, key, zero), jnp.where(low, zero, key)], axis=0)
            return dot_t(q, keys)

        def mix(t, scores):
            i, g = t // pairs, t % pairs
            at = slice(g * pair, (g + 1) * pair)
            val = kv_s[i * length : (i + 1) * length, feat + g * pair : feat + (g + 1) * pair]
            vals = jnp.concatenate([jnp.where(low, val, zero), jnp.where(low, zero, val)], axis=0)
            parts = []
            for h in range(2):
                part = scores[:, h * length : (h + 1) * length]
                peak = jnp.max(part, axis=1, keepdims=True)
                parts.append(jnp.exp2((part - peak) * scale).astype(jnp.bfloat16))
            both = dot_f32(jnp.concatenate(parts, axis=1), jnp.concatenate([vals, marks], axis=1))
            cross = (both[:, :pair] / both[:, pair:]).astype(jnp.bfloat16)
            own = own_s[first + i, :, :, at].reshape(length, pair)
            blended = gates[i] * own.astype(jnp.float32) + cross.astype(jnp.float32)
            mixed_s[i * length : (i + 1) * length, at] = blended.astype(jnp.bfloat16)

        staged(2 * pairs, score, mix)
        res_s[pl.ds(first, 2)] = dot_f32(mixed_s[...], wp_s[...]).astype(jnp.bfloat16).reshape(2, deep, run, feat)
        for i in range(2):

            @pl.when(first + i < total)
            def _(i=i):
                p = ids[first + i]
                pltpu.make_async_copy(
                    res_s.at[first + i], out_ref.at[p // half, :, p % half], sems.at[3, first + i]
                ).start()

        return carry

    lax.fori_loop(0, (total + 1) // 2, unit, 0)

    def finish(n, carry):
        pltpu.make_async_copy(res_s.at[n], out_ref.at[0, :, 0], sems.at[3, n]).wait()
        return carry

    lax.fori_loop(0, total, finish, 0)


def cross_and_project(
    plan, wanted, tiles, cap, me, tile_table, panel_table, valid, half_keep, tok, recv, q, mixes, gain_row, w_qkv, w_proj, earlier
):
    halves, deep, wide, run, feat = tok.shape
    panels = halves * wide
    head_width = feat // HEADS
    length = deep * run
    smem = pl.BlockSpec(memory_space=pltpu.SMEM)
    anym = pl.BlockSpec(memory_space=pl.ANY)
    share = bin(wanted).count("1") / tiles
    tokens = int(panels * length * share)
    many = pltpu.VMEM((panels, deep, run, feat), jnp.bfloat16)
    operands = [me, tile_table, panel_table, valid, half_keep, tok, *recv, q, *mixes, gain_row, w_qkv, w_proj]
    specs = [smem] * 5 + [anym] * (len(recv) + 4) + [pl.BlockSpec((1, feat), lambda: (0, 0))] + [anym] * 2
    aliases = {}
    if earlier is not None:
        aliases = {len(operands): 0}
        operands.append(earlier)
        specs.append(anym)

    def kernel(*refs):
        cross_kernel(plan, tiles, head_width, wanted, len(recv), cap, refs)

    return pl.pallas_call(
        kernel,
        out_shape=jax.ShapeDtypeStruct(tok.shape, jnp.bfloat16),
        in_specs=specs,
        out_specs=anym,
        scratch_shapes=[
            many,
            many,
            many,
            many,
            pltpu.VMEM((feat, 2 * feat), jnp.bfloat16),
            pltpu.VMEM((feat, feat), jnp.bfloat16),
            pltpu.VMEM((2 * length, 2 * feat), jnp.bfloat16),
            pltpu.VMEM((2 * length, feat), jnp.bfloat16),
            pltpu.SMEM((tiles,), jnp.int32),
            pltpu.SMEM((panels,), jnp.int32),
            pltpu.SemaphoreType.DMA((2,)),
            pltpu.SemaphoreType.DMA((5, panels)),
        ],
        input_output_aliases=aliases,
        compiler_params=pltpu.CompilerParams(vmem_limit_bytes=VMEM_LIMIT),
        cost_estimate=pl.CostEstimate(
            flops=2 * tokens * feat * 3 * feat + 8 * tokens * 128 * feat,
            bytes_accessed=tokens * feat * 8 + feat * feat * 6,
            transcendentals=tokens * 128 * HEADS,
        ),
    )(*operands)


def per_device(tokens, gain, w_qkv, w_proj, scene_first, window_valid, partner_tile, partner_panel):
    _, tok_rows, tok_cols, feat = tokens.shape
    run = 16
    wide = tok_cols // run
    tok = tokens.reshape(2, tok_rows // 2, wide, run, feat)
    tiles = partner_tile.shape[1]
    panels = partner_tile.shape[2]
    cap = 2 * max(1, panels // tiles)
    slab_count = scene_first.shape[0]
    me = lax.axis_index("tile").reshape(1).astype(jnp.int32)
    tile_table = partner_tile.reshape(tiles * panels)
    panel_table = partner_panel.reshape(tiles * panels)
    valid = window_valid.reshape(panels)
    gain_row = gain.reshape(1, feat)
    slab_index = lax.axis_index(("scene", "tile"))
    after_index = jnp.minimum(slab_index + 1, slab_count - 1)
    own_first = jnp.logical_or(scene_first[slab_index] == 1, slab_index == 0)
    next_first = jnp.logical_or(scene_first[after_index] == 1, slab_index + 1 >= slab_count)
    keep_before = jnp.logical_not(own_first).astype(jnp.int32)
    keep_after = jnp.logical_not(next_first).astype(jnp.int32)

    def xor(block, bits):
        return lax.ppermute(block, "tile", [(i, i ^ bits) for i in range(tiles)])

    def cross(plan, wanted, recv, mixes, half_keep, earlier):
        return cross_and_project(
            plan,
            wanted,
            tiles,
            cap,
            me,
            tile_table,
            panel_table,
            valid,
            half_keep,
            tok,
            recv,
            q,
            mixes,
            gain_row,
            w_qkv,
            w_proj,
            earlier,
        )

    if tiles == 8:
        fence = lax.optimization_barrier
        odd = slab_index % 2
        direct = jnp.logical_or(slab_index % 4 == 1, slab_index % 4 == 2).astype(jnp.int32)
        near_half = jnp.stack([1 - odd, jnp.where(odd == 1, keep_before, keep_after), direct]).astype(jnp.int32)
        far_half = jnp.stack([odd, jnp.where(odd == 1, keep_after, keep_before), direct]).astype(jnp.int32)
        links_a, links_b, links_c = [], [], []
        for low in range(1, slab_count - 1, 2):
            links_a += [(low ^ 2, low + 1), ((low + 1) ^ 2, low)]
            if low % 4 == 1:
                links_b += [(low, low + 1), (low + 1, low)]
            else:
                links_c += [(low ^ 4, low + 1), ((low + 1) ^ 4, low)]

        rim_x, rim_y, off_x, off_y = split_halves(me, tok)
        own_rim = rim_y
        rim_x, rim_y = xor(rim_x, 2), xor(rim_y, 4)
        off_x, off_y = xor(off_x, 2), xor(off_y, 4)
        q, kv = project_own(tok, gain_row, w_qkv)
        me_next, q = fence((me, q))
        near = xor(pack_near(me_next, tile_table, panel_table, tok, cap), 1)
        edge_b = lax.ppermute(own_rim, ("scene", "tile"), links_b)
        mix_near = window_mix(near_half, (near, near), (0, 1), q, kv, gain_row, w_qkv)
        rim_x, rim_y, mix_near = fence((rim_x, rim_y, mix_near))
        edge_c = lax.ppermute(rim_y, ("scene", "tile"), links_c)
        edge_a = lax.ppermute(rim_x, ("scene", "tile"), links_a)
        off_x, off_y, mix_near = fence((off_x, off_y, mix_near))
        sides = (rim_x, rim_y, off_x, off_y)
        x_same, x_cross, y_same, y_cross, rest = pack_far(me, tile_table, panel_table, tok, sides, cap)
        y_same, rest = xor(y_same, 4), xor(rest, 1)
        edge_a, edge_b, edge_c, x_same, y_cross = fence((edge_a, edge_b, edge_c, x_same, y_cross))
        x_same, y_cross = xor(x_same, 2), xor(y_cross, 5)
        mix_far = window_mix(far_half, (edge_a, edge_b, edge_c), (0, 0, 0), q, kv, gain_row, w_qkv)
        x_cross, mix_far = fence((x_cross, mix_far))
        x_cross = xor(x_cross, 3)
        mixes = (mix_near, mix_far)
        early = (near, *sides, x_same, rest, y_same, y_cross, rest)
        late = (near, *sides, x_same, x_cross, y_same, y_cross, rest)
        out = cross(relay_parts, 0b01110111, early, mixes, near_half, None)
        out = cross(relay_parts, 0b10001000, late, mixes, near_half, out)
    else:
        forward = [(i, i + 1) for i in range(slab_count - 1)]
        backward = [(i + 1, i) for i in range(slab_count - 1)]
        before = lax.ppermute(tok[1], ("scene", "tile"), forward)
        after = lax.ppermute(tok[0], ("scene", "tile"), backward)
        outgoing = pack(me, tile_table, panel_table, tok, tiles, cap)
        recv = [xor(outgoing[r - 1], r) for r in range(1, tiles)]
        q, kv = project_own(tok, gain_row, w_qkv)
        zero = jnp.zeros((), jnp.int32)
        upper = jnp.stack([zero, keep_before])
        mix_up = window_mix(upper, (before, before), (0, 1), q, kv, gain_row, w_qkv)
        mix_down = window_mix(jnp.stack([zero + 1, keep_after]), (after, after), (0, 1), q, kv, gain_row, w_qkv)
        out = cross(direct_parts, (1 << tiles) - 1, recv, (mix_up, mix_down), upper, None)
    return out.reshape(tokens.shape)


def solution(mesh):
    in_specs = (
        P(("scene", "tile"), None, None, None),
        P(),
        P(),
        P(),
        P(),
        P(("scene", "tile"), None),
        P("scene", None, None, None),
        P("scene", None, None),
    )
    out_specs = P(("scene", "tile"), None, None, None)
    return jax.shard_map(per_device, mesh=mesh, in_specs=in_specs, out_specs=out_specs, check_vma=False)
```

```python
import functools

import jax
import jax.numpy as jnp
from jax import lax
from jax.experimental import pallas as pl
from jax.experimental.pallas import tpu as pltpu
from jax.sharding import PartitionSpec as P

HEADS = 16
NORM_EPS = 1e-05
LOG2E = 1.4426950408889634
VMEM_LIMIT = 56 * 1024 * 1024
GROUP = 4


def layer_norm(rows, gain_row):
    values = rows.astype(jnp.float32)
    centred = values - jnp.mean(values, axis=-1, keepdims=True)
    spread = jnp.mean(centred * centred, axis=-1, keepdims=True)
    return (centred * lax.rsqrt(spread + NORM_EPS) * gain_row.astype(jnp.float32)).astype(jnp.bfloat16)


def dot_f32(left, right):
    return jnp.dot(left, right, preferred_element_type=jnp.float32)


def dot_t(left, right):
    return lax.dot_general(left, right, (((1,), (1,)), ((), ())), preferred_element_type=jnp.float32)


def staged(count, first, second):
    held = first(0)
    for g in range(count):
        coming = first(g + 1) if g + 1 < count else None
        second(g, held)
        held = coming


def low_lanes(rows, width, head_width):
    return lax.broadcasted_iota(jnp.int32, (rows, width), 1) < head_width


def pack_kernel(tiles, panels, cap, tile_ref, panel_ref, tok_ref, *rest):
    outs, slab, sem, sems = rest[: tiles - 1], rest[tiles - 1], rest[tiles], rest[tiles + 1]
    me = lax.axis_index("tile")
    load = pltpu.make_async_copy(tok_ref, slab, sem)
    load.start()
    load.wait()
    counts = []
    for r in range(1, tiles):
        asker = me ^ r
        out = outs[r - 1]

        def body(p, count, asker=asker, out=out, r=r):
            hit = jnp.logical_and(tile_ref[0, asker, p] == me, count < cap)

            @pl.when(hit)
            def _():
                j = panel_ref[0, asker, p]
                pltpu.make_async_copy(
                    slab.at[j // (panels // 2), :, j % (panels // 2)], out.at[count], sems.at[r, count]
                ).start()

            return count + hit.astype(jnp.int32)

        counts.append(lax.fori_loop(0, panels, body, jnp.int32(0)))
    for r in range(1, tiles):
        for c in range(cap):

            @pl.when(c < counts[r - 1])
            def _(r=r, c=c):
                pltpu.make_async_copy(slab.at[0, :, 0], outs[r - 1].at[c], sems.at[r, c]).wait()


def pack(tile_table, panel_table, tok, tiles, cap):
    panels = 2 * tok.shape[2]
    block = (cap, tok.shape[1], tok.shape[3], tok.shape[4])
    smem = pl.BlockSpec(memory_space=pltpu.SMEM)
    anym = pl.BlockSpec(memory_space=pl.ANY)
    return pl.pallas_call(
        functools.partial(pack_kernel, tiles, panels, cap),
        out_shape=[jax.ShapeDtypeStruct(block, tok.dtype)] * (tiles - 1),
        in_specs=[smem, smem, anym],
        out_specs=[anym] * (tiles - 1),
        scratch_shapes=[
            pltpu.VMEM(tok.shape, tok.dtype),
            pltpu.SemaphoreType.DMA,
            pltpu.SemaphoreType.DMA((tiles, cap)),
        ],
        cost_estimate=pl.CostEstimate(flops=0, bytes_accessed=16 << 20, transcendentals=0),
    )(tile_table, panel_table, tok)


def copy_through(pairs, bounce, sems):
    loads = [pltpu.make_async_copy(src, bounce.at[k], sems.at[0, k]) for k, (src, _) in enumerate(pairs)]
    for load in loads:
        load.start()
    stores = []
    for k, (_, dst) in enumerate(pairs):
        loads[k].wait()
        store = pltpu.make_async_copy(bounce.at[k], dst, sems.at[1, k])
        store.start()
        stores.append(store)
    for store in stores:
        store.wait()


def halves_kernel(tok_ref, *rest):
    outs, bounce, sems = rest[:4], rest[4], rest[5]
    deep = outs[0].shape[0]
    part = lax.axis_index("tile") & 1
    sources = [
        tok_ref.at[part, :deep],
        tok_ref.at[part, deep:],
        tok_ref.at[1 - part, :deep],
        tok_ref.at[1 - part, deep:],
    ]
    copy_through(list(zip(sources, outs)), bounce, sems)


def split_halves(tok):
    halves, deep, wide, run, feat = tok.shape
    part = (deep // 2, wide, run, feat)
    anym = pl.BlockSpec(memory_space=pl.ANY)
    return pl.pallas_call(
        halves_kernel,
        out_shape=[jax.ShapeDtypeStruct(part, tok.dtype)] * 4,
        in_specs=[anym],
        out_specs=[anym] * 4,
        scratch_shapes=[pltpu.VMEM((4,) + part, tok.dtype), pltpu.SemaphoreType.DMA((2, 4))],
        cost_estimate=pl.CostEstimate(flops=0, bytes_accessed=8 << 20, transcendentals=0),
    )(tok)


def far_kernel(cap, tile_ref, panel_ref, tok_ref, *rest):
    sides, outs, stage, in_sems, out_sems = rest[:4], rest[4:9], *rest[9:]
    halves, deep, wide, run, feat = tok_ref.shape
    panels = halves * wide
    cut = deep // 2
    me = lax.axis_index("tile")
    part = me & 1

    def bring(cond, ref, k, spot):
        @pl.when(cond)
        def _():
            pltpu.make_async_copy(ref, stage.at[k, spot], in_sems.at[k, spot]).start()

    def bring_side(cond, axis, j, k, spot):
        aligned = j // wide == part
        bring(jnp.logical_and(cond, aligned), sides[axis].at[:, j % wide], k, spot)
        bring(jnp.logical_and(cond, jnp.logical_not(aligned)), sides[2 + axis].at[:, j % wide], k, spot)

    totals = []
    for k, (bits, relay) in enumerate(((2, 4), (4, 2), (3, 4), (5, 2))):
        asker = me ^ bits
        axis, rows = (1, slice(cut, deep)) if relay == 4 else (0, slice(0, cut))

        def body(p, count, k=k, asker=asker, relay=relay, axis=axis, rows=rows):
            named = tile_ref[0, asker, p]
            own = jnp.logical_and(named == me, count < 2 * cap)
            other = jnp.logical_and(named == me ^ relay, count < 2 * cap)
            j = panel_ref[0, asker, p]
            bring(own, tok_ref.at[j // wide, rows, j % wide], k, count)
            bring_side(other, axis, j, k, count)
            return count + jnp.logical_or(own, other).astype(jnp.int32)

        totals.append(lax.fori_loop(0, panels, body, jnp.int32(0)))

    def near(p, counts):
        named = tile_ref[0, me ^ 1, p]
        j = panel_ref[0, me ^ 1, p]
        hits = [jnp.logical_and(named == me ^ relay, counts[k] < cap) for k, relay in enumerate((2, 4, 0))]
        for k in range(2):
            bring_side(hits[k], k, j, 4, k * cap + counts[k])
        bring(hits[2], tok_ref.at[j // wide, :cut, j % wide], 4, 2 * cap + counts[2])
        bring(hits[2], tok_ref.at[j // wide, cut:, j % wide], 4, 3 * cap + counts[2])
        return tuple(count + hit.astype(jnp.int32) for count, hit in zip(counts, hits))

    near_totals = lax.fori_loop(0, panels, near, (jnp.int32(0),) * 3)
    used = []
    for k in range(4):
        used += [(k, c, c < totals[k]) for c in range(2 * cap)]
    used += [(4, c, c % cap < near_totals[min(c // cap, 2)]) for c in range(4 * cap)]
    for k, c, cond in used:

        @pl.when(cond)
        def _(k=k, c=c):
            pltpu.make_async_copy(sides[0].at[:, 0], stage.at[k, c], in_sems.at[k, c]).wait()
            pltpu.make_async_copy(stage.at[k, c], outs[k].at[c], out_sems.at[k, c]).start()

    for k, c, cond in used:

        @pl.when(cond)
        def _(k=k, c=c):
            pltpu.make_async_copy(stage.at[k, c], outs[k].at[c], out_sems.at[k, c]).wait()


def pack_far(tile_table, panel_table, tok, sides, cap):
    halves, deep, wide, run, feat = tok.shape
    smem = pl.BlockSpec(memory_space=pltpu.SMEM)
    anym = pl.BlockSpec(memory_space=pl.ANY)
    block = (2 * cap, deep // 2, run, feat)
    return pl.pallas_call(
        functools.partial(far_kernel, cap),
        out_shape=[jax.ShapeDtypeStruct(block, tok.dtype)] * 4
        + [jax.ShapeDtypeStruct((4 * cap,) + block[1:], tok.dtype)],
        in_specs=[smem, smem] + [anym] * 5,
        out_specs=[anym] * 5,
        scratch_shapes=[
            pltpu.VMEM((5, 4 * cap) + block[1:], tok.dtype),
            pltpu.SemaphoreType.DMA((5, 4 * cap)),
            pltpu.SemaphoreType.DMA((5, 4 * cap)),
        ],
        compiler_params=pltpu.CompilerParams(vmem_limit_bytes=VMEM_LIMIT),
        cost_estimate=pl.CostEstimate(flops=0, bytes_accessed=6 << 20, transcendentals=0),
    )(tile_table, panel_table, tok, *sides)


def qkv_kernel(tok_ref, gain_ref, w_ref, q_ref, kv_ref):
    dims = tok_ref.shape
    feat = dims[-1]
    rows = dims[1] * dims[2] * dims[3]
    normed = layer_norm(tok_ref[...].reshape(rows, feat), gain_ref[...])
    q_ref[...] = dot_f32(normed, w_ref[:, :feat]).astype(jnp.bfloat16).reshape(q_ref.shape)
    kv_ref[...] = dot_f32(normed, w_ref[:, feat:]).astype(jnp.bfloat16).reshape(kv_ref.shape)


def project_own(tok, gain_row, w_qkv):
    halves, deep, wide, run, feat = tok.shape
    step = deep // 2
    spec = lambda width: pl.BlockSpec((1, step, wide, run, width), lambda i: (i // 2, i % 2, 0, 0, 0))
    tokens = halves * deep * wide * run
    return pl.pallas_call(
        qkv_kernel,
        grid=(halves * 2,),
        out_shape=[
            jax.ShapeDtypeStruct((halves, deep, wide, run, feat), jnp.bfloat16),
            jax.ShapeDtypeStruct((halves, deep, wide, run, 2 * feat), jnp.bfloat16),
        ],
        in_specs=[
            spec(feat),
            pl.BlockSpec((1, feat), lambda i: (0, 0)),
            pl.BlockSpec((feat, 3 * feat), lambda i: (0, 0), pipeline_mode=pl.Buffered(1)),
        ],
        out_specs=[spec(feat), spec(2 * feat)],
        compiler_params=pltpu.CompilerParams(vmem_limit_bytes=VMEM_LIMIT),
        cost_estimate=pl.CostEstimate(
            flops=2 * tokens * feat * 3 * feat, bytes_accessed=tokens * feat * 8 + feat * feat * 6, transcendentals=0
        ),
    )(tok, gain_row, w_qkv)


def window_kernel(head_width, half_ref, *refs):
    edges, (q_ref, kvo_ref, gain_ref, w_ref, mix_ref, kv_s) = refs[:-6], refs[-6:]
    deep, group, run, feat = mix_ref.shape
    length = deep * run
    bottom = edges[1][...]
    if len(edges) == 3:
        bottom = jnp.where(half_ref[2] == 1, bottom, edges[2][...])
    rows = jnp.concatenate([edges[0][...], bottom], axis=0).reshape(deep * group * run, feat)
    normed = layer_norm(rows, gain_ref[...])
    kv_s[...] = dot_f32(normed, w_ref[:, feat:]).astype(jnp.bfloat16).reshape(kv_s.shape)
    pair = 2 * head_width
    scale = LOG2E * head_width ** (-0.5)
    bias = jnp.where(
        jnp.logical_and(half_ref[1] == 0, lax.broadcasted_iota(jnp.int32, (1, 2 * length), 1) < length), -jnp.inf, 0.0
    )
    low = low_lanes(length, pair, head_width)
    ones = jnp.ones((2 * length, pair), jnp.bfloat16)
    zero = jnp.zeros((length, pair), jnp.bfloat16)
    def panel(i, carry):
        def score(g):
            at = slice(g * pair, (g + 1) * pair)
            q = q_ref[0, :, i, :, at].reshape(length, pair)
            qs = jnp.concatenate([jnp.where(low, q, zero), jnp.where(low, zero, q)], axis=0)
            keys = jnp.concatenate(
                [kv_s[:, i, :, at].reshape(length, pair), kvo_ref[0, :, i, :, at].reshape(length, pair)], axis=0
            )
            return dot_t(qs, keys) + bias

        def mix(g, scores):
            at_v = slice(feat + g * pair, feat + (g + 1) * pair)
            vals = jnp.concatenate(
                [kv_s[:, i, :, at_v].reshape(length, pair), kvo_ref[0, :, i, :, at_v].reshape(length, pair)], axis=0
            )
            peak = jnp.max(scores, axis=1, keepdims=True)
            weights = jnp.exp2((scores - peak) * scale).astype(jnp.bfloat16)
            both = dot_f32(weights, jnp.concatenate([vals, ones], axis=1))
            mixed = both[:, :pair] / both[:, pair:]
            out = jnp.where(low, mixed[:length], mixed[length:])
            mix_ref[:, i, :, g * pair : (g + 1) * pair] = out.astype(jnp.bfloat16).reshape(deep, run, pair)

        staged(feat // pair, score, mix)
        return carry

    lax.fori_loop(0, group, panel, 0)


def window_mix(half_keep, edges, spots, q, kv_own, gain_row, w_qkv):
    _, deep, wide, run, feat = q.shape
    group = min(GROUP, wide)
    head_width = feat // HEADS
    own = lambda width: pl.BlockSpec((1, deep, group, run, width), lambda i, hk: (hk[0], 0, i, 0, 0))
    side = lambda spot: pl.BlockSpec((deep // 2, group, run, feat), lambda i, hk: (spot, i, 0, 0))
    flat = pl.BlockSpec((deep, group, run, feat), lambda i, hk: (0, i, 0, 0))
    tokens = deep * wide * run
    return pl.pallas_call(
        functools.partial(window_kernel, head_width),
        out_shape=jax.ShapeDtypeStruct((deep, wide, run, feat), jnp.bfloat16),
        grid_spec=pltpu.PrefetchScalarGridSpec(
            num_scalar_prefetch=1,
            grid=(wide // group,),
            in_specs=[
                *[side(spot) for spot in spots],
                own(feat),
                own(2 * feat),
                pl.BlockSpec((1, feat), lambda i, hk: (0, 0)),
                pl.BlockSpec((feat, 3 * feat), lambda i, hk: (0, 0), pipeline_mode=pl.Buffered(1)),
            ],
            out_specs=flat,
            scratch_shapes=[pltpu.VMEM((deep, group, run, 2 * feat), jnp.bfloat16)],
        ),
        compiler_params=pltpu.CompilerParams(vmem_limit_bytes=VMEM_LIMIT),
        cost_estimate=pl.CostEstimate(
            flops=2 * tokens * feat * 2 * feat + 8 * tokens * 256 * feat,
            bytes_accessed=tokens * feat * 10 + feat * feat * 6,
            transcendentals=tokens * 256 * HEADS,
        ),
    )(half_keep, *edges, q, kv_own, gain_row, w_qkv)


def direct_parts(recv, tok_ref, tiles, wanted, cap):
    cut = tok_ref.shape[1] // 2
    wide = tok_ref.shape[2]

    def own(j, seen):
        return tok_ref.at[j // wide, :cut, j % wide], tok_ref.at[j // wide, cut:, j % wide]

    def other(r):
        return lambda j, seen: (recv[r - 1].at[seen[r], :cut], recv[r - 1].at[seen[r], cut:])

    return {r: own if r == 0 else other(r) for r in range(tiles) if (wanted >> r) & 1}


def relay_parts(recv, tok_ref, tiles, wanted, cap):
    whole, x_same, x_cross, y_same, y_cross, rest = recv[:4], *recv[4:]
    cut = tok_ref.shape[1] // 2
    wide = tok_ref.shape[2]
    same = lambda k, j: [(True, whole[k].at[:, j % wide]), (False, whole[k + 2].at[:, j % wide])]
    table = {
        0: lambda j, seen: (tok_ref.at[j // wide, :cut, j % wide], tok_ref.at[j // wide, cut:, j % wide]),
        1: lambda j, seen: (rest.at[2 * cap + seen[1]], rest.at[3 * cap + seen[1]]),
        2: lambda j, seen: (same(0, j), x_same.at[seen[2] + seen[6]]),
        3: lambda j, seen: (rest.at[seen[3]], x_cross.at[seen[3] + seen[7]]),
        4: lambda j, seen: (y_same.at[seen[4] + seen[6]], same(1, j)),
        5: lambda j, seen: (y_cross.at[seen[5] + seen[7]], rest.at[cap + seen[5]]),
        6: lambda j, seen: (y_same.at[seen[4] + seen[6]], x_same.at[seen[2] + seen[6]]),
        7: lambda j, seen: (y_cross.at[seen[5] + seen[7]], x_cross.at[seen[3] + seen[7]]),
    }
    return {r: table[r] for r in range(tiles) if (wanted >> r) & 1}


def cross_kernel(plan, tiles, head_width, wanted, recv_count, cap, refs):
    tile_ref, panel_ref, valid_ref, half_ref, tok_ref = refs[:5]
    recv = refs[5 : 5 + recv_count]
    q_ref, mix_a, mix_b, gain_ref, wqkv_ref, wproj_ref = refs[5 + recv_count : 11 + recv_count]
    out_ref, got, q_s, own_s, res_s, wkv_s, wp_s, normed_s, kv_s, mixed_s, seen, ids, w_sem, sems = refs[-14:]
    panels, deep, run, feat = got.shape
    half = panels // 2
    cut = deep // 2
    length = deep * run
    me = lax.axis_index("tile")
    parts = plan(recv, tok_ref, tiles, wanted, cap)
    for t in range(tiles):
        seen[t] = 0

    def fetch(p, count):
        r = tile_ref[0, me, p] ^ me
        hit = ((wanted >> r) & 1) == 1

        @pl.when(hit)
        def _():
            ids[count] = p
            j = panel_ref[0, me, p]
            for k, pick in parts.items():

                @pl.when(r == k)
                def _(pick=pick):
                    for ref, rows, k in zip(pick(j, seen), (slice(0, cut), slice(cut, deep)), (0, 4)):
                        if not isinstance(ref, list):
                            pltpu.make_async_copy(ref, got.at[count, rows], sems.at[k, count]).start()
                            continue
                        for mine, choice in ref:

                            @pl.when((j // half == (me & 1)) == mine)
                            def _(choice=choice, rows=rows, k=k):
                                pltpu.make_async_copy(choice, got.at[count, rows], sems.at[k, count]).start()

            u = p // half
            w = p % half
            pltpu.make_async_copy(q_ref.at[u, :, w], q_s.at[count], sems.at[1, count]).start()

            @pl.when(u == half_ref[0])
            def _():
                pltpu.make_async_copy(mix_a.at[:, w], own_s.at[count], sems.at[2, count]).start()

            @pl.when(u != half_ref[0])
            def _():
                pltpu.make_async_copy(mix_b.at[:, w], own_s.at[count], sems.at[2, count]).start()

        seen[r] = seen[r] + 1
        return count + hit.astype(jnp.int32)

    load_wkv = pltpu.make_async_copy(wqkv_ref.at[:, feat:], wkv_s, w_sem.at[0])
    load_wp = pltpu.make_async_copy(wproj_ref, wp_s, w_sem.at[1])
    load_wkv.start()
    total = lax.fori_loop(0, panels, fetch, jnp.int32(0))
    load_wp.start()

    pair = 2 * head_width
    scale = LOG2E * head_width ** (-0.5)
    low = low_lanes(length, pair, head_width)
    zero = jnp.zeros((length, pair), jnp.bfloat16)
    one = jnp.ones((length, pair), jnp.bfloat16)
    marks = jnp.concatenate([jnp.where(low, one, zero), jnp.where(low, zero, one)], axis=0)
    pairs = feat // pair

    def unit(n, carry):
        first = 2 * n
        for i in range(2):

            @pl.when(first + i < total)
            def _(i=i):
                n_i = first + i
                for k, place in ((0, got.at[n_i, :cut]), (4, got.at[n_i, cut:])):
                    pltpu.make_async_copy(tok_ref.at[0, :cut, 0], place, sems.at[k, n_i]).wait()
                for k, place in ((1, q_s.at[n_i]), (2, own_s.at[n_i])):
                    pltpu.make_async_copy(tok_ref.at[0, :, 0], place, sems.at[k, n_i]).wait()

        rows = got[pl.ds(first, 2)].reshape(2 * length, feat)
        normed_s[...] = layer_norm(rows, gain_ref[...])

        @pl.when(n == 0)
        def _():
            load_wkv.wait()

        kv_s[...] = dot_f32(normed_s[...], wkv_s[...]).astype(jnp.bfloat16)

        @pl.when(n == 0)
        def _():
            load_wp.wait()

        gates = [valid_ref[ids[jnp.minimum(first + i, total - 1)]].astype(jnp.float32) for i in range(2)]

        def score(t):
            i, g = t // pairs, t % pairs
            at = slice(g * pair, (g + 1) * pair)
            q = q_s[first + i, :, :, at].reshape(length, pair)
            key = kv_s[i * length : (i + 1) * length, at]
            keys = jnp.concatenate([jnp.where(low, key, zero), jnp.where(low, zero, key)], axis=0)
            return dot_t(q, keys)

        def mix(t, scores):
            i, g = t // pairs, t % pairs
            at = slice(g * pair, (g + 1) * pair)
            val = kv_s[i * length : (i + 1) * length, feat + g * pair : feat + (g + 1) * pair]
            vals = jnp.concatenate([jnp.where(low, val, zero), jnp.where(low, zero, val)], axis=0)
            parts = []
            for h in range(2):
                part = scores[:, h * length : (h + 1) * length]
                peak = jnp.max(part, axis=1, keepdims=True)
                parts.append(jnp.exp2((part - peak) * scale).astype(jnp.bfloat16))
            both = dot_f32(jnp.concatenate(parts, axis=1), jnp.concatenate([vals, marks], axis=1))
            cross = (both[:, :pair] / both[:, pair:]).astype(jnp.bfloat16)
            own = own_s[first + i, :, :, at].reshape(length, pair)
            blended = gates[i] * own.astype(jnp.float32) + cross.astype(jnp.float32)
            mixed_s[i * length : (i + 1) * length, at] = blended.astype(jnp.bfloat16)

        staged(2 * pairs, score, mix)
        res_s[pl.ds(first, 2)] = dot_f32(mixed_s[...], wp_s[...]).astype(jnp.bfloat16).reshape(2, deep, run, feat)
        for i in range(2):

            @pl.when(first + i < total)
            def _(i=i):
                p = ids[first + i]
                pltpu.make_async_copy(
                    res_s.at[first + i], out_ref.at[p // half, :, p % half], sems.at[3, first + i]
                ).start()

        return carry

    lax.fori_loop(0, (total + 1) // 2, unit, 0)

    @pl.when(total == 0)
    def _():
        load_wkv.wait()
        load_wp.wait()

    def finish(n, carry):
        pltpu.make_async_copy(res_s.at[n], out_ref.at[0, :, 0], sems.at[3, n]).wait()
        return carry

    lax.fori_loop(0, total, finish, 0)


def cross_and_project(
    plan, wanted, tiles, cap, tile_table, panel_table, valid, half_keep, tok, recv, q, mixes, gain_row, w_qkv, w_proj, earlier
):
    halves, deep, wide, run, feat = tok.shape
    panels = halves * wide
    head_width = feat // HEADS
    length = deep * run
    smem = pl.BlockSpec(memory_space=pltpu.SMEM)
    anym = pl.BlockSpec(memory_space=pl.ANY)
    share = bin(wanted).count("1") / tiles
    tokens = int(panels * length * share)
    many = pltpu.VMEM((panels, deep, run, feat), jnp.bfloat16)
    operands = [tile_table, panel_table, valid, half_keep, tok, *recv, q, *mixes, gain_row, w_qkv, w_proj]
    specs = [smem] * 4 + [anym] * (len(recv) + 4) + [pl.BlockSpec((1, feat), lambda: (0, 0))] + [anym] * 2
    aliases = {}
    if earlier is not None:
        aliases = {len(operands): 0}
        operands.append(earlier)
        specs.append(anym)

    def kernel(*refs):
        cross_kernel(plan, tiles, head_width, wanted, len(recv), cap, refs)

    return pl.pallas_call(
        kernel,
        out_shape=jax.ShapeDtypeStruct(tok.shape, jnp.bfloat16),
        in_specs=specs,
        out_specs=anym,
        scratch_shapes=[
            many,
            many,
            many,
            many,
            pltpu.VMEM((feat, 2 * feat), jnp.bfloat16),
            pltpu.VMEM((feat, feat), jnp.bfloat16),
            pltpu.VMEM((2 * length, feat), jnp.bfloat16),
            pltpu.VMEM((2 * length, 2 * feat), jnp.bfloat16),
            pltpu.VMEM((2 * length, feat), jnp.bfloat16),
            pltpu.SMEM((tiles,), jnp.int32),
            pltpu.SMEM((panels,), jnp.int32),
            pltpu.SemaphoreType.DMA((2,)),
            pltpu.SemaphoreType.DMA((5, panels)),
        ],
        input_output_aliases=aliases,
        compiler_params=pltpu.CompilerParams(vmem_limit_bytes=VMEM_LIMIT),
        cost_estimate=pl.CostEstimate(
            flops=2 * tokens * feat * 3 * feat + 8 * tokens * 128 * feat,
            bytes_accessed=tokens * feat * 8 + feat * feat * 6,
            transcendentals=tokens * 128 * HEADS,
        ),
    )(*operands)


def per_device(tokens, gain, w_qkv, w_proj, scene_first, window_valid, partner_tile, partner_panel):
    _, tok_rows, tok_cols, feat = tokens.shape
    run = 16
    wide = tok_cols // run
    tok = tokens.reshape(2, tok_rows // 2, wide, run, feat)
    tiles = partner_tile.shape[1]
    panels = partner_tile.shape[2]
    cap = 2 * max(1, panels // tiles)
    slab_count = scene_first.shape[0]
    tile_table = partner_tile[:, :, :, 0]
    panel_table = partner_panel
    valid = window_valid.reshape(panels)
    gain_row = gain.reshape(1, feat)
    slab_index = lax.axis_index(("scene", "tile"))
    after_index = jnp.minimum(slab_index + 1, slab_count - 1)
    own_first = jnp.logical_or(scene_first[slab_index] == 1, slab_index == 0)
    next_first = jnp.logical_or(scene_first[after_index] == 1, slab_index + 1 >= slab_count)
    keep_before = jnp.logical_not(own_first).astype(jnp.int32)
    keep_after = jnp.logical_not(next_first).astype(jnp.int32)

    def xor(block, bits):
        return lax.ppermute(block, "tile", [(i, i ^ bits) for i in range(tiles)])

    def cross(plan, wanted, recv, mixes, half_keep, earlier):
        return cross_and_project(
            plan,
            wanted,
            tiles,
            cap,
            tile_table,
            panel_table,
            valid,
            half_keep,
            tok,
            recv,
            q,
            mixes,
            gain_row,
            w_qkv,
            w_proj,
            earlier,
        )

    if tiles == 8:
        fence = lax.optimization_barrier
        odd = slab_index % 2
        direct = jnp.logical_or(slab_index % 4 == 1, slab_index % 4 == 2).astype(jnp.int32)
        near_half = jnp.stack([1 - odd, jnp.where(odd == 1, keep_before, keep_after), direct]).astype(jnp.int32)
        far_half = jnp.stack([odd, jnp.where(odd == 1, keep_after, keep_before), direct]).astype(jnp.int32)
        links_a, links_b, links_c = [], [], []
        for low in range(1, slab_count - 1, 2):
            links_a += [(low ^ 2, low + 1), ((low + 1) ^ 2, low)]
            if low % 4 == 1:
                links_b += [(low, low + 1), (low + 1, low)]
            else:
                links_c += [(low ^ 4, low + 1), ((low + 1) ^ 4, low)]

        rim_x, rim_y, off_x, off_y = split_halves(tok)
        rim_x, rim_y, off_x, off_y, gain_next = fence((rim_x, rim_y, off_x, off_y, gain_row))
        near = (xor(off_x, 1), xor(off_y, 1))
        own_rim = rim_y
        rim_x, rim_y = xor(rim_x, 2), xor(rim_y, 4)
        off_x, off_y = xor(off_x, 2), xor(off_y, 4)
        q, kv = project_own(tok, gain_next, w_qkv)
        edge_b = lax.ppermute(own_rim, ("scene", "tile"), links_b)
        mix_near = window_mix(near_half, near, (0, 0), q, kv, gain_row, w_qkv)
        rim_x, rim_y, mix_near = fence((rim_x, rim_y, mix_near))
        edge_c = lax.ppermute(rim_y, ("scene", "tile"), links_c)
        edge_a = lax.ppermute(rim_x, ("scene", "tile"), links_a)
        sides = (rim_x, rim_y, off_x, off_y)
        x_same, y_same, x_cross, y_cross, rest = pack_far(tile_table, panel_table, tok, sides, cap)
        y_same, rest = xor(y_same, 4), xor(rest, 1)
        edge_a, edge_b, edge_c, x_same, x_cross, y_cross = fence((edge_a, edge_b, edge_c, x_same, x_cross, y_cross))
        x_same = xor(x_same, 2)
        mix_far = window_mix(far_half, (edge_a, edge_b, edge_c), (0, 0, 0), q, kv, gain_row, w_qkv)
        x_cross, y_cross, mix_far = fence((x_cross, y_cross, mix_far))
        x_cross, y_cross = xor(x_cross, 3), xor(y_cross, 5)
        mixes = (mix_near, mix_far)
        early = (*sides, x_same, rest, y_same, rest, rest)
        late = (*sides, x_same, x_cross, y_same, y_cross, rest)
        out = cross(relay_parts, 0b01010111, early, mixes, near_half, None)
        out = cross(relay_parts, 0b10101000, late, mixes, near_half, out)
    else:
        forward = [(i, i + 1) for i in range(slab_count - 1)]
        backward = [(i + 1, i) for i in range(slab_count - 1)]
        before = lax.ppermute(tok[1], ("scene", "tile"), forward)
        after = lax.ppermute(tok[0], ("scene", "tile"), backward)
        outgoing = pack(tile_table, panel_table, tok, tiles, cap)
        recv = [xor(outgoing[r - 1], r) for r in range(1, tiles)]
        q, kv = project_own(tok, gain_row, w_qkv)
        zero = jnp.zeros((), jnp.int32)
        upper = jnp.stack([zero, keep_before])
        mix_up = window_mix(upper, (before, before), (0, 1), q, kv, gain_row, w_qkv)
        mix_down = window_mix(jnp.stack([zero + 1, keep_after]), (after, after), (0, 1), q, kv, gain_row, w_qkv)
        out = cross(direct_parts, (1 << tiles) - 1, recv, (mix_up, mix_down), upper, None)
    return out.reshape(tokens.shape)


def solution(mesh):
    in_specs = (
        P(("scene", "tile"), None, None, None),
        P(),
        P(),
        P(),
        P(),
        P(("scene", "tile"), None),
        P("scene", None, None, None),
        P("scene", None, None),
    )
    out_specs = P(("scene", "tile"), None, None, None)
    return jax.shard_map(per_device, mesh=mesh, in_specs=in_specs, out_specs=out_specs, check_vma=False)
```

```python
import functools

import jax
import jax.numpy as jnp
from jax import lax
from jax.experimental import pallas as pl
from jax.experimental.pallas import tpu as pltpu
from jax.sharding import PartitionSpec as P

HEADS = 16
NORM_EPS = 1e-05
LOG2E = 1.4426950408889634
VMEM_LIMIT = 63 * 1024 * 1024
GROUP = 4


def layer_norm(rows, gain_row):
    values = rows.astype(jnp.float32)
    centred = values - jnp.mean(values, axis=-1, keepdims=True)
    spread = jnp.mean(centred * centred, axis=-1, keepdims=True)
    return (centred * lax.rsqrt(spread + NORM_EPS) * gain_row.astype(jnp.float32)).astype(jnp.bfloat16)


def dot_f32(left, right):
    return jnp.dot(left, right, preferred_element_type=jnp.float32)


def dot_t(left, right):
    return lax.dot_general(left, right, (((1,), (1,)), ((), ())), preferred_element_type=jnp.float32)


def staged(count, first, second):
    held = first(0)
    for g in range(count):
        coming = first(g + 1) if g + 1 < count else None
        second(g, held)
        held = coming


def low_lanes(rows, width, head_width):
    return lax.broadcasted_iota(jnp.int32, (rows, width), 1) < head_width


def pack_kernel(tiles, panels, cap, tile_ref, panel_ref, tok_ref, *rest):
    outs, slab, sem, sems = rest[: tiles - 1], rest[tiles - 1], rest[tiles], rest[tiles + 1]
    me = lax.axis_index("tile")
    load = pltpu.make_async_copy(tok_ref, slab, sem)
    load.start()
    load.wait()
    counts = []
    for r in range(1, tiles):
        asker = me ^ r
        out = outs[r - 1]

        def body(p, count, asker=asker, out=out, r=r):
            hit = jnp.logical_and(tile_ref[0, asker, p] == me, count < cap)

            @pl.when(hit)
            def _():
                j = panel_ref[0, asker, p]
                pltpu.make_async_copy(
                    slab.at[j // (panels // 2), :, j % (panels // 2)], out.at[count], sems.at[r, count]
                ).start()

            return count + hit.astype(jnp.int32)

        counts.append(lax.fori_loop(0, panels, body, jnp.int32(0)))
    for r in range(1, tiles):
        for c in range(cap):

            @pl.when(c < counts[r - 1])
            def _(r=r, c=c):
                pltpu.make_async_copy(slab.at[0, :, 0], outs[r - 1].at[c], sems.at[r, c]).wait()


def pack(tile_table, panel_table, tok, tiles, cap):
    panels = 2 * tok.shape[2]
    block = (cap, tok.shape[1], tok.shape[3], tok.shape[4])
    smem = pl.BlockSpec(memory_space=pltpu.SMEM)
    anym = pl.BlockSpec(memory_space=pl.ANY)
    return pl.pallas_call(
        functools.partial(pack_kernel, tiles, panels, cap),
        out_shape=[jax.ShapeDtypeStruct(block, tok.dtype)] * (tiles - 1),
        in_specs=[smem, smem, anym],
        out_specs=[anym] * (tiles - 1),
        scratch_shapes=[
            pltpu.VMEM(tok.shape, tok.dtype),
            pltpu.SemaphoreType.DMA,
            pltpu.SemaphoreType.DMA((tiles, cap)),
        ],
        cost_estimate=pl.CostEstimate(flops=0, bytes_accessed=16 << 20, transcendentals=0),
    )(tile_table, panel_table, tok)


def copy_through(pairs, bounce, sems):
    loads = [pltpu.make_async_copy(src, bounce.at[k], sems.at[0, k]) for k, (src, _) in enumerate(pairs)]
    for load in loads:
        load.start()
    stores = []
    for k, (_, dst) in enumerate(pairs):
        loads[k].wait()
        store = pltpu.make_async_copy(bounce.at[k], dst, sems.at[1, k])
        store.start()
        stores.append(store)
    for store in stores:
        store.wait()


def halves_kernel(tok_ref, *rest):
    outs, bounce, sems = rest[:4], rest[4], rest[5]
    deep = outs[0].shape[0]
    part = lax.axis_index("tile") & 1
    sources = [
        tok_ref.at[part, :deep],
        tok_ref.at[part, deep:],
        tok_ref.at[1 - part, :deep],
        tok_ref.at[1 - part, deep:],
    ]
    copy_through(list(zip(sources, outs)), bounce, sems)


def split_halves(tok):
    halves, deep, wide, run, feat = tok.shape
    part = (deep // 2, wide, run, feat)
    anym = pl.BlockSpec(memory_space=pl.ANY)
    return pl.pallas_call(
        halves_kernel,
        out_shape=[jax.ShapeDtypeStruct(part, tok.dtype)] * 4,
        in_specs=[anym],
        out_specs=[anym] * 4,
        scratch_shapes=[pltpu.VMEM((4,) + part, tok.dtype), pltpu.SemaphoreType.DMA((2, 4))],
        cost_estimate=pl.CostEstimate(flops=0, bytes_accessed=8 << 20, transcendentals=0),
    )(tok)


def far_kernel(cap, tile_ref, panel_ref, tok_ref, *rest):
    sides, outs, stage, in_sems, out_sems = rest[:4], rest[4:9], *rest[9:]
    halves, deep, wide, run, feat = tok_ref.shape
    panels = halves * wide
    cut = deep // 2
    me = lax.axis_index("tile")
    part = me & 1

    def bring(cond, ref, k, spot):
        @pl.when(cond)
        def _():
            pltpu.make_async_copy(ref, stage.at[k, spot], in_sems.at[k, spot]).start()

    def bring_side(cond, axis, j, k, spot):
        aligned = j // wide == part
        bring(jnp.logical_and(cond, aligned), sides[axis].at[:, j % wide], k, spot)
        bring(jnp.logical_and(cond, jnp.logical_not(aligned)), sides[2 + axis].at[:, j % wide], k, spot)

    totals = []
    for k, (bits, relay) in enumerate(((2, 4), (4, 2), (3, 4), (5, 2))):
        asker = me ^ bits
        axis, rows = (1, slice(cut, deep)) if relay == 4 else (0, slice(0, cut))

        def body(p, count, k=k, asker=asker, relay=relay, axis=axis, rows=rows):
            named = tile_ref[0, asker, p]
            own = jnp.logical_and(named == me, count < 2 * cap)
            other = jnp.logical_and(named == me ^ relay, count < 2 * cap)
            j = panel_ref[0, asker, p]
            bring(own, tok_ref.at[j // wide, rows, j % wide], k, count)
            bring_side(other, axis, j, k, count)
            return count + jnp.logical_or(own, other).astype(jnp.int32)

        totals.append(lax.fori_loop(0, panels, body, jnp.int32(0)))

    def near(p, counts):
        named = tile_ref[0, me ^ 1, p]
        j = panel_ref[0, me ^ 1, p]
        hits = [jnp.logical_and(named == me ^ relay, counts[k] < cap) for k, relay in enumerate((2, 4, 0))]
        for k in range(2):
            bring_side(hits[k], k, j, 4, k * cap + counts[k])
        bring(hits[2], tok_ref.at[j // wide, :cut, j % wide], 4, 2 * cap + counts[2])
        bring(hits[2], tok_ref.at[j // wide, cut:, j % wide], 4, 3 * cap + counts[2])
        return tuple(count + hit.astype(jnp.int32) for count, hit in zip(counts, hits))

    near_totals = lax.fori_loop(0, panels, near, (jnp.int32(0),) * 3)
    used = []
    for k in range(4):
        used += [(k, c, c < totals[k]) for c in range(2 * cap)]
    used += [(4, c, c % cap < near_totals[min(c // cap, 2)]) for c in range(4 * cap)]
    for k, c, cond in used:

        @pl.when(cond)
        def _(k=k, c=c):
            pltpu.make_async_copy(sides[0].at[:, 0], stage.at[k, c], in_sems.at[k, c]).wait()
            pltpu.make_async_copy(stage.at[k, c], outs[k].at[c], out_sems.at[k, c]).start()

    for k, c, cond in used:

        @pl.when(cond)
        def _(k=k, c=c):
            pltpu.make_async_copy(stage.at[k, c], outs[k].at[c], out_sems.at[k, c]).wait()


def pack_far(tile_table, panel_table, tok, sides, cap):
    halves, deep, wide, run, feat = tok.shape
    smem = pl.BlockSpec(memory_space=pltpu.SMEM)
    anym = pl.BlockSpec(memory_space=pl.ANY)
    block = (2 * cap, deep // 2, run, feat)
    return pl.pallas_call(
        functools.partial(far_kernel, cap),
        out_shape=[jax.ShapeDtypeStruct(block, tok.dtype)] * 4
        + [jax.ShapeDtypeStruct((4 * cap,) + block[1:], tok.dtype)],
        in_specs=[smem, smem] + [anym] * 5,
        out_specs=[anym] * 5,
        scratch_shapes=[
            pltpu.VMEM((5, 4 * cap) + block[1:], tok.dtype),
            pltpu.SemaphoreType.DMA((5, 4 * cap)),
            pltpu.SemaphoreType.DMA((5, 4 * cap)),
        ],
        compiler_params=pltpu.CompilerParams(vmem_limit_bytes=VMEM_LIMIT),
        cost_estimate=pl.CostEstimate(flops=0, bytes_accessed=6 << 20, transcendentals=0),
    )(tile_table, panel_table, tok, *sides)


def qkv_kernel(tok_ref, gain_ref, w_ref, q_ref, kv_ref):
    dims = tok_ref.shape
    feat = dims[-1]
    rows = dims[1] * dims[2] * dims[3]
    normed = layer_norm(tok_ref[...].reshape(rows, feat), gain_ref[...])
    q_ref[...] = dot_f32(normed, w_ref[:, :feat]).astype(jnp.bfloat16).reshape(q_ref.shape)
    kv_ref[...] = dot_f32(normed, w_ref[:, feat:]).astype(jnp.bfloat16).reshape(kv_ref.shape)


def project_own(tok, gain_row, w_qkv):
    halves, deep, wide, run, feat = tok.shape
    step = deep // 2
    spec = lambda width: pl.BlockSpec((1, step, wide, run, width), lambda i: (i // 2, i % 2, 0, 0, 0))
    tokens = halves * deep * wide * run
    return pl.pallas_call(
        qkv_kernel,
        grid=(halves * 2,),
        out_shape=[
            jax.ShapeDtypeStruct((halves, deep, wide, run, feat), jnp.bfloat16),
            jax.ShapeDtypeStruct((halves, deep, wide, run, 2 * feat), jnp.bfloat16),
        ],
        in_specs=[
            spec(feat),
            pl.BlockSpec((feat,), lambda i: (0,)),
            pl.BlockSpec((feat, 3 * feat), lambda i: (0, 0), pipeline_mode=pl.Buffered(1)),
        ],
        out_specs=[spec(feat), spec(2 * feat)],
        compiler_params=pltpu.CompilerParams(vmem_limit_bytes=VMEM_LIMIT),
        cost_estimate=pl.CostEstimate(
            flops=2 * tokens * feat * 3 * feat, bytes_accessed=tokens * feat * 8 + feat * feat * 6, transcendentals=0
        ),
    )(tok, gain_row, w_qkv)


def window_kernel(head_width, half_ref, *refs):
    edges, (q_ref, kvo_ref, gain_ref, w_ref, mix_ref, kv_s) = refs[:-6], refs[-6:]
    deep, group, run, feat = mix_ref.shape
    length = deep * run
    bottom = edges[1][...]
    if len(edges) == 3:
        bottom = jnp.where(half_ref[2] == 1, bottom, edges[2][...])
    rows = jnp.concatenate([edges[0][...], bottom], axis=0).reshape(deep * group * run, feat)
    normed = layer_norm(rows, gain_ref[...])
    kv_s[...] = dot_f32(normed, w_ref[:, feat:]).astype(jnp.bfloat16).reshape(kv_s.shape)
    pair = 2 * head_width
    scale = LOG2E * head_width ** (-0.5)
    bias = jnp.where(
        jnp.logical_and(half_ref[1] == 0, lax.broadcasted_iota(jnp.int32, (1, 2 * length), 1) < length), -jnp.inf, 0.0
    )
    low = low_lanes(length, pair, head_width)
    ones = jnp.ones((2 * length, pair), jnp.bfloat16)
    zero = jnp.zeros((length, pair), jnp.bfloat16)
    def panel(i, carry):
        def score(g):
            at = slice(g * pair, (g + 1) * pair)
            q = q_ref[0, :, i, :, at].reshape(length, pair)
            qs = jnp.concatenate([jnp.where(low, q, zero), jnp.where(low, zero, q)], axis=0)
            keys = jnp.concatenate(
                [kv_s[:, i, :, at].reshape(length, pair), kvo_ref[0, :, i, :, at].reshape(length, pair)], axis=0
            )
            return dot_t(qs, keys) + bias

        def mix(g, scores):
            at_v = slice(feat + g * pair, feat + (g + 1) * pair)
            vals = jnp.concatenate(
                [kv_s[:, i, :, at_v].reshape(length, pair), kvo_ref[0, :, i, :, at_v].reshape(length, pair)], axis=0
            )
            peak = jnp.max(scores, axis=1, keepdims=True)
            weights = jnp.exp2((scores - peak) * scale).astype(jnp.bfloat16)
            both = dot_f32(weights, jnp.concatenate([vals, ones], axis=1))
            mixed = both[:, :pair] / both[:, pair:]
            out = jnp.where(low, mixed[:length], mixed[length:])
            mix_ref[:, i, :, g * pair : (g + 1) * pair] = out.astype(jnp.bfloat16).reshape(deep, run, pair)

        staged(feat // pair, score, mix)
        return carry

    lax.fori_loop(0, group, panel, 0)


def window_mix(half_keep, edges, spots, q, kv_own, gain_row, w_qkv):
    _, deep, wide, run, feat = q.shape
    group = min(GROUP, wide)
    head_width = feat // HEADS
    own = lambda width: pl.BlockSpec((1, deep, group, run, width), lambda i, hk: (hk[0], 0, i, 0, 0))
    side = lambda spot: pl.BlockSpec((deep // 2, group, run, feat), lambda i, hk: (spot, i, 0, 0))
    flat = pl.BlockSpec((deep, group, run, feat), lambda i, hk: (0, i, 0, 0))
    tokens = deep * wide * run
    return pl.pallas_call(
        functools.partial(window_kernel, head_width),
        out_shape=jax.ShapeDtypeStruct((deep, wide, run, feat), jnp.bfloat16),
        grid_spec=pltpu.PrefetchScalarGridSpec(
            num_scalar_prefetch=1,
            grid=(wide // group,),
            in_specs=[
                *[side(spot) for spot in spots],
                own(feat),
                own(2 * feat),
                pl.BlockSpec((feat,), lambda i, hk: (0,)),
                pl.BlockSpec((feat, 3 * feat), lambda i, hk: (0, 0), pipeline_mode=pl.Buffered(1)),
            ],
            out_specs=flat,
            scratch_shapes=[pltpu.VMEM((deep, group, run, 2 * feat), jnp.bfloat16)],
        ),
        compiler_params=pltpu.CompilerParams(vmem_limit_bytes=VMEM_LIMIT),
        cost_estimate=pl.CostEstimate(
            flops=2 * tokens * feat * 2 * feat + 8 * tokens * 256 * feat,
            bytes_accessed=tokens * feat * 10 + feat * feat * 6,
            transcendentals=tokens * 256 * HEADS,
        ),
    )(half_keep, *edges, q, kv_own, gain_row, w_qkv)


def direct_parts(recv, tok_ref, tiles, wanted, cap):
    cut = tok_ref.shape[1] // 2
    wide = tok_ref.shape[2]

    def own(j, seen):
        return tok_ref.at[j // wide, :cut, j % wide], tok_ref.at[j // wide, cut:, j % wide]

    def other(r):
        return lambda j, seen: (recv[r - 1].at[seen[r], :cut], recv[r - 1].at[seen[r], cut:])

    return {r: own if r == 0 else other(r) for r in range(tiles) if (wanted >> r) & 1}


def relay_parts(recv, tok_ref, tiles, wanted, cap):
    whole, x_same, x_cross, y_same, y_cross, rest = recv[:4], *recv[4:]
    cut = tok_ref.shape[1] // 2
    wide = tok_ref.shape[2]
    same = lambda k, j: [(True, whole[k].at[:, j % wide]), (False, whole[k + 2].at[:, j % wide])]
    table = {
        0: lambda j, seen: (tok_ref.at[j // wide, :cut, j % wide], tok_ref.at[j // wide, cut:, j % wide]),
        1: lambda j, seen: (rest.at[2 * cap + seen[1]], rest.at[3 * cap + seen[1]]),
        2: lambda j, seen: (same(0, j), x_same.at[seen[2] + seen[6]]),
        3: lambda j, seen: (rest.at[seen[3]], x_cross.at[seen[3] + seen[7]]),
        4: lambda j, seen: (y_same.at[seen[4] + seen[6]], same(1, j)),
        5: lambda j, seen: (y_cross.at[seen[5] + seen[7]], rest.at[cap + seen[5]]),
        6: lambda j, seen: (y_same.at[seen[4] + seen[6]], x_same.at[seen[2] + seen[6]]),
        7: lambda j, seen: (y_cross.at[seen[5] + seen[7]], x_cross.at[seen[3] + seen[7]]),
    }
    return {r: table[r] for r in range(tiles) if (wanted >> r) & 1}


def cross_kernel(plan, tiles, head_width, wanted, recv_count, cap, refs):
    tile_ref, panel_ref, valid_ref, half_ref, tok_ref = refs[:5]
    recv = refs[5 : 5 + recv_count]
    q_ref, mix_a, mix_b, gain_ref, wqkv_ref, wproj_ref = refs[5 + recv_count : 11 + recv_count]
    out_ref, got, q_s, own_s, res_s, wkv_s, wp_s, normed_s, kv_s, mixed_s, seen, ids, w_sem, sems = refs[-14:]
    panels, deep, run, feat = got.shape
    half = panels // 2
    cut = deep // 2
    length = deep * run
    me = lax.axis_index("tile")
    parts = plan(recv, tok_ref, tiles, wanted, cap)
    for t in range(tiles):
        seen[t] = 0

    def fetch(p, count):
        r = tile_ref[0, me, p] ^ me
        hit = ((wanted >> r) & 1) == 1

        @pl.when(hit)
        def _():
            ids[count] = p
            j = panel_ref[0, me, p]
            for k, pick in parts.items():

                @pl.when(r == k)
                def _(pick=pick):
                    for ref, rows, k in zip(pick(j, seen), (slice(0, cut), slice(cut, deep)), (0, 4)):
                        if not isinstance(ref, list):
                            pltpu.make_async_copy(ref, got.at[count, rows], sems.at[k, count]).start()
                            continue
                        for mine, choice in ref:

                            @pl.when((j // half == (me & 1)) == mine)
                            def _(choice=choice, rows=rows, k=k):
                                pltpu.make_async_copy(choice, got.at[count, rows], sems.at[k, count]).start()

            u = p // half
            w = p % half
            pltpu.make_async_copy(q_ref.at[u, :, w], q_s.at[count], sems.at[1, count]).start()

            @pl.when(u == half_ref[0])
            def _():
                pltpu.make_async_copy(mix_a.at[:, w], own_s.at[count], sems.at[2, count]).start()

            @pl.when(u != half_ref[0])
            def _():
                pltpu.make_async_copy(mix_b.at[:, w], own_s.at[count], sems.at[2, count]).start()

        seen[r] = seen[r] + 1
        return count + hit.astype(jnp.int32)

    load_wkv = pltpu.make_async_copy(wqkv_ref.at[:, feat:], wkv_s, w_sem.at[0])
    load_wp = pltpu.make_async_copy(wproj_ref, wp_s, w_sem.at[1])
    load_wkv.start()
    total = lax.fori_loop(0, panels, fetch, jnp.int32(0))
    load_wp.start()

    pair = 2 * head_width
    scale = LOG2E * head_width ** (-0.5)
    low = low_lanes(length, pair, head_width)
    zero = jnp.zeros((length, pair), jnp.bfloat16)
    one = jnp.ones((length, pair), jnp.bfloat16)
    marks = jnp.concatenate([jnp.where(low, one, zero), jnp.where(low, zero, one)], axis=0)
    pairs = feat // pair

    def unit(n, carry):
        first = 2 * n
        for i in range(2):

            @pl.when(first + i < total)
            def _(i=i):
                n_i = first + i
                for k, place in ((0, got.at[n_i, :cut]), (4, got.at[n_i, cut:])):
                    pltpu.make_async_copy(tok_ref.at[0, :cut, 0], place, sems.at[k, n_i]).wait()
                for k, place in ((1, q_s.at[n_i]), (2, own_s.at[n_i])):
                    pltpu.make_async_copy(tok_ref.at[0, :, 0], place, sems.at[k, n_i]).wait()

        rows = got[pl.ds(first, 2)].reshape(2 * length, feat)
        normed_s[...] = layer_norm(rows, gain_ref[...])

        @pl.when(n == 0)
        def _():
            load_wkv.wait()

        kv_s[...] = dot_f32(normed_s[...], wkv_s[...]).astype(jnp.bfloat16)

        @pl.when(n == 0)
        def _():
            load_wp.wait()

        gates = [valid_ref[ids[jnp.minimum(first + i, total - 1)]].astype(jnp.float32) for i in range(2)]

        def score(t):
            i, g = t // pairs, t % pairs
            at = slice(g * pair, (g + 1) * pair)
            q = q_s[first + i, :, :, at].reshape(length, pair)
            key = kv_s[i * length : (i + 1) * length, at]
            keys = jnp.concatenate([jnp.where(low, key, zero), jnp.where(low, zero, key)], axis=0)
            return dot_t(q, keys)

        def mix(t, scores):
            i, g = t // pairs, t % pairs
            at = slice(g * pair, (g + 1) * pair)
            val = kv_s[i * length : (i + 1) * length, feat + g * pair : feat + (g + 1) * pair]
            vals = jnp.concatenate([jnp.where(low, val, zero), jnp.where(low, zero, val)], axis=0)
            parts = []
            for h in range(2):
                part = scores[:, h * length : (h + 1) * length]
                peak = jnp.max(part, axis=1, keepdims=True)
                parts.append(jnp.exp2((part - peak) * scale).astype(jnp.bfloat16))
            both = dot_f32(jnp.concatenate(parts, axis=1), jnp.concatenate([vals, marks], axis=1))
            cross = (both[:, :pair] / both[:, pair:]).astype(jnp.bfloat16)
            own = own_s[first + i, :, :, at].reshape(length, pair)
            blended = gates[i] * own.astype(jnp.float32) + cross.astype(jnp.float32)
            mixed_s[i * length : (i + 1) * length, at] = blended.astype(jnp.bfloat16)

        staged(2 * pairs, score, mix)
        res_s[pl.ds(first, 2)] = dot_f32(mixed_s[...], wp_s[...]).astype(jnp.bfloat16).reshape(2, deep, run, feat)
        for i in range(2):

            @pl.when(first + i < total)
            def _(i=i):
                p = ids[first + i]
                pltpu.make_async_copy(
                    res_s.at[first + i], out_ref.at[p // half, :, p % half], sems.at[3, first + i]
                ).start()

        return carry

    lax.fori_loop(0, (total + 1) // 2, unit, 0)

    @pl.when(total == 0)
    def _():
        load_wkv.wait()
        load_wp.wait()

    def finish(n, carry):
        pltpu.make_async_copy(res_s.at[n], out_ref.at[0, :, 0], sems.at[3, n]).wait()
        return carry

    lax.fori_loop(0, total, finish, 0)


def cross_and_project(
    plan, wanted, tiles, cap, tile_table, panel_table, valid, half_keep, tok, recv, q, mixes, gain_row, w_qkv, w_proj, earlier
):
    halves, deep, wide, run, feat = tok.shape
    panels = halves * wide
    head_width = feat // HEADS
    length = deep * run
    smem = pl.BlockSpec(memory_space=pltpu.SMEM)
    anym = pl.BlockSpec(memory_space=pl.ANY)
    share = bin(wanted).count("1") / tiles
    tokens = int(panels * length * share)
    many = pltpu.VMEM((panels, deep, run, feat), jnp.bfloat16)
    operands = [tile_table, panel_table, valid, half_keep, tok, *recv, q, *mixes, gain_row, w_qkv, w_proj]
    specs = [smem] * 4 + [anym] * (len(recv) + 4) + [pl.BlockSpec((feat,), lambda: (0,))] + [anym] * 2
    aliases = {}
    if earlier is not None:
        aliases = {len(operands): 0}
        operands.append(earlier)
        specs.append(anym)

    def kernel(*refs):
        cross_kernel(plan, tiles, head_width, wanted, len(recv), cap, refs)

    return pl.pallas_call(
        kernel,
        out_shape=jax.ShapeDtypeStruct(tok.shape, jnp.bfloat16),
        in_specs=specs,
        out_specs=anym,
        scratch_shapes=[
            many,
            many,
            many,
            many,
            pltpu.VMEM((feat, 2 * feat), jnp.bfloat16),
            pltpu.VMEM((feat, feat), jnp.bfloat16),
            pltpu.VMEM((2 * length, feat), jnp.bfloat16),
            pltpu.VMEM((2 * length, 2 * feat), jnp.bfloat16),
            pltpu.VMEM((2 * length, feat), jnp.bfloat16),
            pltpu.SMEM((tiles,), jnp.int32),
            pltpu.SMEM((panels,), jnp.int32),
            pltpu.SemaphoreType.DMA((2,)),
            pltpu.SemaphoreType.DMA((5, panels)),
        ],
        input_output_aliases=aliases,
        compiler_params=pltpu.CompilerParams(vmem_limit_bytes=VMEM_LIMIT),
        cost_estimate=pl.CostEstimate(
            flops=2 * tokens * feat * 3 * feat + 8 * tokens * 128 * feat,
            bytes_accessed=tokens * feat * 8 + feat * feat * 6,
            transcendentals=tokens * 128 * HEADS,
        ),
    )(*operands)


def per_device(tokens, gain, w_qkv, w_proj, scene_first, window_valid, partner_tile, partner_panel):
    _, tok_rows, tok_cols, feat = tokens.shape
    run = 16
    wide = tok_cols // run
    tok = tokens.reshape(2, tok_rows // 2, wide, run, feat)
    tiles = partner_tile.shape[1]
    panels = partner_tile.shape[2]
    cap = 2 * max(1, panels // tiles)
    slab_count = scene_first.shape[0]
    tile_table = partner_tile[:, :, :, 0]
    panel_table = partner_panel
    valid = window_valid.reshape(panels)
    gain_row = gain
    slab_index = lax.axis_index(("scene", "tile"))
    after_index = jnp.minimum(slab_index + 1, slab_count - 1)
    own_first = jnp.logical_or(scene_first[slab_index] == 1, slab_index == 0)
    next_first = jnp.logical_or(scene_first[after_index] == 1, slab_index + 1 >= slab_count)
    keep_before = jnp.logical_not(own_first).astype(jnp.int32)
    keep_after = jnp.logical_not(next_first).astype(jnp.int32)

    def xor(block, bits):
        return lax.ppermute(block, "tile", [(i, i ^ bits) for i in range(tiles)])

    def cross(plan, wanted, recv, mixes, half_keep, earlier):
        return cross_and_project(
            plan,
            wanted,
            tiles,
            cap,
            tile_table,
            panel_table,
            valid,
            half_keep,
            tok,
            recv,
            q,
            mixes,
            gain_row,
            w_qkv,
            w_proj,
            earlier,
        )

    if tiles == 8:
        fence = lax.optimization_barrier
        odd = slab_index % 2
        direct = jnp.logical_or(slab_index % 4 == 1, slab_index % 4 == 2).astype(jnp.int32)
        near_half = jnp.stack([1 - odd, jnp.where(odd == 1, keep_before, keep_after), direct]).astype(jnp.int32)
        far_half = jnp.stack([odd, jnp.where(odd == 1, keep_after, keep_before), direct]).astype(jnp.int32)
        near_half, far_half = fence((near_half, far_half))
        links_a, links_b, links_c = [], [], []
        for low in range(1, slab_count - 1, 2):
            links_a += [(low ^ 2, low + 1), ((low + 1) ^ 2, low)]
            if low % 4 == 1:
                links_b += [(low, low + 1), (low + 1, low)]
            else:
                links_c += [(low ^ 4, low + 1), ((low + 1) ^ 4, low)]

        rim_x, rim_y, off_x, off_y = split_halves(tok)
        rim_x, rim_y, off_x, off_y, gain_next = fence((rim_x, rim_y, off_x, off_y, gain_row))
        near = (xor(off_x, 1), xor(off_y, 1))
        own_rim = rim_y
        rim_x, rim_y = xor(rim_x, 2), xor(rim_y, 4)
        off_x, off_y = xor(off_x, 2), xor(off_y, 4)
        q, kv = project_own(tok, gain_next, w_qkv)
        edge_b = lax.ppermute(own_rim, ("scene", "tile"), links_b)
        mix_near = window_mix(near_half, near, (0, 0), q, kv, gain_row, w_qkv)
        rim_x, rim_y, mix_near = fence((rim_x, rim_y, mix_near))
        edge_c = lax.ppermute(rim_y, ("scene", "tile"), links_c)
        edge_a = lax.ppermute(rim_x, ("scene", "tile"), links_a)
        sides = (rim_x, rim_y, off_x, off_y)
        x_same, y_same, x_cross, y_cross, rest = pack_far(tile_table, panel_table, tok, sides, cap)
        y_same, rest = xor(y_same, 4), xor(rest, 1)
        edge_a, edge_b, edge_c, x_same, x_cross, y_cross = fence((edge_a, edge_b, edge_c, x_same, x_cross, y_cross))
        x_same = xor(x_same, 2)
        mix_far = window_mix(far_half, (edge_a, edge_b, edge_c), (0, 0, 0), q, kv, gain_row, w_qkv)
        x_cross, y_cross, mix_far = fence((x_cross, y_cross, mix_far))
        x_cross, y_cross = xor(x_cross, 3), xor(y_cross, 5)
        mixes = (mix_near, mix_far)
        early = (*sides, x_same, rest, y_same, rest, rest)
        late = (*sides, x_same, x_cross, y_same, y_cross, rest)
        out = cross(relay_parts, 0b01010111, early, mixes, near_half, None)
        out = cross(relay_parts, 0b10101000, late, mixes, near_half, out)
    else:
        forward = [(i, i + 1) for i in range(slab_count - 1)]
        backward = [(i + 1, i) for i in range(slab_count - 1)]
        before = lax.ppermute(tok[1], ("scene", "tile"), forward)
        after = lax.ppermute(tok[0], ("scene", "tile"), backward)
        outgoing = pack(tile_table, panel_table, tok, tiles, cap)
        recv = [xor(outgoing[r - 1], r) for r in range(1, tiles)]
        q, kv = project_own(tok, gain_row, w_qkv)
        zero = jnp.zeros((), jnp.int32)
        upper = jnp.stack([zero, keep_before])
        mix_up = window_mix(upper, (before, before), (0, 1), q, kv, gain_row, w_qkv)
        mix_down = window_mix(jnp.stack([zero + 1, keep_after]), (after, after), (0, 1), q, kv, gain_row, w_qkv)
        out = cross(direct_parts, (1 << tiles) - 1, recv, (mix_up, mix_down), upper, None)
    return out.reshape(tokens.shape)


def solution(mesh):
    in_specs = (
        P(("scene", "tile"), None, None, None),
        P(),
        P(),
        P(),
        P(),
        P(("scene", "tile"), None),
        P("scene", None, None, None),
        P("scene", None, None),
    )
    out_specs = P(("scene", "tile"), None, None, None)
    return jax.shard_map(per_device, mesh=mesh, in_specs=in_specs, out_specs=out_specs, check_vma=False)
```

```python
import functools

import jax
import jax.numpy as jnp
from jax import lax
from jax.experimental import pallas as pl
from jax.experimental.pallas import tpu as pltpu
from jax.sharding import PartitionSpec as P

HEADS = 16
NORM_EPS = 1e-05
LOG2E = 1.4426950408889634
VMEM_LIMIT = 63 * 1024 * 1024
GROUP = 4


def layer_norm(rows, gain_row):
    values = rows.astype(jnp.float32)
    centred = values - jnp.mean(values, axis=-1, keepdims=True)
    spread = jnp.mean(centred * centred, axis=-1, keepdims=True)
    return (centred * lax.rsqrt(spread + NORM_EPS) * gain_row.astype(jnp.float32)).astype(jnp.bfloat16)


def dot_f32(left, right):
    return jnp.dot(left, right, preferred_element_type=jnp.float32)


def dot_t(left, right):
    return lax.dot_general(left, right, (((1,), (1,)), ((), ())), preferred_element_type=jnp.float32)


def staged(count, first, second):
    held = first(0)
    for g in range(count):
        coming = first(g + 1) if g + 1 < count else None
        second(g, held)
        held = coming


def low_lanes(rows, width, head_width):
    return lax.broadcasted_iota(jnp.int32, (rows, width), 1) < head_width


def pack_kernel(tiles, panels, cap, tile_ref, panel_ref, tok_ref, *rest):
    outs, slab, sem, sems = rest[: tiles - 1], rest[tiles - 1], rest[tiles], rest[tiles + 1]
    me = lax.axis_index("tile")
    load = pltpu.make_async_copy(tok_ref, slab, sem)
    load.start()
    load.wait()
    counts = []
    for r in range(1, tiles):
        asker = me ^ r
        out = outs[r - 1]

        def body(p, count, asker=asker, out=out, r=r):
            hit = jnp.logical_and(tile_ref[0, asker, p] == me, count < cap)

            @pl.when(hit)
            def _():
                j = panel_ref[0, asker, p]
                pltpu.make_async_copy(
                    slab.at[j // (panels // 2), :, j % (panels // 2)], out.at[count], sems.at[r, count]
                ).start()

            return count + hit.astype(jnp.int32)

        counts.append(lax.fori_loop(0, panels, body, jnp.int32(0)))
    for r in range(1, tiles):
        for c in range(cap):

            @pl.when(c < counts[r - 1])
            def _(r=r, c=c):
                pltpu.make_async_copy(slab.at[0, :, 0], outs[r - 1].at[c], sems.at[r, c]).wait()


def pack(tile_table, panel_table, tok, tiles, cap):
    panels = 2 * tok.shape[2]
    block = (cap, tok.shape[1], tok.shape[3], tok.shape[4])
    smem = pl.BlockSpec(memory_space=pltpu.SMEM)
    anym = pl.BlockSpec(memory_space=pl.ANY)
    return pl.pallas_call(
        functools.partial(pack_kernel, tiles, panels, cap),
        out_shape=[jax.ShapeDtypeStruct(block, tok.dtype)] * (tiles - 1),
        in_specs=[smem, smem, anym],
        out_specs=[anym] * (tiles - 1),
        scratch_shapes=[
            pltpu.VMEM(tok.shape, tok.dtype),
            pltpu.SemaphoreType.DMA,
            pltpu.SemaphoreType.DMA((tiles, cap)),
        ],
        cost_estimate=pl.CostEstimate(flops=0, bytes_accessed=16 << 20, transcendentals=0),
    )(tile_table, panel_table, tok)


def copy_through(pairs, bounce, sems):
    loads = [pltpu.make_async_copy(src, bounce.at[k], sems.at[0, k]) for k, (src, _) in enumerate(pairs)]
    for load in loads:
        load.start()
    stores = []
    for k, (_, dst) in enumerate(pairs):
        loads[k].wait()
        store = pltpu.make_async_copy(bounce.at[k], dst, sems.at[1, k])
        store.start()
        stores.append(store)
    for store in stores:
        store.wait()


def halves_kernel(start, tok_ref, rim_ref, off_ref, bounce, sems):
    deep = rim_ref.shape[0]
    part = lax.axis_index("tile") & 1
    bite = deep // 2
    pairs = []
    for u, out in ((1 - part, off_ref), (part, rim_ref)):
        for k in range(0, deep, bite):
            pairs.append((tok_ref.at[u, start + k : start + k + bite], out.at[k : k + bite]))
    copy_through(pairs, bounce, sems)


def split_half(start, tok):
    halves, deep, wide, run, feat = tok.shape
    part = (deep // 2, wide, run, feat)
    anym = pl.BlockSpec(memory_space=pl.ANY)
    return pl.pallas_call(
        functools.partial(halves_kernel, start),
        out_shape=[jax.ShapeDtypeStruct(part, tok.dtype)] * 2,
        in_specs=[anym],
        out_specs=[anym] * 2,
        scratch_shapes=[pltpu.VMEM((4, part[0] // 2) + part[1:], tok.dtype), pltpu.SemaphoreType.DMA((2, 4))],
        cost_estimate=pl.CostEstimate(flops=0, bytes_accessed=8 << 20, transcendentals=0),
    )(tok)


def far_kernel(cap, tile_ref, panel_ref, tok_ref, *rest):
    sides, outs, stage, in_sems, out_sems = rest[:4], rest[4:9], *rest[9:]
    halves, deep, wide, run, feat = tok_ref.shape
    panels = halves * wide
    cut = deep // 2
    me = lax.axis_index("tile")
    part = me & 1

    def bring(cond, ref, k, spot):
        @pl.when(cond)
        def _():
            pltpu.make_async_copy(ref, stage.at[k, spot], in_sems.at[k, spot]).start()

    def bring_side(cond, axis, j, k, spot):
        aligned = j // wide == part
        bring(jnp.logical_and(cond, aligned), sides[axis].at[:, j % wide], k, spot)
        bring(jnp.logical_and(cond, jnp.logical_not(aligned)), sides[2 + axis].at[:, j % wide], k, spot)

    totals = []
    for k, (bits, relay) in enumerate(((2, 4), (4, 2), (3, 4), (5, 2))):
        asker = me ^ bits
        axis, rows = (1, slice(cut, deep)) if relay == 4 else (0, slice(0, cut))

        def body(p, count, k=k, asker=asker, relay=relay, axis=axis, rows=rows):
            named = tile_ref[0, asker, p]
            own = jnp.logical_and(named == me, count < 2 * cap)
            other = jnp.logical_and(named == me ^ relay, count < 2 * cap)
            j = panel_ref[0, asker, p]
            bring(own, tok_ref.at[j // wide, rows, j % wide], k, count)
            bring_side(other, axis, j, k, count)
            return count + jnp.logical_or(own, other).astype(jnp.int32)

        totals.append(lax.fori_loop(0, panels, body, jnp.int32(0)))

    def near(p, counts):
        named = tile_ref[0, me ^ 1, p]
        j = panel_ref[0, me ^ 1, p]
        hits = [jnp.logical_and(named == me ^ relay, counts[k] < cap) for k, relay in enumerate((2, 4, 0))]
        for k in range(2):
            bring_side(hits[k], k, j, 4, k * cap + counts[k])
        bring(hits[2], tok_ref.at[j // wide, :cut, j % wide], 4, 2 * cap + counts[2])
        bring(hits[2], tok_ref.at[j // wide, cut:, j % wide], 4, 3 * cap + counts[2])
        return tuple(count + hit.astype(jnp.int32) for count, hit in zip(counts, hits))

    near_totals = lax.fori_loop(0, panels, near, (jnp.int32(0),) * 3)
    used = []
    for k in range(4):
        used += [(k, c, c < totals[k]) for c in range(2 * cap)]
    used += [(4, c, c % cap < near_totals[min(c // cap, 2)]) for c in range(4 * cap)]
    for k, c, cond in used:

        @pl.when(cond)
        def _(k=k, c=c):
            pltpu.make_async_copy(sides[0].at[:, 0], stage.at[k, c], in_sems.at[k, c]).wait()
            pltpu.make_async_copy(stage.at[k, c], outs[k].at[c], out_sems.at[k, c]).start()

    for k, c, cond in used:

        @pl.when(cond)
        def _(k=k, c=c):
            pltpu.make_async_copy(stage.at[k, c], outs[k].at[c], out_sems.at[k, c]).wait()


def pack_far(tile_table, panel_table, tok, sides, cap):
    halves, deep, wide, run, feat = tok.shape
    smem = pl.BlockSpec(memory_space=pltpu.SMEM)
    anym = pl.BlockSpec(memory_space=pl.ANY)
    block = (2 * cap, deep // 2, run, feat)
    return pl.pallas_call(
        functools.partial(far_kernel, cap),
        out_shape=[jax.ShapeDtypeStruct(block, tok.dtype)] * 4
        + [jax.ShapeDtypeStruct((4 * cap,) + block[1:], tok.dtype)],
        in_specs=[smem, smem] + [anym] * 5,
        out_specs=[anym] * 5,
        scratch_shapes=[
            pltpu.VMEM((5, 4 * cap) + block[1:], tok.dtype),
            pltpu.SemaphoreType.DMA((5, 4 * cap)),
            pltpu.SemaphoreType.DMA((5, 4 * cap)),
        ],
        compiler_params=pltpu.CompilerParams(vmem_limit_bytes=VMEM_LIMIT),
        cost_estimate=pl.CostEstimate(flops=0, bytes_accessed=6 << 20, transcendentals=0),
    )(tile_table, panel_table, tok, *sides)


def qkv_kernel(tok_ref, gain_ref, w_ref, q_ref, kv_ref):
    dims = tok_ref.shape
    feat = dims[-1]
    rows = dims[1] * dims[2] * dims[3]
    normed = layer_norm(tok_ref[...].reshape(rows, feat), gain_ref[...])
    q_ref[...] = dot_f32(normed, w_ref[:, :feat]).astype(jnp.bfloat16).reshape(q_ref.shape)
    kv_ref[...] = dot_f32(normed, w_ref[:, feat:]).astype(jnp.bfloat16).reshape(kv_ref.shape)


def project_own(tok, gain_row, w_qkv):
    halves, deep, wide, run, feat = tok.shape
    step = deep // 2
    spec = lambda width: pl.BlockSpec((1, step, wide, run, width), lambda i: (i // 2, i % 2, 0, 0, 0))
    tokens = halves * deep * wide * run
    return pl.pallas_call(
        qkv_kernel,
        grid=(halves * 2,),
        out_shape=[
            jax.ShapeDtypeStruct((halves, deep, wide, run, feat), jnp.bfloat16),
            jax.ShapeDtypeStruct((halves, deep, wide, run, 2 * feat), jnp.bfloat16),
        ],
        in_specs=[
            spec(feat),
            pl.BlockSpec((feat,), lambda i: (0,)),
            pl.BlockSpec((feat, 3 * feat), lambda i: (0, 0), pipeline_mode=pl.Buffered(1)),
        ],
        out_specs=[spec(feat), spec(2 * feat)],
        compiler_params=pltpu.CompilerParams(vmem_limit_bytes=VMEM_LIMIT),
        cost_estimate=pl.CostEstimate(
            flops=2 * tokens * feat * 3 * feat, bytes_accessed=tokens * feat * 8 + feat * feat * 6, transcendentals=0
        ),
    )(tok, gain_row, w_qkv)


def window_kernel(head_width, half_ref, *refs):
    edges, (q_ref, kvo_ref, gain_ref, wk_ref, wv_ref, mix_ref, kv_s) = refs[:-7], refs[-7:]
    deep, group, run, feat = mix_ref.shape
    length = deep * run
    bottom = edges[1][...]
    if len(edges) == 3:
        bottom = jnp.where(half_ref[2] == 1, bottom, edges[2][...])
    rows = jnp.concatenate([edges[0][...], bottom], axis=0).reshape(deep * group * run, feat)
    normed = layer_norm(rows, gain_ref[...])
    half_shape = kv_s.shape[:-1] + (feat,)
    kv_s[..., :feat] = dot_f32(normed, wk_ref[...]).astype(jnp.bfloat16).reshape(half_shape)
    kv_s[..., feat:] = dot_f32(normed, wv_ref[...]).astype(jnp.bfloat16).reshape(half_shape)
    pair = 2 * head_width
    scale = LOG2E * head_width ** (-0.5)
    bias = jnp.where(
        jnp.logical_and(half_ref[1] == 0, lax.broadcasted_iota(jnp.int32, (1, 2 * length), 1) < length), -jnp.inf, 0.0
    )
    low = low_lanes(length, pair, head_width)
    ones = jnp.ones((2 * length, pair), jnp.bfloat16)
    zero = jnp.zeros((length, pair), jnp.bfloat16)
    def panel(i, carry):
        def score(g):
            at = slice(g * pair, (g + 1) * pair)
            q = q_ref[0, :, i, :, at].reshape(length, pair)
            qs = jnp.concatenate([jnp.where(low, q, zero), jnp.where(low, zero, q)], axis=0)
            keys = jnp.concatenate(
                [kv_s[:, i, :, at].reshape(length, pair), kvo_ref[0, :, i, :, at].reshape(length, pair)], axis=0
            )
            return dot_t(qs, keys) + bias

        def mix(g, scores):
            at_v = slice(feat + g * pair, feat + (g + 1) * pair)
            vals = jnp.concatenate(
                [kv_s[:, i, :, at_v].reshape(length, pair), kvo_ref[0, :, i, :, at_v].reshape(length, pair)], axis=0
            )
            peak = jnp.max(scores, axis=1, keepdims=True)
            weights = jnp.exp2((scores - peak) * scale).astype(jnp.bfloat16)
            both = dot_f32(weights, jnp.concatenate([vals, ones], axis=1))
            mixed = both[:, :pair] / both[:, pair:]
            out = jnp.where(low, mixed[:length], mixed[length:])
            mix_ref[:, i, :, g * pair : (g + 1) * pair] = out.astype(jnp.bfloat16).reshape(deep, run, pair)

        staged(feat // pair, score, mix)
        return carry

    lax.fori_loop(0, group, panel, 0)


def window_mix(half_keep, edges, spots, q, kv_own, gain_row, w_qkv):
    _, deep, wide, run, feat = q.shape
    group = min(GROUP, wide)
    head_width = feat // HEADS
    own = lambda width: pl.BlockSpec((1, deep, group, run, width), lambda i, hk: (hk[0], 0, i, 0, 0))
    side = lambda spot: pl.BlockSpec((deep // 2, group, run, feat), lambda i, hk: (spot, i, 0, 0))
    flat = pl.BlockSpec((deep, group, run, feat), lambda i, hk: (0, i, 0, 0))
    tokens = deep * wide * run
    return pl.pallas_call(
        functools.partial(window_kernel, head_width),
        out_shape=jax.ShapeDtypeStruct((deep, wide, run, feat), jnp.bfloat16),
        grid_spec=pltpu.PrefetchScalarGridSpec(
            num_scalar_prefetch=1,
            grid=(wide // group,),
            in_specs=[
                *[side(spot) for spot in spots],
                own(feat),
                own(2 * feat),
                pl.BlockSpec((feat,), lambda i, hk: (0,)),
                *[
                    pl.BlockSpec((feat, feat), lambda i, hk, k=k: (0, k), pipeline_mode=pl.Buffered(1))
                    for k in (1, 2)
                ],
            ],
            out_specs=flat,
            scratch_shapes=[pltpu.VMEM((deep, group, run, 2 * feat), jnp.bfloat16)],
        ),
        compiler_params=pltpu.CompilerParams(vmem_limit_bytes=VMEM_LIMIT),
        cost_estimate=pl.CostEstimate(
            flops=2 * tokens * feat * 2 * feat + 8 * tokens * 256 * feat,
            bytes_accessed=tokens * feat * 10 + feat * feat * 6,
            transcendentals=tokens * 256 * HEADS,
        ),
    )(half_keep, *edges, q, kv_own, gain_row, w_qkv, w_qkv)


def direct_parts(recv, tok_ref, tiles, wanted, cap):
    cut = tok_ref.shape[1] // 2
    wide = tok_ref.shape[2]

    def own(j, seen):
        return tok_ref.at[j // wide, :cut, j % wide], tok_ref.at[j // wide, cut:, j % wide]

    def other(r):
        return lambda j, seen: (recv[r - 1].at[seen[r], :cut], recv[r - 1].at[seen[r], cut:])

    return {r: own if r == 0 else other(r) for r in range(tiles) if (wanted >> r) & 1}


def relay_parts(recv, tok_ref, tiles, wanted, cap):
    whole, x_same, x_cross, y_same, y_cross, rest = recv[:4], *recv[4:]
    cut = tok_ref.shape[1] // 2
    wide = tok_ref.shape[2]
    same = lambda k, j: [(True, whole[k].at[:, j % wide]), (False, whole[k + 2].at[:, j % wide])]
    table = {
        0: lambda j, seen: (tok_ref.at[j // wide, :cut, j % wide], tok_ref.at[j // wide, cut:, j % wide]),
        1: lambda j, seen: (rest.at[2 * cap + seen[1]], rest.at[3 * cap + seen[1]]),
        2: lambda j, seen: (same(0, j), x_same.at[seen[2] + seen[6]]),
        3: lambda j, seen: (rest.at[seen[3]], x_cross.at[seen[3] + seen[7]]),
        4: lambda j, seen: (y_same.at[seen[4] + seen[6]], same(1, j)),
        5: lambda j, seen: (y_cross.at[seen[5] + seen[7]], rest.at[cap + seen[5]]),
        6: lambda j, seen: (y_same.at[seen[4] + seen[6]], x_same.at[seen[2] + seen[6]]),
        7: lambda j, seen: (y_cross.at[seen[5] + seen[7]], x_cross.at[seen[3] + seen[7]]),
    }
    return {r: table[r] for r in range(tiles) if (wanted >> r) & 1}


def cross_kernel(plan, tiles, head_width, wanted, recv_count, cap, refs):
    tile_ref, panel_ref, valid_ref, half_ref, tok_ref = refs[:5]
    recv = refs[5 : 5 + recv_count]
    q_ref, mix_a, mix_b, gain_ref, wqkv_ref, wproj_ref = refs[5 + recv_count : 11 + recv_count]
    out_ref, got, q_s, own_s, res_s, wkv_s, wp_s, normed_s, kv_s, mixed_s, seen, ids, w_sem, sems = refs[-14:]
    panels, deep, run, feat = got.shape
    half = panels // 2
    cut = deep // 2
    length = deep * run
    me = lax.axis_index("tile")
    parts = plan(recv, tok_ref, tiles, wanted, cap)
    for t in range(tiles):
        seen[t] = 0

    def fetch(p, count):
        r = tile_ref[0, me, p] ^ me
        hit = ((wanted >> r) & 1) == 1

        @pl.when(hit)
        def _():
            ids[count] = p
            j = panel_ref[0, me, p]
            for k, pick in parts.items():

                @pl.when(r == k)
                def _(pick=pick):
                    for ref, rows, k in zip(pick(j, seen), (slice(0, cut), slice(cut, deep)), (0, 4)):
                        if not isinstance(ref, list):
                            pltpu.make_async_copy(ref, got.at[count, rows], sems.at[k, count]).start()
                            continue
                        for mine, choice in ref:

                            @pl.when((j // half == (me & 1)) == mine)
                            def _(choice=choice, rows=rows, k=k):
                                pltpu.make_async_copy(choice, got.at[count, rows], sems.at[k, count]).start()

            u = p // half
            w = p % half
            pltpu.make_async_copy(q_ref.at[u, :, w], q_s.at[count], sems.at[1, count]).start()

            @pl.when(u == half_ref[0])
            def _():
                pltpu.make_async_copy(mix_a.at[:, w], own_s.at[count], sems.at[2, count]).start()

            @pl.when(u != half_ref[0])
            def _():
                pltpu.make_async_copy(mix_b.at[:, w], own_s.at[count], sems.at[2, count]).start()

        seen[r] = seen[r] + 1
        return count + hit.astype(jnp.int32)

    load_wkv = pltpu.make_async_copy(wqkv_ref.at[:, feat:], wkv_s, w_sem.at[0])
    load_wp = pltpu.make_async_copy(wproj_ref, wp_s, w_sem.at[1])
    load_wkv.start()
    total = lax.fori_loop(0, panels, fetch, jnp.int32(0))
    load_wp.start()

    pair = 2 * head_width
    scale = LOG2E * head_width ** (-0.5)
    low = low_lanes(length, pair, head_width)
    zero = jnp.zeros((length, pair), jnp.bfloat16)
    one = jnp.ones((length, pair), jnp.bfloat16)
    marks = jnp.concatenate([jnp.where(low, one, zero), jnp.where(low, zero, one)], axis=0)
    pairs = feat // pair

    def unit(n, carry):
        first = 2 * n
        for i in range(2):

            @pl.when(first + i < total)
            def _(i=i):
                n_i = first + i
                for k, place in ((0, got.at[n_i, :cut]), (4, got.at[n_i, cut:])):
                    pltpu.make_async_copy(tok_ref.at[0, :cut, 0], place, sems.at[k, n_i]).wait()
                for k, place in ((1, q_s.at[n_i]), (2, own_s.at[n_i])):
                    pltpu.make_async_copy(tok_ref.at[0, :, 0], place, sems.at[k, n_i]).wait()

        rows = got[pl.ds(first, 2)].reshape(2 * length, feat)
        normed_s[...] = layer_norm(rows, gain_ref[...])

        @pl.when(n == 0)
        def _():
            load_wkv.wait()

        kv_s[...] = dot_f32(normed_s[...], wkv_s[...]).astype(jnp.bfloat16)

        @pl.when(n == 0)
        def _():
            load_wp.wait()

        gates = [valid_ref[ids[jnp.minimum(first + i, total - 1)]].astype(jnp.float32) for i in range(2)]

        def score(t):
            i, g = t // pairs, t % pairs
            at = slice(g * pair, (g + 1) * pair)
            q = q_s[first + i, :, :, at].reshape(length, pair)
            key = kv_s[i * length : (i + 1) * length, at]
            keys = jnp.concatenate([jnp.where(low, key, zero), jnp.where(low, zero, key)], axis=0)
            return dot_t(q, keys)

        def mix(t, scores):
            i, g = t // pairs, t % pairs
            at = slice(g * pair, (g + 1) * pair)
            val = kv_s[i * length : (i + 1) * length, feat + g * pair : feat + (g + 1) * pair]
            vals = jnp.concatenate([jnp.where(low, val, zero), jnp.where(low, zero, val)], axis=0)
            parts = []
            for h in range(2):
                part = scores[:, h * length : (h + 1) * length]
                peak = jnp.max(part, axis=1, keepdims=True)
                parts.append(jnp.exp2((part - peak) * scale).astype(jnp.bfloat16))
            both = dot_f32(jnp.concatenate(parts, axis=1), jnp.concatenate([vals, marks], axis=1))
            cross = (both[:, :pair] / both[:, pair:]).astype(jnp.bfloat16)
            own = own_s[first + i, :, :, at].reshape(length, pair)
            blended = gates[i] * own.astype(jnp.float32) + cross.astype(jnp.float32)
            mixed_s[i * length : (i + 1) * length, at] = blended.astype(jnp.bfloat16)

        staged(2 * pairs, score, mix)
        res_s[pl.ds(first, 2)] = dot_f32(mixed_s[...], wp_s[...]).astype(jnp.bfloat16).reshape(2, deep, run, feat)
        for i in range(2):

            @pl.when(first + i < total)
            def _(i=i):
                p = ids[first + i]
                pltpu.make_async_copy(
                    res_s.at[first + i], out_ref.at[p // half, :, p % half], sems.at[3, first + i]
                ).start()

        return carry

    lax.fori_loop(0, (total + 1) // 2, unit, 0)

    @pl.when(total == 0)
    def _():
        load_wkv.wait()
        load_wp.wait()

    def finish(n, carry):
        pltpu.make_async_copy(res_s.at[n], out_ref.at[0, :, 0], sems.at[3, n]).wait()
        return carry

    lax.fori_loop(0, total, finish, 0)


def cross_and_project(
    plan, wanted, tiles, cap, tile_table, panel_table, valid, half_keep, tok, recv, q, mixes, gain_row, w_qkv, w_proj, earlier
):
    halves, deep, wide, run, feat = tok.shape
    panels = halves * wide
    head_width = feat // HEADS
    length = deep * run
    smem = pl.BlockSpec(memory_space=pltpu.SMEM)
    anym = pl.BlockSpec(memory_space=pl.ANY)
    share = bin(wanted).count("1") / tiles
    tokens = int(panels * length * share)
    many = pltpu.VMEM((panels, deep, run, feat), jnp.bfloat16)
    operands = [tile_table, panel_table, valid, half_keep, tok, *recv, q, *mixes, gain_row, w_qkv, w_proj]
    specs = [smem] * 4 + [anym] * (len(recv) + 4) + [pl.BlockSpec((feat,), lambda: (0,))] + [anym] * 2
    aliases = {}
    if earlier is not None:
        aliases = {len(operands): 0}
        operands.append(earlier)
        specs.append(anym)

    def kernel(*refs):
        cross_kernel(plan, tiles, head_width, wanted, len(recv), cap, refs)

    return pl.pallas_call(
        kernel,
        out_shape=jax.ShapeDtypeStruct(tok.shape, jnp.bfloat16),
        in_specs=specs,
        out_specs=anym,
        scratch_shapes=[
            many,
            many,
            many,
            many,
            pltpu.VMEM((feat, 2 * feat), jnp.bfloat16),
            pltpu.VMEM((feat, feat), jnp.bfloat16),
            pltpu.VMEM((2 * length, feat), jnp.bfloat16),
            pltpu.VMEM((2 * length, 2 * feat), jnp.bfloat16),
            pltpu.VMEM((2 * length, feat), jnp.bfloat16),
            pltpu.SMEM((tiles,), jnp.int32),
            pltpu.SMEM((panels,), jnp.int32),
            pltpu.SemaphoreType.DMA((2,)),
            pltpu.SemaphoreType.DMA((5, panels)),
        ],
        input_output_aliases=aliases,
        compiler_params=pltpu.CompilerParams(vmem_limit_bytes=VMEM_LIMIT),
        cost_estimate=pl.CostEstimate(
            flops=2 * tokens * feat * 3 * feat + 8 * tokens * 128 * feat,
            bytes_accessed=tokens * feat * 8 + feat * feat * 6,
            transcendentals=tokens * 128 * HEADS,
        ),
    )(*operands)


def per_device(tokens, gain, w_qkv, w_proj, scene_first, window_valid, partner_tile, partner_panel):
    _, tok_rows, tok_cols, feat = tokens.shape
    run = 16
    wide = tok_cols // run
    tok = tokens.reshape(2, tok_rows // 2, wide, run, feat)
    tiles = partner_tile.shape[1]
    panels = partner_tile.shape[2]
    cap = 2 * max(1, panels // tiles)
    slab_count = scene_first.shape[0]
    tile_table = partner_tile[:, :, :, 0]
    panel_table = partner_panel
    valid = window_valid.reshape(panels)
    gain_row = gain
    slab_index = lax.axis_index(("scene", "tile"))
    after_index = jnp.minimum(slab_index + 1, slab_count - 1)
    own_first = jnp.logical_or(scene_first[slab_index] == 1, slab_index == 0)
    next_first = jnp.logical_or(scene_first[after_index] == 1, slab_index + 1 >= slab_count)
    keep_before = jnp.logical_not(own_first).astype(jnp.int32)
    keep_after = jnp.logical_not(next_first).astype(jnp.int32)

    def xor(block, bits):
        return lax.ppermute(block, "tile", [(i, i ^ bits) for i in range(tiles)])

    def cross(plan, wanted, recv, mixes, half_keep, earlier):
        return cross_and_project(
            plan,
            wanted,
            tiles,
            cap,
            tile_table,
            panel_table,
            valid,
            half_keep,
            tok,
            recv,
            q,
            mixes,
            gain_row,
            w_qkv,
            w_proj,
            earlier,
        )

    if tiles == 8:
        fence = lax.optimization_barrier
        odd = slab_index % 2
        direct = jnp.logical_or(slab_index % 4 == 1, slab_index % 4 == 2).astype(jnp.int32)
        near_half = jnp.stack([1 - odd, jnp.where(odd == 1, keep_before, keep_after), direct]).astype(jnp.int32)
        far_half = jnp.stack([odd, jnp.where(odd == 1, keep_after, keep_before), direct]).astype(jnp.int32)
        near_half, far_half = fence((near_half, far_half))
        links_a, links_b, links_c = [], [], []
        for low in range(1, slab_count - 1, 2):
            links_a += [(low ^ 2, low + 1), ((low + 1) ^ 2, low)]
            if low % 4 == 1:
                links_b += [(low, low + 1), (low + 1, low)]
            else:
                links_c += [(low ^ 4, low + 1), ((low + 1) ^ 4, low)]

        rim_x, off_x = split_half(0, tok)
        tok_next, off_x = fence((tok, off_x))
        rim_y, off_y = split_half(tok.shape[1] // 2, tok_next)
        rim_y, off_y, gain_next = fence((rim_y, off_y, gain_row))
        near = (xor(off_x, 1), xor(off_y, 1))
        own_rim = rim_y
        rim_x, rim_y = xor(rim_x, 2), xor(rim_y, 4)
        off_x, off_y = xor(off_x, 2), xor(off_y, 4)
        q, kv = project_own(tok, gain_next, w_qkv)
        edge_b = lax.ppermute(own_rim, ("scene", "tile"), links_b)
        mix_near = window_mix(near_half, near, (0, 0), q, kv, gain_row, w_qkv)
        rim_x, rim_y, mix_near = fence((rim_x, rim_y, mix_near))
        edge_c = lax.ppermute(rim_y, ("scene", "tile"), links_c)
        edge_a = lax.ppermute(rim_x, ("scene", "tile"), links_a)
        sides = (rim_x, rim_y, off_x, off_y)
        x_same, y_same, x_cross, y_cross, rest = pack_far(tile_table, panel_table, tok, sides, cap)
        y_same, rest = xor(y_same, 4), xor(rest, 1)
        edge_a, edge_b, edge_c, x_same, x_cross, y_cross = fence((edge_a, edge_b, edge_c, x_same, x_cross, y_cross))
        x_same = xor(x_same, 2)
        mix_far = window_mix(far_half, (edge_a, edge_b, edge_c), (0, 0, 0), q, kv, gain_row, w_qkv)
        x_cross, y_cross, mix_far = fence((x_cross, y_cross, mix_far))
        x_cross, y_cross = xor(x_cross, 3), xor(y_cross, 5)
        mixes = (mix_near, mix_far)
        early = (*sides, x_same, rest, y_same, rest, rest)
        late = (*sides, x_same, x_cross, y_same, y_cross, rest)
        out = cross(relay_parts, 0b01010111, early, mixes, near_half, None)
        out = cross(relay_parts, 0b10101000, late, mixes, near_half, out)
    else:
        forward = [(i, i + 1) for i in range(slab_count - 1)]
        backward = [(i + 1, i) for i in range(slab_count - 1)]
        before = lax.ppermute(tok[1], ("scene", "tile"), forward)
        after = lax.ppermute(tok[0], ("scene", "tile"), backward)
        outgoing = pack(tile_table, panel_table, tok, tiles, cap)
        recv = [xor(outgoing[r - 1], r) for r in range(1, tiles)]
        q, kv = project_own(tok, gain_row, w_qkv)
        zero = jnp.zeros((), jnp.int32)
        upper = jnp.stack([zero, keep_before])
        mix_up = window_mix(upper, (before, before), (0, 1), q, kv, gain_row, w_qkv)
        mix_down = window_mix(jnp.stack([zero + 1, keep_after]), (after, after), (0, 1), q, kv, gain_row, w_qkv)
        out = cross(direct_parts, (1 << tiles) - 1, recv, (mix_up, mix_down), upper, None)
    return out.reshape(tokens.shape)


def solution(mesh):
    in_specs = (
        P(("scene", "tile"), None, None, None),
        P(),
        P(),
        P(),
        P(),
        P(("scene", "tile"), None),
        P("scene", None, None, None),
        P("scene", None, None),
    )
    out_specs = P(("scene", "tile"), None, None, None)
    return jax.shard_map(per_device, mesh=mesh, in_specs=in_specs, out_specs=out_specs, check_vma=False)
```

```python
import functools

import jax
import jax.numpy as jnp
from jax import lax
from jax.experimental import pallas as pl
from jax.experimental.pallas import tpu as pltpu
from jax.sharding import PartitionSpec as P

HEADS = 16
NORM_EPS = 1e-05
LOG2E = 1.4426950408889634
VMEM_LIMIT = 63 * 1024 * 1024
GROUP = 4


def layer_norm(rows, gain_row):
    values = rows.astype(jnp.float32)
    centred = values - jnp.mean(values, axis=-1, keepdims=True)
    spread = jnp.mean(centred * centred, axis=-1, keepdims=True)
    return (centred * lax.rsqrt(spread + NORM_EPS) * gain_row.astype(jnp.float32)).astype(jnp.bfloat16)


def dot_f32(left, right):
    return jnp.dot(left, right, preferred_element_type=jnp.float32)


def dot_t(left, right):
    return lax.dot_general(left, right, (((1,), (1,)), ((), ())), preferred_element_type=jnp.float32)


def staged(count, first, second):
    held = first(0)
    for g in range(count):
        coming = first(g + 1) if g + 1 < count else None
        second(g, held)
        held = coming


def low_lanes(rows, width, head_width):
    return lax.broadcasted_iota(jnp.int32, (rows, width), 1) < head_width


def pack_kernel(tiles, panels, cap, tile_ref, panel_ref, tok_ref, *rest):
    outs, slab, sem, sems = rest[: tiles - 1], rest[tiles - 1], rest[tiles], rest[tiles + 1]
    me = lax.axis_index("tile")
    load = pltpu.make_async_copy(tok_ref, slab, sem)
    load.start()
    load.wait()
    counts = []
    for r in range(1, tiles):
        asker = me ^ r
        out = outs[r - 1]

        def body(p, count, asker=asker, out=out, r=r):
            hit = jnp.logical_and(tile_ref[0, asker, p] == me, count < cap)

            @pl.when(hit)
            def _():
                j = panel_ref[0, asker, p]
                pltpu.make_async_copy(
                    slab.at[j // (panels // 2), :, j % (panels // 2)], out.at[count], sems.at[r, count]
                ).start()

            return count + hit.astype(jnp.int32)

        counts.append(lax.fori_loop(0, panels, body, jnp.int32(0)))
    for r in range(1, tiles):
        for c in range(cap):

            @pl.when(c < counts[r - 1])
            def _(r=r, c=c):
                pltpu.make_async_copy(slab.at[0, :, 0], outs[r - 1].at[c], sems.at[r, c]).wait()


def pack(tile_table, panel_table, tok, tiles, cap):
    panels = 2 * tok.shape[2]
    block = (cap, tok.shape[1], tok.shape[3], tok.shape[4])
    smem = pl.BlockSpec(memory_space=pltpu.SMEM)
    anym = pl.BlockSpec(memory_space=pl.ANY)
    return pl.pallas_call(
        functools.partial(pack_kernel, tiles, panels, cap),
        out_shape=[jax.ShapeDtypeStruct(block, tok.dtype)] * (tiles - 1),
        in_specs=[smem, smem, anym],
        out_specs=[anym] * (tiles - 1),
        scratch_shapes=[
            pltpu.VMEM(tok.shape, tok.dtype),
            pltpu.SemaphoreType.DMA,
            pltpu.SemaphoreType.DMA((tiles, cap)),
        ],
        cost_estimate=pl.CostEstimate(flops=0, bytes_accessed=16 << 20, transcendentals=0),
    )(tile_table, panel_table, tok)


def copy_through(pairs, bounce, sems):
    loads = [pltpu.make_async_copy(src, bounce.at[k], sems.at[0, k]) for k, (src, _) in enumerate(pairs)]
    for load in loads:
        load.start()
    stores = []
    for k, (_, dst) in enumerate(pairs):
        loads[k].wait()
        store = pltpu.make_async_copy(bounce.at[k], dst, sems.at[1, k])
        store.start()
        stores.append(store)
    for store in stores:
        store.wait()


def halves_kernel(picks, tok_ref, *rest):
    outs, bounce, sems = rest[: len(picks)], rest[-2], rest[-1]
    deep = outs[0].shape[0]
    part = lax.axis_index("tile") & 1
    bite = deep // 2
    pairs = []
    for (rim, start), out in zip(picks, outs):
        u = part if rim else 1 - part
        for k in range(0, deep, bite):
            pairs.append((tok_ref.at[u, start + k : start + k + bite], out.at[k : k + bite]))
    copy_through(pairs, bounce, sems)


def split_halves(picks, tok):
    halves, deep, wide, run, feat = tok.shape
    part = (deep // 2, wide, run, feat)
    count = len(picks)
    anym = pl.BlockSpec(memory_space=pl.ANY)
    return pl.pallas_call(
        functools.partial(halves_kernel, picks),
        out_shape=[jax.ShapeDtypeStruct(part, tok.dtype)] * count,
        in_specs=[anym],
        out_specs=[anym] * count,
        scratch_shapes=[
            pltpu.VMEM((2 * count, part[0] // 2) + part[1:], tok.dtype),
            pltpu.SemaphoreType.DMA((2, 2 * count)),
        ],
        cost_estimate=pl.CostEstimate(flops=0, bytes_accessed=count << 21, transcendentals=0),
    )(tok)


def far_kernel(cap, tile_ref, panel_ref, tok_ref, *rest):
    sides, outs, stage, in_sems, out_sems = rest[:4], rest[4:9], *rest[9:]
    halves, deep, wide, run, feat = tok_ref.shape
    panels = halves * wide
    cut = deep // 2
    me = lax.axis_index("tile")
    part = me & 1

    def bring(cond, ref, k, spot):
        @pl.when(cond)
        def _():
            pltpu.make_async_copy(ref, stage.at[k, spot], in_sems.at[k, spot]).start()

    def bring_side(cond, axis, j, k, spot):
        aligned = j // wide == part
        bring(jnp.logical_and(cond, aligned), sides[axis].at[:, j % wide], k, spot)
        bring(jnp.logical_and(cond, jnp.logical_not(aligned)), sides[2 + axis].at[:, j % wide], k, spot)

    totals = []
    for k, (bits, relay) in enumerate(((2, 4), (4, 2), (3, 4), (5, 2))):
        asker = me ^ bits
        axis, rows = (1, slice(cut, deep)) if relay == 4 else (0, slice(0, cut))

        def body(p, count, k=k, asker=asker, relay=relay, axis=axis, rows=rows):
            named = tile_ref[0, asker, p]
            own = jnp.logical_and(named == me, count < 2 * cap)
            other = jnp.logical_and(named == me ^ relay, count < 2 * cap)
            j = panel_ref[0, asker, p]
            bring(own, tok_ref.at[j // wide, rows, j % wide], k, count)
            bring_side(other, axis, j, k, count)
            return count + jnp.logical_or(own, other).astype(jnp.int32)

        totals.append(lax.fori_loop(0, panels, body, jnp.int32(0)))

    def near(p, counts):
        named = tile_ref[0, me ^ 1, p]
        j = panel_ref[0, me ^ 1, p]
        hits = [jnp.logical_and(named == me ^ relay, counts[k] < cap) for k, relay in enumerate((2, 4, 0))]
        for k in range(2):
            bring_side(hits[k], k, j, 4, k * cap + counts[k])
        bring(hits[2], tok_ref.at[j // wide, :cut, j % wide], 4, 2 * cap + counts[2])
        bring(hits[2], tok_ref.at[j // wide, cut:, j % wide], 4, 3 * cap + counts[2])
        return tuple(count + hit.astype(jnp.int32) for count, hit in zip(counts, hits))

    near_totals = lax.fori_loop(0, panels, near, (jnp.int32(0),) * 3)
    used = []
    for k in range(4):
        used += [(k, c, c < totals[k]) for c in range(2 * cap)]
    used += [(4, c, c % cap < near_totals[min(c // cap, 2)]) for c in range(4 * cap)]
    for k, c, cond in used:

        @pl.when(cond)
        def _(k=k, c=c):
            pltpu.make_async_copy(sides[0].at[:, 0], stage.at[k, c], in_sems.at[k, c]).wait()
            pltpu.make_async_copy(stage.at[k, c], outs[k].at[c], out_sems.at[k, c]).start()

    for k, c, cond in used:

        @pl.when(cond)
        def _(k=k, c=c):
            pltpu.make_async_copy(stage.at[k, c], outs[k].at[c], out_sems.at[k, c]).wait()


def pack_far(tile_table, panel_table, tok, sides, cap):
    halves, deep, wide, run, feat = tok.shape
    smem = pl.BlockSpec(memory_space=pltpu.SMEM)
    anym = pl.BlockSpec(memory_space=pl.ANY)
    block = (2 * cap, deep // 2, run, feat)
    return pl.pallas_call(
        functools.partial(far_kernel, cap),
        out_shape=[jax.ShapeDtypeStruct(block, tok.dtype)] * 4
        + [jax.ShapeDtypeStruct((4 * cap,) + block[1:], tok.dtype)],
        in_specs=[smem, smem] + [anym] * 5,
        out_specs=[anym] * 5,
        scratch_shapes=[
            pltpu.VMEM((5, 4 * cap) + block[1:], tok.dtype),
            pltpu.SemaphoreType.DMA((5, 4 * cap)),
            pltpu.SemaphoreType.DMA((5, 4 * cap)),
        ],
        compiler_params=pltpu.CompilerParams(vmem_limit_bytes=VMEM_LIMIT),
        cost_estimate=pl.CostEstimate(flops=0, bytes_accessed=6 << 20, transcendentals=0),
    )(tile_table, panel_table, tok, *sides)


def qkv_kernel(tok_ref, gain_ref, w_ref, q_ref, kv_ref):
    dims = tok_ref.shape
    feat = dims[-1]
    rows = dims[1] * dims[2] * dims[3]
    normed = layer_norm(tok_ref[...].reshape(rows, feat), gain_ref[...])
    q_ref[...] = dot_f32(normed, w_ref[:, :feat]).astype(jnp.bfloat16).reshape(q_ref.shape)
    kv_ref[...] = dot_f32(normed, w_ref[:, feat:]).astype(jnp.bfloat16).reshape(kv_ref.shape)


def project_own(tok, gain_row, w_qkv):
    halves, deep, wide, run, feat = tok.shape
    step = deep // 2
    spec = lambda width: pl.BlockSpec((1, step, wide, run, width), lambda i: (i // 2, i % 2, 0, 0, 0))
    tokens = halves * deep * wide * run
    return pl.pallas_call(
        qkv_kernel,
        grid=(halves * 2,),
        out_shape=[
            jax.ShapeDtypeStruct((halves, deep, wide, run, feat), jnp.bfloat16),
            jax.ShapeDtypeStruct((halves, deep, wide, run, 2 * feat), jnp.bfloat16),
        ],
        in_specs=[
            spec(feat),
            pl.BlockSpec((feat,), lambda i: (0,)),
            pl.BlockSpec((feat, 3 * feat), lambda i: (0, 0), pipeline_mode=pl.Buffered(1)),
        ],
        out_specs=[spec(feat), spec(2 * feat)],
        compiler_params=pltpu.CompilerParams(vmem_limit_bytes=VMEM_LIMIT),
        cost_estimate=pl.CostEstimate(
            flops=2 * tokens * feat * 3 * feat, bytes_accessed=tokens * feat * 8 + feat * feat * 6, transcendentals=0
        ),
    )(tok, gain_row, w_qkv)


def window_kernel(head_width, half_ref, *refs):
    edges, (q_ref, kvo_ref, gain_ref, wk_ref, wv_ref, mix_ref, kv_s) = refs[:-7], refs[-7:]
    deep, group, run, feat = mix_ref.shape
    length = deep * run
    bottom = edges[1][...]
    if len(edges) == 3:
        bottom = jnp.where(half_ref[2] == 1, bottom, edges[2][...])
    rows = jnp.concatenate([edges[0][...], bottom], axis=0).reshape(deep * group * run, feat)
    normed = layer_norm(rows, gain_ref[...])
    half_shape = kv_s.shape[:-1] + (feat,)
    kv_s[..., :feat] = dot_f32(normed, wk_ref[...]).astype(jnp.bfloat16).reshape(half_shape)
    kv_s[..., feat:] = dot_f32(normed, wv_ref[...]).astype(jnp.bfloat16).reshape(half_shape)
    pair = 2 * head_width
    scale = LOG2E * head_width ** (-0.5)
    bias = jnp.where(
        jnp.logical_and(half_ref[1] == 0, lax.broadcasted_iota(jnp.int32, (1, 2 * length), 1) < length), -jnp.inf, 0.0
    )
    low = low_lanes(length, pair, head_width)
    ones = jnp.ones((2 * length, pair), jnp.bfloat16)
    zero = jnp.zeros((length, pair), jnp.bfloat16)
    def panel(i, carry):
        def score(g):
            at = slice(g * pair, (g + 1) * pair)
            q = q_ref[0, :, i, :, at].reshape(length, pair)
            qs = jnp.concatenate([jnp.where(low, q, zero), jnp.where(low, zero, q)], axis=0)
            keys = jnp.concatenate(
                [kv_s[:, i, :, at].reshape(length, pair), kvo_ref[0, :, i, :, at].reshape(length, pair)], axis=0
            )
            return dot_t(qs, keys) + bias

        def mix(g, scores):
            at_v = slice(feat + g * pair, feat + (g + 1) * pair)
            vals = jnp.concatenate(
                [kv_s[:, i, :, at_v].reshape(length, pair), kvo_ref[0, :, i, :, at_v].reshape(length, pair)], axis=0
            )
            peak = jnp.max(scores, axis=1, keepdims=True)
            weights = jnp.exp2((scores - peak) * scale).astype(jnp.bfloat16)
            both = dot_f32(weights, jnp.concatenate([vals, ones], axis=1))
            mixed = both[:, :pair] / both[:, pair:]
            out = jnp.where(low, mixed[:length], mixed[length:])
            mix_ref[:, i, :, g * pair : (g + 1) * pair] = out.astype(jnp.bfloat16).reshape(deep, run, pair)

        staged(feat // pair, score, mix)
        return carry

    lax.fori_loop(0, group, panel, 0)


def window_mix(half_keep, edges, spots, q, kv_own, gain_row, w_qkv):
    _, deep, wide, run, feat = q.shape
    group = min(GROUP, wide)
    head_width = feat // HEADS
    own = lambda width: pl.BlockSpec((1, deep, group, run, width), lambda i, hk: (hk[0], 0, i, 0, 0))
    side = lambda spot: pl.BlockSpec((deep // 2, group, run, feat), lambda i, hk: (spot, i, 0, 0))
    flat = pl.BlockSpec((deep, group, run, feat), lambda i, hk: (0, i, 0, 0))
    tokens = deep * wide * run
    return pl.pallas_call(
        functools.partial(window_kernel, head_width),
        out_shape=jax.ShapeDtypeStruct((deep, wide, run, feat), jnp.bfloat16),
        grid_spec=pltpu.PrefetchScalarGridSpec(
            num_scalar_prefetch=1,
            grid=(wide // group,),
            in_specs=[
                *[side(spot) for spot in spots],
                own(feat),
                own(2 * feat),
                pl.BlockSpec((feat,), lambda i, hk: (0,)),
                *[
                    pl.BlockSpec((feat, feat), lambda i, hk, k=k: (0, k), pipeline_mode=pl.Buffered(1))
                    for k in (1, 2)
                ],
            ],
            out_specs=flat,
            scratch_shapes=[pltpu.VMEM((deep, group, run, 2 * feat), jnp.bfloat16)],
        ),
        compiler_params=pltpu.CompilerParams(vmem_limit_bytes=VMEM_LIMIT),
        cost_estimate=pl.CostEstimate(
            flops=2 * tokens * feat * 2 * feat + 8 * tokens * 256 * feat,
            bytes_accessed=tokens * feat * 10 + feat * feat * 6,
            transcendentals=tokens * 256 * HEADS,
        ),
    )(half_keep, *edges, q, kv_own, gain_row, w_qkv, w_qkv)


def direct_parts(recv, tok_ref, tiles, wanted, cap):
    cut = tok_ref.shape[1] // 2
    wide = tok_ref.shape[2]

    def own(j, seen):
        return tok_ref.at[j // wide, :cut, j % wide], tok_ref.at[j // wide, cut:, j % wide]

    def other(r):
        return lambda j, seen: (recv[r - 1].at[seen[r], :cut], recv[r - 1].at[seen[r], cut:])

    return {r: own if r == 0 else other(r) for r in range(tiles) if (wanted >> r) & 1}


def relay_parts(recv, tok_ref, tiles, wanted, cap):
    whole, x_same, x_cross, y_same, y_cross, rest = recv[:4], *recv[4:]
    cut = tok_ref.shape[1] // 2
    wide = tok_ref.shape[2]
    same = lambda k, j: [(True, whole[k].at[:, j % wide]), (False, whole[k + 2].at[:, j % wide])]
    table = {
        0: lambda j, seen: (tok_ref.at[j // wide, :cut, j % wide], tok_ref.at[j // wide, cut:, j % wide]),
        1: lambda j, seen: (rest.at[2 * cap + seen[1]], rest.at[3 * cap + seen[1]]),
        2: lambda j, seen: (same(0, j), x_same.at[seen[2] + seen[6]]),
        3: lambda j, seen: (rest.at[seen[3]], x_cross.at[seen[3] + seen[7]]),
        4: lambda j, seen: (y_same.at[seen[4] + seen[6]], same(1, j)),
        5: lambda j, seen: (y_cross.at[seen[5] + seen[7]], rest.at[cap + seen[5]]),
        6: lambda j, seen: (y_same.at[seen[4] + seen[6]], x_same.at[seen[2] + seen[6]]),
        7: lambda j, seen: (y_cross.at[seen[5] + seen[7]], x_cross.at[seen[3] + seen[7]]),
    }
    return {r: table[r] for r in range(tiles) if (wanted >> r) & 1}


def cross_kernel(plan, tiles, head_width, wanted, recv_count, cap, refs):
    tile_ref, panel_ref, valid_ref, half_ref, tok_ref = refs[:5]
    recv = refs[5 : 5 + recv_count]
    q_ref, mix_a, mix_b, gain_ref, wqkv_ref, wproj_ref = refs[5 + recv_count : 11 + recv_count]
    out_ref, got, q_s, own_s, res_s, wkv_s, wp_s, normed_s, kv_s, mixed_s, seen, ids, slots, w_sem, sems = refs[-15:]
    panels, deep, run, feat = got.shape
    half = panels // 2
    cut = deep // 2
    length = deep * run
    me = lax.axis_index("tile")
    parts = plan(recv, tok_ref, tiles, wanted, cap)
    for t in range(tiles):
        seen[t] = 0

    def record(p, count):
        r = tile_ref[0, me, p] ^ me
        hit = ((wanted >> r) & 1) == 1

        @pl.when(hit)
        def _():
            ids[count] = p
            for t in range(tiles):
                slots[count, t] = seen[t]

        seen[r] = seen[r] + 1
        return count + hit.astype(jnp.int32)

    def fetch(n):
        p = ids[n]
        j = panel_ref[0, me, p]
        r = tile_ref[0, me, p] ^ me
        for k, pick in parts.items():

            @pl.when(r == k)
            def _(pick=pick):
                for ref, rows, k in zip(pick(j, slots.at[n]), (slice(0, cut), slice(cut, deep)), (0, 4)):
                    if not isinstance(ref, list):
                        pltpu.make_async_copy(ref, got.at[n, rows], sems.at[k, n]).start()
                        continue
                    for mine, choice in ref:

                        @pl.when((j // half == (me & 1)) == mine)
                        def _(choice=choice, rows=rows, k=k):
                            pltpu.make_async_copy(choice, got.at[n, rows], sems.at[k, n]).start()

        u = p // half
        w = p % half
        pltpu.make_async_copy(q_ref.at[u, :, w], q_s.at[n], sems.at[1, n]).start()

        @pl.when(u == half_ref[0])
        def _():
            pltpu.make_async_copy(mix_a.at[:, w], own_s.at[n], sems.at[2, n]).start()

        @pl.when(u != half_ref[0])
        def _():
            pltpu.make_async_copy(mix_b.at[:, w], own_s.at[n], sems.at[2, n]).start()

    def fetch_unit(n):
        def one(i, carry):
            fetch(i)
            return carry

        lax.fori_loop(2 * n, jnp.minimum(2 * n + 2, total), one, 0)

    load_wkv = pltpu.make_async_copy(wqkv_ref.at[:, feat:], wkv_s, w_sem.at[0])
    load_wp = pltpu.make_async_copy(wproj_ref, wp_s, w_sem.at[1])
    load_wkv.start()
    total = lax.fori_loop(0, panels, record, jnp.int32(0))
    fetch_unit(0)
    load_wp.start()

    pair = 2 * head_width
    scale = LOG2E * head_width ** (-0.5)
    low = low_lanes(length, pair, head_width)
    zero = jnp.zeros((length, pair), jnp.bfloat16)
    one = jnp.ones((length, pair), jnp.bfloat16)
    marks = jnp.concatenate([jnp.where(low, one, zero), jnp.where(low, zero, one)], axis=0)
    pairs = feat // pair

    def unit(n, carry):
        first = 2 * n
        for i in range(2):

            @pl.when(first + i < total)
            def _(i=i):
                n_i = first + i
                for k, place in ((0, got.at[n_i, :cut]), (4, got.at[n_i, cut:])):
                    pltpu.make_async_copy(tok_ref.at[0, :cut, 0], place, sems.at[k, n_i]).wait()
                for k, place in ((1, q_s.at[n_i]), (2, own_s.at[n_i])):
                    pltpu.make_async_copy(tok_ref.at[0, :, 0], place, sems.at[k, n_i]).wait()

        rows = got[pl.ds(first, 2)].reshape(2 * length, feat)
        normed_s[...] = layer_norm(rows, gain_ref[...])

        @pl.when(n == 0)
        def _():
            load_wkv.wait()

        fetch_unit(n + 1)
        kv_s[...] = dot_f32(normed_s[...], wkv_s[...]).astype(jnp.bfloat16)

        @pl.when(n == 0)
        def _():
            load_wp.wait()

        gates = [valid_ref[ids[jnp.minimum(first + i, total - 1)]].astype(jnp.float32) for i in range(2)]

        def score(t):
            i, g = t // pairs, t % pairs
            at = slice(g * pair, (g + 1) * pair)
            q = q_s[first + i, :, :, at].reshape(length, pair)
            key = kv_s[i * length : (i + 1) * length, at]
            keys = jnp.concatenate([jnp.where(low, key, zero), jnp.where(low, zero, key)], axis=0)
            return dot_t(q, keys)

        def mix(t, scores):
            i, g = t // pairs, t % pairs
            at = slice(g * pair, (g + 1) * pair)
            val = kv_s[i * length : (i + 1) * length, feat + g * pair : feat + (g + 1) * pair]
            vals = jnp.concatenate([jnp.where(low, val, zero), jnp.where(low, zero, val)], axis=0)
            parts = []
            for h in range(2):
                part = scores[:, h * length : (h + 1) * length]
                peak = jnp.max(part, axis=1, keepdims=True)
                parts.append(jnp.exp2((part - peak) * scale).astype(jnp.bfloat16))
            both = dot_f32(jnp.concatenate(parts, axis=1), jnp.concatenate([vals, marks], axis=1))
            cross = (both[:, :pair] / both[:, pair:]).astype(jnp.bfloat16)
            own = own_s[first + i, :, :, at].reshape(length, pair)
            blended = gates[i] * own.astype(jnp.float32) + cross.astype(jnp.float32)
            mixed_s[i * length : (i + 1) * length, at] = blended.astype(jnp.bfloat16)

        staged(2 * pairs, score, mix)
        res_s[pl.ds(first, 2)] = dot_f32(mixed_s[...], wp_s[...]).astype(jnp.bfloat16).reshape(2, deep, run, feat)
        for i in range(2):

            @pl.when(first + i < total)
            def _(i=i):
                p = ids[first + i]
                pltpu.make_async_copy(
                    res_s.at[first + i], out_ref.at[p // half, :, p % half], sems.at[3, first + i]
                ).start()

        return carry

    lax.fori_loop(0, (total + 1) // 2, unit, 0)

    @pl.when(total == 0)
    def _():
        load_wkv.wait()
        load_wp.wait()

    def finish(n, carry):
        pltpu.make_async_copy(res_s.at[n], out_ref.at[0, :, 0], sems.at[3, n]).wait()
        return carry

    lax.fori_loop(0, total, finish, 0)


def cross_and_project(
    plan, wanted, tiles, cap, tile_table, panel_table, valid, half_keep, tok, recv, q, mixes, gain_row, w_qkv, w_proj, earlier
):
    halves, deep, wide, run, feat = tok.shape
    panels = halves * wide
    head_width = feat // HEADS
    length = deep * run
    smem = pl.BlockSpec(memory_space=pltpu.SMEM)
    anym = pl.BlockSpec(memory_space=pl.ANY)
    share = bin(wanted).count("1") / tiles
    tokens = int(panels * length * share)
    many = pltpu.VMEM((panels, deep, run, feat), jnp.bfloat16)
    operands = [tile_table, panel_table, valid, half_keep, tok, *recv, q, *mixes, gain_row, w_qkv, w_proj]
    specs = [smem] * 4 + [anym] * (len(recv) + 4) + [pl.BlockSpec((feat,), lambda: (0,))] + [anym] * 2
    aliases = {}
    if earlier is not None:
        aliases = {len(operands): 0}
        operands.append(earlier)
        specs.append(anym)

    def kernel(*refs):
        cross_kernel(plan, tiles, head_width, wanted, len(recv), cap, refs)

    return pl.pallas_call(
        kernel,
        out_shape=jax.ShapeDtypeStruct(tok.shape, jnp.bfloat16),
        in_specs=specs,
        out_specs=anym,
        scratch_shapes=[
            many,
            many,
            many,
            many,
            pltpu.VMEM((feat, 2 * feat), jnp.bfloat16),
            pltpu.VMEM((feat, feat), jnp.bfloat16),
            pltpu.VMEM((2 * length, feat), jnp.bfloat16),
            pltpu.VMEM((2 * length, 2 * feat), jnp.bfloat16),
            pltpu.VMEM((2 * length, feat), jnp.bfloat16),
            pltpu.SMEM((tiles,), jnp.int32),
            pltpu.SMEM((panels,), jnp.int32),
            pltpu.SMEM((panels, tiles), jnp.int32),
            pltpu.SemaphoreType.DMA((2,)),
            pltpu.SemaphoreType.DMA((5, panels)),
        ],
        input_output_aliases=aliases,
        compiler_params=pltpu.CompilerParams(vmem_limit_bytes=VMEM_LIMIT),
        cost_estimate=pl.CostEstimate(
            flops=2 * tokens * feat * 3 * feat + 8 * tokens * 128 * feat,
            bytes_accessed=tokens * feat * 8 + feat * feat * 6,
            transcendentals=tokens * 128 * HEADS,
        ),
    )(*operands)


def per_device(tokens, gain, w_qkv, w_proj, scene_first, window_valid, partner_tile, partner_panel):
    _, tok_rows, tok_cols, feat = tokens.shape
    run = 16
    wide = tok_cols // run
    tok = tokens.reshape(2, tok_rows // 2, wide, run, feat)
    tiles = partner_tile.shape[1]
    panels = partner_tile.shape[2]
    cap = 2 * max(1, panels // tiles)
    slab_count = scene_first.shape[0]
    tile_table = partner_tile[:, :, :, 0]
    panel_table = partner_panel
    valid = window_valid.reshape(panels)
    gain_row = gain
    slab_index = lax.axis_index(("scene", "tile"))
    after_index = jnp.minimum(slab_index + 1, slab_count - 1)
    own_first = jnp.logical_or(scene_first[slab_index] == 1, slab_index == 0)
    next_first = jnp.logical_or(scene_first[after_index] == 1, slab_index + 1 >= slab_count)
    keep_before = jnp.logical_not(own_first).astype(jnp.int32)
    keep_after = jnp.logical_not(next_first).astype(jnp.int32)

    def xor(block, bits):
        return lax.ppermute(block, "tile", [(i, i ^ bits) for i in range(tiles)])

    def cross(plan, wanted, recv, mixes, half_keep, earlier):
        return cross_and_project(
            plan,
            wanted,
            tiles,
            cap,
            tile_table,
            panel_table,
            valid,
            half_keep,
            tok,
            recv,
            q,
            mixes,
            gain_row,
            w_qkv,
            w_proj,
            earlier,
        )

    if tiles == 8:
        fence = lax.optimization_barrier
        odd = slab_index % 2
        direct = jnp.logical_or(slab_index % 4 == 1, slab_index % 4 == 2).astype(jnp.int32)
        near_half = jnp.stack([1 - odd, jnp.where(odd == 1, keep_before, keep_after), direct]).astype(jnp.int32)
        far_half = jnp.stack([odd, jnp.where(odd == 1, keep_after, keep_before), direct]).astype(jnp.int32)
        near_half, far_half = fence((near_half, far_half))
        links_a, links_b, links_c = [], [], []
        for low in range(1, slab_count - 1, 2):
            links_a += [(low ^ 2, low + 1), ((low + 1) ^ 2, low)]
            if low % 4 == 1:
                links_b += [(low, low + 1), (low + 1, low)]
            else:
                links_c += [(low ^ 4, low + 1), ((low + 1) ^ 4, low)]

        cut = tok.shape[1] // 2
        (off_x,) = split_halves(((False, 0),), tok)
        tok_next, off_x = fence((tok, off_x))
        off_y, rim_x, rim_y = split_halves(((False, cut), (True, 0), (True, cut)), tok_next)
        rim_x, rim_y, off_y, gain_next = fence((rim_x, rim_y, off_y, gain_row))
        near = (xor(off_x, 1), xor(off_y, 1))
        own_rim = rim_y
        rim_x, rim_y = xor(rim_x, 2), xor(rim_y, 4)
        off_x, off_y = xor(off_x, 2), xor(off_y, 4)
        q, kv = project_own(tok, gain_next, w_qkv)
        edge_b = lax.ppermute(own_rim, ("scene", "tile"), links_b)
        mix_near = window_mix(near_half, near, (0, 0), q, kv, gain_row, w_qkv)
        rim_x, rim_y, mix_near = fence((rim_x, rim_y, mix_near))
        edge_c = lax.ppermute(rim_y, ("scene", "tile"), links_c)
        edge_a = lax.ppermute(rim_x, ("scene", "tile"), links_a)
        sides = (rim_x, rim_y, off_x, off_y)
        x_same, y_same, x_cross, y_cross, rest = pack_far(tile_table, panel_table, tok, sides, cap)
        y_same, rest = xor(y_same, 4), xor(rest, 1)
        edge_a, edge_b, edge_c, x_same, x_cross, y_cross = fence((edge_a, edge_b, edge_c, x_same, x_cross, y_cross))
        x_same = xor(x_same, 2)
        mix_far = window_mix(far_half, (edge_a, edge_b, edge_c), (0, 0, 0), q, kv, gain_row, w_qkv)
        x_cross, y_cross, mix_far = fence((x_cross, y_cross, mix_far))
        x_cross, y_cross = xor(x_cross, 3), xor(y_cross, 5)
        mixes = (mix_near, mix_far)
        early = (*sides, x_same, rest, y_same, rest, rest)
        late = (*sides, x_same, x_cross, y_same, y_cross, rest)
        out = cross(relay_parts, 0b01010111, early, mixes, near_half, None)
        out = cross(relay_parts, 0b10101000, late, mixes, near_half, out)
    else:
        forward = [(i, i + 1) for i in range(slab_count - 1)]
        backward = [(i + 1, i) for i in range(slab_count - 1)]
        before = lax.ppermute(tok[1], ("scene", "tile"), forward)
        after = lax.ppermute(tok[0], ("scene", "tile"), backward)
        outgoing = pack(tile_table, panel_table, tok, tiles, cap)
        recv = [xor(outgoing[r - 1], r) for r in range(1, tiles)]
        q, kv = project_own(tok, gain_row, w_qkv)
        zero = jnp.zeros((), jnp.int32)
        upper = jnp.stack([zero, keep_before])
        mix_up = window_mix(upper, (before, before), (0, 1), q, kv, gain_row, w_qkv)
        mix_down = window_mix(jnp.stack([zero + 1, keep_after]), (after, after), (0, 1), q, kv, gain_row, w_qkv)
        out = cross(direct_parts, (1 << tiles) - 1, recv, (mix_up, mix_down), upper, None)
    return out.reshape(tokens.shape)


def solution(mesh):
    in_specs = (
        P(("scene", "tile"), None, None, None),
        P(),
        P(),
        P(),
        P(),
        P(("scene", "tile"), None),
        P("scene", None, None, None),
        P("scene", None, None),
    )
    out_specs = P(("scene", "tile"), None, None, None)
    return jax.shard_map(per_device, mesh=mesh, in_specs=in_specs, out_specs=out_specs, check_vma=False)
```

```python
import functools

import jax
import jax.numpy as jnp
from jax import lax
from jax.experimental import pallas as pl
from jax.experimental.pallas import tpu as pltpu
from jax.sharding import PartitionSpec as P

HEADS = 16
NORM_EPS = 1e-05
LOG2E = 1.4426950408889634
VMEM_LIMIT = 63 * 1024 * 1024
GROUP = 4


def layer_norm(rows, gain_row):
    values = rows.astype(jnp.float32)
    centred = values - jnp.mean(values, axis=-1, keepdims=True)
    spread = jnp.mean(centred * centred, axis=-1, keepdims=True)
    return (centred * lax.rsqrt(spread + NORM_EPS) * gain_row.astype(jnp.float32)).astype(jnp.bfloat16)


def dot_f32(left, right):
    return jnp.dot(left, right, preferred_element_type=jnp.float32)


def dot_t(left, right):
    return lax.dot_general(left, right, (((1,), (1,)), ((), ())), preferred_element_type=jnp.float32)


def staged(count, first, second):
    held = first(0)
    for g in range(count):
        coming = first(g + 1) if g + 1 < count else None
        second(g, held)
        held = coming


def low_lanes(rows, width, head_width):
    return lax.broadcasted_iota(jnp.int32, (rows, width), 1) < head_width


def pack_kernel(tiles, panels, cap, tile_ref, panel_ref, tok_ref, *rest):
    outs, slab, sem, sems = rest[: tiles - 1], rest[tiles - 1], rest[tiles], rest[tiles + 1]
    me = lax.axis_index("tile")
    load = pltpu.make_async_copy(tok_ref, slab, sem)
    load.start()
    load.wait()
    counts = []
    for r in range(1, tiles):
        asker = me ^ r
        out = outs[r - 1]

        def body(p, count, asker=asker, out=out, r=r):
            hit = jnp.logical_and(tile_ref[0, asker, p] == me, count < cap)

            @pl.when(hit)
            def _():
                j = panel_ref[0, asker, p]
                pltpu.make_async_copy(
                    slab.at[j // (panels // 2), :, j % (panels // 2)], out.at[count], sems.at[r, count]
                ).start()

            return count + hit.astype(jnp.int32)

        counts.append(lax.fori_loop(0, panels, body, jnp.int32(0)))
    for r in range(1, tiles):
        for c in range(cap):

            @pl.when(c < counts[r - 1])
            def _(r=r, c=c):
                pltpu.make_async_copy(slab.at[0, :, 0], outs[r - 1].at[c], sems.at[r, c]).wait()


def pack(tile_table, panel_table, tok, tiles, cap):
    panels = 2 * tok.shape[2]
    block = (cap, tok.shape[1], tok.shape[3], tok.shape[4])
    smem = pl.BlockSpec(memory_space=pltpu.SMEM)
    anym = pl.BlockSpec(memory_space=pl.ANY)
    return pl.pallas_call(
        functools.partial(pack_kernel, tiles, panels, cap),
        out_shape=[jax.ShapeDtypeStruct(block, tok.dtype)] * (tiles - 1),
        in_specs=[smem, smem, anym],
        out_specs=[anym] * (tiles - 1),
        scratch_shapes=[
            pltpu.VMEM(tok.shape, tok.dtype),
            pltpu.SemaphoreType.DMA,
            pltpu.SemaphoreType.DMA((tiles, cap)),
        ],
        cost_estimate=pl.CostEstimate(flops=0, bytes_accessed=16 << 20, transcendentals=0),
    )(tile_table, panel_table, tok)


def copy_through(pairs, bounce, sems):
    loads = [pltpu.make_async_copy(src, bounce.at[k], sems.at[0, k]) for k, (src, _) in enumerate(pairs)]
    for load in loads:
        load.start()
    stores = []
    for k, (_, dst) in enumerate(pairs):
        loads[k].wait()
        store = pltpu.make_async_copy(bounce.at[k], dst, sems.at[1, k])
        store.start()
        stores.append(store)
    for store in stores:
        store.wait()


def halves_kernel(picks, tok_ref, *rest):
    outs, bounce, sems = rest[: len(picks)], rest[-2], rest[-1]
    deep = outs[0].shape[0]
    part = lax.axis_index("tile") & 1
    bite = deep // 2
    pairs = []
    for (rim, start), out in zip(picks, outs):
        u = part if rim else 1 - part
        for k in range(0, deep, bite):
            pairs.append((tok_ref.at[u, start + k : start + k + bite], out.at[k : k + bite]))
    copy_through(pairs, bounce, sems)


def split_halves(picks, tok):
    halves, deep, wide, run, feat = tok.shape
    part = (deep // 2, wide, run, feat)
    count = len(picks)
    anym = pl.BlockSpec(memory_space=pl.ANY)
    return pl.pallas_call(
        functools.partial(halves_kernel, picks),
        out_shape=[jax.ShapeDtypeStruct(part, tok.dtype)] * count,
        in_specs=[anym],
        out_specs=[anym] * count,
        scratch_shapes=[
            pltpu.VMEM((2 * count, part[0] // 2) + part[1:], tok.dtype),
            pltpu.SemaphoreType.DMA((2, 2 * count)),
        ],
        cost_estimate=pl.CostEstimate(flops=0, bytes_accessed=count << 21, transcendentals=0),
    )(tok)


def far_kernel(cap, tile_ref, panel_ref, tok_ref, *rest):
    sides, outs, stage, in_sems, out_sems = rest[:4], rest[4:9], *rest[9:]
    halves, deep, wide, run, feat = tok_ref.shape
    panels = halves * wide
    cut = deep // 2
    me = lax.axis_index("tile")
    part = me & 1

    def bring(cond, ref, k, spot):
        @pl.when(cond)
        def _():
            pltpu.make_async_copy(ref, stage.at[k, spot], in_sems.at[k, spot]).start()

    def bring_side(cond, axis, j, k, spot):
        aligned = j // wide == part
        bring(jnp.logical_and(cond, aligned), sides[axis].at[:, j % wide], k, spot)
        bring(jnp.logical_and(cond, jnp.logical_not(aligned)), sides[2 + axis].at[:, j % wide], k, spot)

    totals = []
    for k, (bits, relay) in enumerate(((2, 4), (4, 2), (3, 4), (5, 2))):
        asker = me ^ bits
        axis, rows = (1, slice(cut, deep)) if relay == 4 else (0, slice(0, cut))

        def body(p, count, k=k, asker=asker, relay=relay, axis=axis, rows=rows):
            named = tile_ref[0, asker, p]
            own = jnp.logical_and(named == me, count < 2 * cap)
            other = jnp.logical_and(named == me ^ relay, count < 2 * cap)
            j = panel_ref[0, asker, p]
            bring(own, tok_ref.at[j // wide, rows, j % wide], k, count)
            bring_side(other, axis, j, k, count)
            return count + jnp.logical_or(own, other).astype(jnp.int32)

        totals.append(lax.fori_loop(0, panels, body, jnp.int32(0)))

    def near(p, counts):
        named = tile_ref[0, me ^ 1, p]
        j = panel_ref[0, me ^ 1, p]
        hits = [jnp.logical_and(named == me ^ relay, counts[k] < cap) for k, relay in enumerate((2, 4, 0))]
        for k in range(2):
            bring_side(hits[k], k, j, 4, k * cap + counts[k])
        bring(hits[2], tok_ref.at[j // wide, :cut, j % wide], 4, 2 * cap + counts[2])
        bring(hits[2], tok_ref.at[j // wide, cut:, j % wide], 4, 3 * cap + counts[2])
        return tuple(count + hit.astype(jnp.int32) for count, hit in zip(counts, hits))

    near_totals = lax.fori_loop(0, panels, near, (jnp.int32(0),) * 3)
    used = []
    for k in range(4):
        used += [(k, c, c < totals[k]) for c in range(2 * cap)]
    used += [(4, c, c % cap < near_totals[min(c // cap, 2)]) for c in range(4 * cap)]
    for k, c, cond in used:

        @pl.when(cond)
        def _(k=k, c=c):
            pltpu.make_async_copy(sides[0].at[:, 0], stage.at[k, c], in_sems.at[k, c]).wait()
            pltpu.make_async_copy(stage.at[k, c], outs[k].at[c], out_sems.at[k, c]).start()

    for k, c, cond in used:

        @pl.when(cond)
        def _(k=k, c=c):
            pltpu.make_async_copy(stage.at[k, c], outs[k].at[c], out_sems.at[k, c]).wait()


def pack_far(tile_table, panel_table, tok, sides, cap):
    halves, deep, wide, run, feat = tok.shape
    smem = pl.BlockSpec(memory_space=pltpu.SMEM)
    anym = pl.BlockSpec(memory_space=pl.ANY)
    block = (2 * cap, deep // 2, run, feat)
    return pl.pallas_call(
        functools.partial(far_kernel, cap),
        out_shape=[jax.ShapeDtypeStruct(block, tok.dtype)] * 4
        + [jax.ShapeDtypeStruct((4 * cap,) + block[1:], tok.dtype)],
        in_specs=[smem, smem] + [anym] * 5,
        out_specs=[anym] * 5,
        scratch_shapes=[
            pltpu.VMEM((5, 4 * cap) + block[1:], tok.dtype),
            pltpu.SemaphoreType.DMA((5, 4 * cap)),
            pltpu.SemaphoreType.DMA((5, 4 * cap)),
        ],
        compiler_params=pltpu.CompilerParams(vmem_limit_bytes=VMEM_LIMIT),
        cost_estimate=pl.CostEstimate(flops=0, bytes_accessed=6 << 20, transcendentals=0),
    )(tile_table, panel_table, tok, *sides)


def qkv_kernel(tok_ref, gain_ref, w_ref, q_ref, kv_ref):
    dims = tok_ref.shape
    feat = dims[-1]
    rows = dims[1] * dims[2] * dims[3]
    normed = layer_norm(tok_ref[...].reshape(rows, feat), gain_ref[...])
    q_ref[...] = dot_f32(normed, w_ref[:, :feat]).astype(jnp.bfloat16).reshape(q_ref.shape)
    kv_ref[...] = dot_f32(normed, w_ref[:, feat:]).astype(jnp.bfloat16).reshape(kv_ref.shape)


def project_own(tok, gain_row, w_qkv):
    halves, deep, wide, run, feat = tok.shape
    step = deep // 2
    spec = lambda width: pl.BlockSpec((1, step, wide, run, width), lambda i: (i // 2, i % 2, 0, 0, 0))
    tokens = halves * deep * wide * run
    return pl.pallas_call(
        qkv_kernel,
        grid=(halves * 2,),
        out_shape=[
            jax.ShapeDtypeStruct((halves, deep, wide, run, feat), jnp.bfloat16),
            jax.ShapeDtypeStruct((halves, deep, wide, run, 2 * feat), jnp.bfloat16),
        ],
        in_specs=[
            spec(feat),
            pl.BlockSpec((feat,), lambda i: (0,)),
            pl.BlockSpec((feat, 3 * feat), lambda i: (0, 0), pipeline_mode=pl.Buffered(1)),
        ],
        out_specs=[spec(feat), spec(2 * feat)],
        compiler_params=pltpu.CompilerParams(vmem_limit_bytes=VMEM_LIMIT),
        cost_estimate=pl.CostEstimate(
            flops=2 * tokens * feat * 3 * feat, bytes_accessed=tokens * feat * 8 + feat * feat * 6, transcendentals=0
        ),
    )(tok, gain_row, w_qkv)


def window_kernel(head_width, half_ref, *refs):
    edges, (q_ref, kvo_ref, gain_ref, wk_ref, wv_ref, mix_ref, kv_s) = refs[:-7], refs[-7:]
    deep, group, run, feat = mix_ref.shape
    length = deep * run
    bottom = edges[1][...]
    if len(edges) == 3:
        bottom = jnp.where(half_ref[2] == 1, bottom, edges[2][...])
    rows = jnp.concatenate([edges[0][...], bottom], axis=0).reshape(deep * group * run, feat)
    normed = layer_norm(rows, gain_ref[...])
    half_shape = kv_s.shape[:-1] + (feat,)
    kv_s[..., :feat] = dot_f32(normed, wk_ref[...]).astype(jnp.bfloat16).reshape(half_shape)
    kv_s[..., feat:] = dot_f32(normed, wv_ref[...]).astype(jnp.bfloat16).reshape(half_shape)
    pair = 2 * head_width
    scale = LOG2E * head_width ** (-0.5)
    bias = jnp.where(
        jnp.logical_and(half_ref[1] == 0, lax.broadcasted_iota(jnp.int32, (1, 2 * length), 1) < length), -jnp.inf, 0.0
    )
    low = low_lanes(length, pair, head_width)
    ones = jnp.ones((2 * length, pair), jnp.bfloat16)
    zero = jnp.zeros((length, pair), jnp.bfloat16)
    def panel(i, carry):
        def score(g):
            at = slice(g * pair, (g + 1) * pair)
            q = q_ref[0, :, i, :, at].reshape(length, pair)
            qs = jnp.concatenate([jnp.where(low, q, zero), jnp.where(low, zero, q)], axis=0)
            keys = jnp.concatenate(
                [kv_s[:, i, :, at].reshape(length, pair), kvo_ref[0, :, i, :, at].reshape(length, pair)], axis=0
            )
            return dot_t(qs, keys) + bias

        def mix(g, scores):
            at_v = slice(feat + g * pair, feat + (g + 1) * pair)
            vals = jnp.concatenate(
                [kv_s[:, i, :, at_v].reshape(length, pair), kvo_ref[0, :, i, :, at_v].reshape(length, pair)], axis=0
            )
            peak = jnp.max(scores, axis=1, keepdims=True)
            weights = jnp.exp2((scores - peak) * scale).astype(jnp.bfloat16)
            both = dot_f32(weights, jnp.concatenate([vals, ones], axis=1))
            mixed = both[:, :pair] / both[:, pair:]
            out = jnp.where(low, mixed[:length], mixed[length:])
            mix_ref[:, i, :, g * pair : (g + 1) * pair] = out.astype(jnp.bfloat16).reshape(deep, run, pair)

        staged(feat // pair, score, mix)
        return carry

    lax.fori_loop(0, group, panel, 0)


def window_mix(half_keep, edges, spots, q, kv_own, gain_row, w_qkv):
    _, deep, wide, run, feat = q.shape
    group = min(GROUP, wide)
    head_width = feat // HEADS
    own = lambda width: pl.BlockSpec((1, deep, group, run, width), lambda i, hk: (hk[0], 0, i, 0, 0))
    side = lambda spot: pl.BlockSpec((deep // 2, group, run, feat), lambda i, hk: (spot, i, 0, 0))
    flat = pl.BlockSpec((deep, group, run, feat), lambda i, hk: (0, i, 0, 0))
    tokens = deep * wide * run
    return pl.pallas_call(
        functools.partial(window_kernel, head_width),
        out_shape=jax.ShapeDtypeStruct((deep, wide, run, feat), jnp.bfloat16),
        grid_spec=pltpu.PrefetchScalarGridSpec(
            num_scalar_prefetch=1,
            grid=(wide // group,),
            in_specs=[
                *[side(spot) for spot in spots],
                own(feat),
                own(2 * feat),
                pl.BlockSpec((feat,), lambda i, hk: (0,)),
                *[
                    pl.BlockSpec((feat, feat), lambda i, hk, k=k: (0, k), pipeline_mode=pl.Buffered(1))
                    for k in (1, 2)
                ],
            ],
            out_specs=flat,
            scratch_shapes=[pltpu.VMEM((deep, group, run, 2 * feat), jnp.bfloat16)],
        ),
        compiler_params=pltpu.CompilerParams(vmem_limit_bytes=VMEM_LIMIT),
        cost_estimate=pl.CostEstimate(
            flops=2 * tokens * feat * 2 * feat + 8 * tokens * 256 * feat,
            bytes_accessed=tokens * feat * 10 + feat * feat * 6,
            transcendentals=tokens * 256 * HEADS,
        ),
    )(half_keep, *edges, q, kv_own, gain_row, w_qkv, w_qkv)


def direct_parts(recv, tok_ref, tiles, wanted, cap):
    cut = tok_ref.shape[1] // 2
    wide = tok_ref.shape[2]

    def own(j, seen):
        return tok_ref.at[j // wide, :cut, j % wide], tok_ref.at[j // wide, cut:, j % wide]

    def other(r):
        return lambda j, seen: (recv[r - 1].at[seen[r], :cut], recv[r - 1].at[seen[r], cut:])

    return {r: own if r == 0 else other(r) for r in range(tiles) if (wanted >> r) & 1}


def relay_parts(recv, tok_ref, tiles, wanted, cap):
    whole, x_same, x_cross, y_same, y_cross, rest = recv[:4], *recv[4:]
    cut = tok_ref.shape[1] // 2
    wide = tok_ref.shape[2]
    same = lambda k, j: [(True, whole[k].at[:, j % wide]), (False, whole[k + 2].at[:, j % wide])]
    table = {
        0: lambda j, seen: (tok_ref.at[j // wide, :cut, j % wide], tok_ref.at[j // wide, cut:, j % wide]),
        1: lambda j, seen: (rest.at[2 * cap + seen[1]], rest.at[3 * cap + seen[1]]),
        2: lambda j, seen: (same(0, j), x_same.at[seen[2] + seen[6]]),
        3: lambda j, seen: (rest.at[seen[3]], x_cross.at[seen[3] + seen[7]]),
        4: lambda j, seen: (y_same.at[seen[4] + seen[6]], same(1, j)),
        5: lambda j, seen: (y_cross.at[seen[5] + seen[7]], rest.at[cap + seen[5]]),
        6: lambda j, seen: (y_same.at[seen[4] + seen[6]], x_same.at[seen[2] + seen[6]]),
        7: lambda j, seen: (y_cross.at[seen[5] + seen[7]], x_cross.at[seen[3] + seen[7]]),
    }
    return {r: table[r] for r in range(tiles) if (wanted >> r) & 1}


def cross_kernel(plan, tiles, head_width, wanted, recv_count, cap, refs):
    tile_ref, panel_ref, valid_ref, half_ref, tok_ref = refs[:5]
    recv = refs[5 : 5 + recv_count]
    q_ref, mix_a, mix_b, gain_ref, wqkv_ref, wproj_ref = refs[5 + recv_count : 11 + recv_count]
    out_ref, got, q_s, own_s, res_s, wkv_s, wp_s, normed_s, kv_s, mixed_s, seen, ids, slots, w_sem, sems = refs[-15:]
    panels, deep, run, feat = got.shape
    half = panels // 2
    cut = deep // 2
    length = deep * run
    me = lax.axis_index("tile")
    parts = plan(recv, tok_ref, tiles, wanted, cap)
    for t in range(tiles):
        seen[t] = 0

    def record(p, count):
        r = tile_ref[0, me, p] ^ me
        hit = ((wanted >> r) & 1) == 1

        @pl.when(hit)
        def _():
            ids[count] = p
            for t in range(tiles):
                slots[count, t] = seen[t]

        seen[r] = seen[r] + 1
        return count + hit.astype(jnp.int32)

    def fetch(n):
        p = ids[n]
        j = panel_ref[0, me, p]
        r = tile_ref[0, me, p] ^ me
        for k, pick in parts.items():

            @pl.when(r == k)
            def _(pick=pick):
                for ref, rows, k in zip(pick(j, slots.at[n]), (slice(0, cut), slice(cut, deep)), (0, 4)):
                    if not isinstance(ref, list):
                        pltpu.make_async_copy(ref, got.at[n, rows], sems.at[k, n]).start()
                        continue
                    for mine, choice in ref:

                        @pl.when((j // half == (me & 1)) == mine)
                        def _(choice=choice, rows=rows, k=k):
                            pltpu.make_async_copy(choice, got.at[n, rows], sems.at[k, n]).start()

        u = p // half
        w = p % half
        pltpu.make_async_copy(q_ref.at[u, :, w], q_s.at[n], sems.at[1, n]).start()

        @pl.when(u == half_ref[0])
        def _():
            pltpu.make_async_copy(mix_a.at[:, w], own_s.at[n], sems.at[2, n]).start()

        @pl.when(u != half_ref[0])
        def _():
            pltpu.make_async_copy(mix_b.at[:, w], own_s.at[n], sems.at[2, n]).start()

    def fetch_unit(n):
        def one(i, carry):
            fetch(i)
            return carry

        lax.fori_loop(2 * n, jnp.minimum(2 * n + 2, total), one, 0)

    load_wkv = pltpu.make_async_copy(wqkv_ref.at[:, feat:], wkv_s, w_sem.at[0])
    load_wp = pltpu.make_async_copy(wproj_ref, wp_s, w_sem.at[1])
    load_wkv.start()
    total = lax.fori_loop(0, panels, record, jnp.int32(0))
    fetch_unit(0)
    load_wp.start()

    pair = 2 * head_width
    scale = LOG2E * head_width ** (-0.5)
    low = low_lanes(length, pair, head_width)
    zero = jnp.zeros((length, pair), jnp.bfloat16)
    one = jnp.ones((length, pair), jnp.bfloat16)
    marks = jnp.concatenate([jnp.where(low, one, zero), jnp.where(low, zero, one)], axis=0)
    pairs = feat // pair

    def unit(n, carry):
        first = 2 * n
        for i in range(2):

            @pl.when(first + i < total)
            def _(i=i):
                n_i = first + i
                for k, place in ((0, got.at[n_i, :cut]), (4, got.at[n_i, cut:])):
                    pltpu.make_async_copy(tok_ref.at[0, :cut, 0], place, sems.at[k, n_i]).wait()
                for k, place in ((1, q_s.at[n_i]), (2, own_s.at[n_i])):
                    pltpu.make_async_copy(tok_ref.at[0, :, 0], place, sems.at[k, n_i]).wait()

        rows = got[pl.ds(first, 2)].reshape(2 * length, feat)
        normed_s[...] = layer_norm(rows, gain_ref[...])

        @pl.when(n == 0)
        def _():
            load_wkv.wait()

        fetch_unit(n + 1)
        kv_s[...] = dot_f32(normed_s[...], wkv_s[...]).astype(jnp.bfloat16)

        @pl.when(n == 0)
        def _():
            load_wp.wait()

        gates = [valid_ref[ids[jnp.minimum(first + i, total - 1)]].astype(jnp.float32) for i in range(2)]

        def score(t):
            i, g = t // pairs, t % pairs
            at = slice(g * pair, (g + 1) * pair)
            q = q_s[first + i, :, :, at].reshape(length, pair)
            key = kv_s[i * length : (i + 1) * length, at]
            keys = jnp.concatenate([jnp.where(low, key, zero), jnp.where(low, zero, key)], axis=0)
            return dot_t(q, keys)

        def mix(t, scores):
            i, g = t // pairs, t % pairs
            at = slice(g * pair, (g + 1) * pair)
            val = kv_s[i * length : (i + 1) * length, feat + g * pair : feat + (g + 1) * pair]
            vals = jnp.concatenate([jnp.where(low, val, zero), jnp.where(low, zero, val)], axis=0)
            parts = []
            for h in range(2):
                part = scores[:, h * length : (h + 1) * length]
                peak = jnp.max(part, axis=1, keepdims=True)
                parts.append(jnp.exp2((part - peak) * scale).astype(jnp.bfloat16))
            both = dot_f32(jnp.concatenate(parts, axis=1), jnp.concatenate([vals, marks], axis=1))
            cross = (both[:, :pair] / both[:, pair:]).astype(jnp.bfloat16)
            own = own_s[first + i, :, :, at].reshape(length, pair)
            blended = gates[i] * own.astype(jnp.float32) + cross.astype(jnp.float32)
            mixed_s[i * length : (i + 1) * length, at] = blended.astype(jnp.bfloat16)

        staged(2 * pairs, score, mix)
        res_s[pl.ds(first, 2)] = dot_f32(mixed_s[...], wp_s[...]).astype(jnp.bfloat16).reshape(2, deep, run, feat)
        for i in range(2):

            @pl.when(first + i < total)
            def _(i=i):
                p = ids[first + i]
                pltpu.make_async_copy(
                    res_s.at[first + i], out_ref.at[p // half, :, p % half], sems.at[3, first + i]
                ).start()

        return carry

    lax.fori_loop(0, (total + 1) // 2, unit, 0)

    @pl.when(total == 0)
    def _():
        load_wkv.wait()
        load_wp.wait()

    def finish(n, carry):
        pltpu.make_async_copy(res_s.at[n], out_ref.at[0, :, 0], sems.at[3, n]).wait()
        return carry

    lax.fori_loop(0, total, finish, 0)


def cross_and_project(
    plan, wanted, tiles, cap, tile_table, panel_table, valid, half_keep, tok, recv, q, mixes, gain_row, w_qkv, w_proj, earlier
):
    halves, deep, wide, run, feat = tok.shape
    panels = halves * wide
    head_width = feat // HEADS
    length = deep * run
    smem = pl.BlockSpec(memory_space=pltpu.SMEM)
    anym = pl.BlockSpec(memory_space=pl.ANY)
    share = bin(wanted).count("1") / tiles
    tokens = int(panels * length * share)
    many = pltpu.VMEM((panels, deep, run, feat), jnp.bfloat16)
    operands = [tile_table, panel_table, valid, half_keep, tok, *recv, q, *mixes, gain_row, w_qkv, w_proj]
    specs = [smem] * 4 + [anym] * (len(recv) + 4) + [pl.BlockSpec((feat,), lambda: (0,))] + [anym] * 2
    aliases = {}
    if earlier is not None:
        aliases = {len(operands): 0}
        operands.append(earlier)
        specs.append(anym)

    def kernel(*refs):
        cross_kernel(plan, tiles, head_width, wanted, len(recv), cap, refs)

    return pl.pallas_call(
        kernel,
        out_shape=jax.ShapeDtypeStruct(tok.shape, jnp.bfloat16),
        in_specs=specs,
        out_specs=anym,
        scratch_shapes=[
            many,
            many,
            many,
            many,
            pltpu.VMEM((feat, 2 * feat), jnp.bfloat16),
            pltpu.VMEM((feat, feat), jnp.bfloat16),
            pltpu.VMEM((2 * length, feat), jnp.bfloat16),
            pltpu.VMEM((2 * length, 2 * feat), jnp.bfloat16),
            pltpu.VMEM((2 * length, feat), jnp.bfloat16),
            pltpu.SMEM((tiles,), jnp.int32),
            pltpu.SMEM((panels,), jnp.int32),
            pltpu.SMEM((panels, tiles), jnp.int32),
            pltpu.SemaphoreType.DMA((2,)),
            pltpu.SemaphoreType.DMA((5, panels)),
        ],
        input_output_aliases=aliases,
        compiler_params=pltpu.CompilerParams(vmem_limit_bytes=VMEM_LIMIT),
        cost_estimate=pl.CostEstimate(
            flops=2 * tokens * feat * 3 * feat + 8 * tokens * 128 * feat,
            bytes_accessed=tokens * feat * 8 + feat * feat * 6,
            transcendentals=tokens * 128 * HEADS,
        ),
    )(*operands)


def per_device(tokens, gain, w_qkv, w_proj, scene_first, window_valid, partner_tile, partner_panel):
    _, tok_rows, tok_cols, feat = tokens.shape
    run = 16
    wide = tok_cols // run
    tok = tokens.reshape(2, tok_rows // 2, wide, run, feat)
    tiles = partner_tile.shape[1]
    panels = partner_tile.shape[2]
    cap = 2 * max(1, panels // tiles)
    slab_count = scene_first.shape[0]
    tile_table = partner_tile[:, :, :, 0]
    panel_table = partner_panel
    valid = window_valid.reshape(panels)
    gain_row = gain
    slab_index = lax.axis_index(("scene", "tile"))
    after_index = jnp.minimum(slab_index + 1, slab_count - 1)
    own_first = jnp.logical_or(scene_first[slab_index] == 1, slab_index == 0)
    next_first = jnp.logical_or(scene_first[after_index] == 1, slab_index + 1 >= slab_count)
    keep_before = jnp.logical_not(own_first).astype(jnp.int32)
    keep_after = jnp.logical_not(next_first).astype(jnp.int32)

    def xor(block, bits):
        return lax.ppermute(block, "tile", [(i, i ^ bits) for i in range(tiles)])

    def cross(plan, wanted, recv, mixes, half_keep, earlier):
        return cross_and_project(
            plan,
            wanted,
            tiles,
            cap,
            tile_table,
            panel_table,
            valid,
            half_keep,
            tok,
            recv,
            q,
            mixes,
            gain_row,
            w_qkv,
            w_proj,
            earlier,
        )

    if tiles == 8:
        fence = lax.optimization_barrier
        odd = slab_index % 2
        direct = jnp.logical_or(slab_index % 4 == 1, slab_index % 4 == 2).astype(jnp.int32)
        near_half = jnp.stack([1 - odd, jnp.where(odd == 1, keep_before, keep_after), direct]).astype(jnp.int32)
        far_half = jnp.stack([odd, jnp.where(odd == 1, keep_after, keep_before), direct]).astype(jnp.int32)
        near_half, far_half = fence((near_half, far_half))
        links_a, links_b, links_c = [], [], []
        for low in range(1, slab_count - 1, 2):
            links_a += [(low ^ 2, low + 1), ((low + 1) ^ 2, low)]
            if low % 4 == 1:
                links_b += [(low, low + 1), (low + 1, low)]
            else:
                links_c += [(low ^ 4, low + 1), ((low + 1) ^ 4, low)]

        cut = tok.shape[1] // 2
        (off_x,) = split_halves(((False, 0),), tok)
        tok_next, off_x = fence((tok, off_x))
        off_y, rim_x, rim_y = split_halves(((False, cut), (True, 0), (True, cut)), tok_next)
        rim_x, rim_y, off_y, gain_next = fence((rim_x, rim_y, off_y, gain_row))
        near = (xor(off_x, 1), xor(off_y, 1))
        own_rim = rim_y
        rim_x, rim_y = xor(rim_x, 2), xor(rim_y, 4)
        off_x, off_y = xor(off_x, 2), xor(off_y, 4)
        q, kv = project_own(tok, gain_next, w_qkv)
        edge_b = lax.ppermute(own_rim, ("scene", "tile"), links_b)
        mix_near = window_mix(near_half, near, (0, 0), q, kv, gain_row, w_qkv)
        rim_x, rim_y, mix_near = fence((rim_x, rim_y, mix_near))
        edge_c = lax.ppermute(rim_y, ("scene", "tile"), links_c)
        edge_a = lax.ppermute(rim_x, ("scene", "tile"), links_a)
        sides = (rim_x, rim_y, off_x, off_y)
        x_same, y_same, x_cross, y_cross, rest = pack_far(tile_table, panel_table, tok, sides, cap)
        y_same, rest = xor(y_same, 4), xor(rest, 1)
        edge_a, edge_c, x_same, x_cross, y_cross = fence((edge_a, edge_c, x_same, x_cross, y_cross))
        x_same = xor(x_same, 2)
        mix_far = window_mix(far_half, (edge_a, edge_b, edge_c), (0, 0, 0), q, kv, gain_row, w_qkv)
        x_cross, y_cross, mix_far = fence((x_cross, y_cross, mix_far))
        x_cross, y_cross = xor(x_cross, 3), xor(y_cross, 5)
        mixes = (mix_near, mix_far)
        early = (*sides, x_same, rest, y_same, rest, rest)
        late = (*sides, x_same, x_cross, y_same, y_cross, rest)
        out = cross(relay_parts, 0b01010111, early, mixes, near_half, None)
        out = cross(relay_parts, 0b10101000, late, mixes, near_half, out)
    else:
        forward = [(i, i + 1) for i in range(slab_count - 1)]
        backward = [(i + 1, i) for i in range(slab_count - 1)]
        before = lax.ppermute(tok[1], ("scene", "tile"), forward)
        after = lax.ppermute(tok[0], ("scene", "tile"), backward)
        outgoing = pack(tile_table, panel_table, tok, tiles, cap)
        recv = [xor(outgoing[r - 1], r) for r in range(1, tiles)]
        q, kv = project_own(tok, gain_row, w_qkv)
        zero = jnp.zeros((), jnp.int32)
        upper = jnp.stack([zero, keep_before])
        mix_up = window_mix(upper, (before, before), (0, 1), q, kv, gain_row, w_qkv)
        mix_down = window_mix(jnp.stack([zero + 1, keep_after]), (after, after), (0, 1), q, kv, gain_row, w_qkv)
        out = cross(direct_parts, (1 << tiles) - 1, recv, (mix_up, mix_down), upper, None)
    return out.reshape(tokens.shape)


def solution(mesh):
    in_specs = (
        P(("scene", "tile"), None, None, None),
        P(),
        P(),
        P(),
        P(),
        P(("scene", "tile"), None),
        P("scene", None, None, None),
        P("scene", None, None),
    )
    out_specs = P(("scene", "tile"), None, None, None)
    return jax.shard_map(per_device, mesh=mesh, in_specs=in_specs, out_specs=out_specs, check_vma=False)
```
